32 devices in a mesh: row: 4 (over z), col: 8 (over y, x, core).
Axes of the slice: x: 2, y: 2, z: 4, core: 2. Of those that a mesh axis runs over, the one named last changes fastest.
Arguments:
- observed: float32 [4096, 2048], P('row', 'col'), may hold values from -12 to 12
- kernels: float32 [8, 65, 65], replicated, may hold values from -0.0625 to 0.0625
- occupied: int32 [16, 8], replicated, may hold values from 0 to 1, as said below
- kernel_index: int32 [16, 8], replicated, may hold values from 0 to 7
Outputs:
- corrected: float32 [4096, 2048], P('row', 'col')
- residual: float32 [4096, 2048], P('row', 'col')
The draws below stay inside these ranges and needn't reach their ends.
Inputs may be any that keep to these rules, and one draw needn't show every extreme that they name: The tiles with occupied = 1 are those whose centres lie inside one disk; at least one tile is occupied and at least one is not.
All inputs are finite; a program needn't handle non-finite values.
Results may differ from the reference program's by a relative error of at most 0.0003.
Values sent between devices are 32-bit elements; how exact they have to be, the bound alone decides.
No kernel may reach another device: no remote copies, remote signals or barrier semaphores. Data moves between devices by JAX's collectives and lax.ppermute only.
A program may use at most 128 MiB of HBM per device.

```python
import jax
import jax.numpy as jnp
from jax import lax

TILE = 256
HALO = 64
KW = 65
NK = 8
ITERS = 3
NTR = 16
NTC = 8
NROWS = 4096
NCOLS = 2048


def draw_observed(key, part):
    row_frac = jnp.arange(NROWS, dtype=jnp.float32)[:, None] / NROWS
    col_frac = jnp.arange(NCOLS, dtype=jnp.float32)[None, :] / NCOLS
    brightness = 0.5 + 0.75 * (row_frac + col_frac)
    noise_part = jnp.clip(jax.random.normal(key, (NROWS, NCOLS), jnp.float32), -6.0, 6.0)
    return brightness * noise_part


def draw_occupied(key, part):
    key_list = jax.random.split(jax.random.fold_in(key, 17), 3)
    short_side = min(NTR, NTC)
    center_row = jax.random.randint(key_list[0], (), NTR * 64 // 3, NTR * 64 - NTR * 64 // 3 + 1)
    center_col = jax.random.randint(key_list[1], (), NTC * 64 // 3, NTC * 64 - NTC * 64 // 3 + 1)
    radius = jax.random.randint(key_list[2], (), short_side * 64 // 3 + 32, short_side * 32 + 1)
    tile_rows = 64 * jnp.arange(NTR, dtype=jnp.int32)[:, None] + 32
    tile_cols = 64 * jnp.arange(NTC, dtype=jnp.int32)[None, :] + 32
    distance = (tile_rows - center_row) ** 2 + (tile_cols - center_col) ** 2
    return (distance <= radius * radius).astype(jnp.int32)


def place_ends(entries, own_key, low, top_value):
    longest = entries.shape.index(max(entries.shape))
    spots = []
    for shift in (0, 1):
        where = [jax.random.randint(jax.random.fold_in(own_key, axis), (), 0, length) for axis, length in enumerate(entries.shape)]
        where[longest] = (where[longest] + shift) % entries.shape[longest]
        spots.append(tuple(where))
    return entries.at[spots[0]].set(low).at[spots[1]].set(top_value)


def noise(key, dims, deviation, bound, held_as=jnp.bfloat16):
    return jnp.clip(deviation * jax.random.normal(key, dims, jnp.float32), -bound, bound).astype(held_as)


def setup_inputs(seed: int = 0) -> dict:
    seeds = jax.random.split(jax.random.key(seed), 5)
    observed = draw_observed(jax.random.fold_in(seeds[4], 71), 0)
    kernels = noise(seeds[1], (NK, KW, KW), (2 * KW * KW) ** -0.5, 0.0625, jnp.float32)
    occupied = draw_occupied(jax.random.fold_in(seeds[4], 71), 0)
    kernel_index = place_ends(jax.random.randint(seeds[3], (NTR, NTC), 0, NK), jax.random.fold_in(seeds[3], 1), 0, NK - 1).astype(jnp.int32)
    return {"observed": observed, "kernels": kernels, "occupied": occupied, "kernel_index": kernel_index}


def kernel_spectra(kernels):
    win_size = TILE + 2 * HALO
    padded = jnp.zeros((kernels.shape[0], win_size, win_size), jnp.float32)
    padded = padded.at[:, :KW, :KW].set(kernels)
    transformed = jnp.fft.fft2(padded)
    return jnp.real(transformed) ** 2 + jnp.imag(transformed) ** 2


def operate(vector, spectra, occupied, kernel_index):
    win_size = TILE + 2 * HALO
    tile_cols = occupied.shape[1]
    padded = jnp.pad(vector, HALO)
    flat_occ = occupied.reshape(-1)
    flat_kernel = kernel_index.reshape(-1)

    def add_tile(buffer, tile_num):
        tile_row = tile_num // tile_cols
        tile_col = tile_num % tile_cols
        row_start = (tile_row * TILE).astype(jnp.int32)
        col_start = (tile_col * TILE).astype(jnp.int32)
        window = lax.dynamic_slice(padded, (row_start, col_start), (win_size, win_size))
        spectrum = lax.dynamic_index_in_dim(spectra, flat_kernel[tile_num], 0, keepdims=False)
        result = jnp.real(jnp.fft.ifft2(spectrum * jnp.fft.fft2(window)))
        weight = flat_occ[tile_num].astype(vector.dtype)
        current = lax.dynamic_slice(buffer, (row_start, col_start), (win_size, win_size))
        buffer = lax.dynamic_update_slice(buffer, current + weight * result, (row_start, col_start))
        return buffer, None

    tile_nums = jnp.arange(occupied.shape[0] * tile_cols, dtype=jnp.int32)
    buffer, unused = lax.scan(add_tile, jnp.zeros_like(padded), tile_nums)
    return vector + buffer[HALO:-HALO, HALO:-HALO]


def reference(observed, kernels, occupied, kernel_index):
    spectra = kernel_spectra(kernels)
    corrected = jnp.zeros_like(observed)
    residual = observed
    direction = observed
    energy = jnp.sum(residual * residual)
    for iteration in range(ITERS):
        mapped = operate(direction, spectra, occupied, kernel_index)
        step_len = energy / jnp.sum(direction * mapped)
        corrected = corrected + step_len * direction
        residual = residual - step_len * mapped
        fresh = jnp.sum(residual * residual)
        direction = residual + (fresh / energy) * direction
        energy = fresh
    return corrected, residual
```

```python
import functools
import math

import jax
import jax.numpy as jnp
import numpy as np
from jax import lax
from jax.experimental import pallas as pl
from jax.experimental.pallas import tpu as pltpu
from jax.sharding import PartitionSpec as P

TILE = 256
HALO = 64
KW = 65
ITERS = 3
WIN = TILE + 2 * HALO
THIRD = WIN // 3
HALF = THIRD // 2
SLOTS = 2 * THIRD
BF = jnp.bfloat16
F32 = jnp.float32


def hi_lo(table):
    high = table.astype(np.float32).astype(jnp.bfloat16)
    low = (table - high.astype(np.float64)).astype(np.float32).astype(jnp.bfloat16)
    return high, low


@functools.cache
def tables():
    spots = np.arange(THIRD)
    low_freq = 3 * np.arange(HALF)
    full = math.sqrt(2.0 / WIN)
    cos_part = np.cos(2 * np.pi * (low_freq[:, None] * spots % WIN) / WIN) * full
    sin_part = np.sin(2 * np.pi * (low_freq[:, None] * spots % WIN) / WIN) * full
    cos_part[0] = math.sqrt(1.0 / WIN)
    sin_part[0] = np.where(spots % 2 == 0, 1.0, -1.0) * math.sqrt(1.0 / WIN)
    small = np.concatenate([cos_part, sin_part])
    angle = 2 * np.pi * ((3 * spots[:, None] + 1) * spots % WIN) / WIN
    root = math.sqrt(3.0) / 2
    large = full * np.block(
        [[np.cos(angle), -root * np.sin(angle)], [np.sin(angle), root * np.cos(angle)]]
    )
    freqs = np.concatenate([low_freq, low_freq, 3 * spots + 1])
    freqs[HALF] = WIN // 2
    taps = np.arange(THIRD)
    turn = 2 * np.pi * (freqs[:, None] * taps % WIN) / WIN
    keep = (taps < KW)[None, :]
    sines = np.sin(turn)
    sines[0] = 0.0
    sines[HALF] = 0.0
    waves = np.concatenate([np.cos(turn) * keep, sines * keep])

    sh, sl = hi_lo(small)
    gh, gl = hi_lo(large)
    wh, wl = hi_lo(waves)
    zero = np.zeros_like(sh.T)
    return dict(
        g_right=np.concatenate([gh.T, gl.T, gh.T], 0),
        g_right_inv=np.concatenate([gh, gl, gh], 0),
        f_right=np.block([[sh.T, sl.T], [sh.T, zero]]),
        f_right_inv=np.block([[sh, sl], [sh, zero]]),
        g_left=np.concatenate([gh, gl], 0),
        g_left_inv=np.concatenate([gh.T, gl.T], 0),
        f_left=np.block([[sh, sh], [sl, zero]]),
        f_left_inv=np.block([[sh.T, sh.T], [sl.T, zero]]),
        w_left=np.concatenate([wh, wl, wh], 1),
        w_right=np.concatenate([wh.T, wl.T, wh.T], 0),
    )


NAMES = (
    "g_right", "g_right_inv", "f_right", "f_right_inv",
    "g_left", "g_left_inv", "f_left", "f_left_inv",
)


def split(value):
    high = value.astype(BF)
    return high, (value - high.astype(F32)).astype(BF)


def dot(left, right):
    return jnp.dot(left, right, preferred_element_type=F32)


def right_large(value, table):
    high, low = split(value)
    return dot(jnp.concatenate([high, high, low], 1), table[...])


def right_small(value, table):
    high, low = split(value)
    both = dot(jnp.concatenate([high, low], 1), table[...])
    return both[:, :THIRD] + both[:, THIRD:]


def left_large(value, table):
    high, low = split(value)
    both = dot(table[...], high)
    return both[:SLOTS] + both[SLOTS:] + dot(table[:SLOTS], low)


def left_small(value, table):
    high, low = split(value)
    both = dot(table[...], jnp.concatenate([high, low], 0))
    return both[:THIRD] + both[THIRD:]


def butterfly(first, second, third):
    total = second + third
    return first + total, first - 0.5 * total, second - third


def unbutterfly(plain, real, diff):
    base = plain - 0.5 * real
    return plain + real, base + diff, base - diff


def spectra_kernel(kid, occ, ker_ref, left_ref, right_ref, out_ref):
    def body(slot, carry):
        @pl.when(occ[slot] != 0)
        def _():
            high, low = split(ker_ref[kid[slot]])
            half = dot(left_ref[...], jnp.concatenate([high, high, low], 0))
            high, low = split(half)
            quads = dot(jnp.concatenate([high, high, low], 1), right_ref[...])
            cc = quads[:SLOTS, :SLOTS]
            cs = quads[:SLOTS, SLOTS:]
            sc = quads[SLOTS:, :SLOTS]
            ss = quads[SLOTS:, SLOTS:]
            out_ref[slot, 0] = cc * cc + ss * ss + (sc * sc + cs * cs)
            out_ref[slot, 1] = 2.0 * (sc * cs - cc * ss)

        return carry

    lax.fori_loop(0, out_ref.shape[0], body, 0)


def apply_spectrum(low_rows, high_rows, spec_ref, slot):
    lanes = lax.broadcasted_iota(jnp.int32, (1, THIRD), 1)
    sign = jnp.where(lanes < HALF, -1.0, 1.0).astype(F32)

    def band(cos_rows, sin_rows, cos_at, sin_at, size):
        pc = spec_ref[slot, 0, pl.ds(cos_at, size), :]
        ps = spec_ref[slot, 0, pl.ds(sin_at, size), :] if sin_at != cos_at else pc
        cross = spec_ref[slot, 1, pl.ds(cos_at, size), :]
        d0, d1 = cross[:, :THIRD] * sign, cross[:, THIRD:]
        c0, c1, c2 = (cos_rows[:, i * THIRD : (i + 1) * THIRD] for i in range(3))
        s0, s1, s2 = (sin_rows[:, i * THIRD : (i + 1) * THIRD] for i in range(3))
        new_cos = jnp.concatenate(
            [
                pc[:, :THIRD] * c0 + d0 * pltpu.roll(s0, HALF, 1),
                pc[:, THIRD:] * c1 - d1 * s2,
                pc[:, THIRD:] * c2 + d1 * s1,
            ],
            1,
        )
        new_sin = jnp.concatenate(
            [
                ps[:, :THIRD] * s0 - d0 * pltpu.roll(c0, HALF, 1),
                ps[:, THIRD:] * s1 + d1 * c2,
                ps[:, THIRD:] * s2 - d1 * c1,
            ],
            1,
        )
        return new_cos, new_sin

    low = band(low_rows[:HALF], low_rows[HALF:], 0, HALF, HALF)
    high = band(high_rows[:THIRD], high_rows[THIRD:], THIRD, THIRD, THIRD)
    return jnp.concatenate(low, 0), jnp.concatenate(high, 0)


def window_product(blocks, spec_ref, slot, tabs):
    halves = []
    for block in blocks:
        t0, t1, t2 = (block[:, i * THIRD : (i + 1) * THIRD] for i in range(3))
        plain, real, diff = butterfly(t0, t1, t2)
        halves.append(
            jnp.concatenate(
                [
                    right_small(plain, tabs["f_right"]),
                    right_large(jnp.concatenate([real, diff], 1), tabs["g_right"]),
                ],
                1,
            )
        )
    plain, real, diff = butterfly(*halves)
    low_rows = left_small(plain, tabs["f_left"])
    high_rows = left_large(jnp.concatenate([real, diff], 0), tabs["g_left"])
    low_rows, high_rows = apply_spectrum(low_rows, high_rows, spec_ref, slot)
    plain = left_small(low_rows, tabs["f_left_inv"])
    both = left_large(high_rows, tabs["g_left_inv"])
    results = []
    for block in unbutterfly(plain, both[:THIRD], both[THIRD:]):
        plain = right_small(block[:, :THIRD], tabs["f_right_inv"])
        both = right_large(block[:, THIRD:], tabs["g_right_inv"])
        results.append(
            jnp.concatenate(unbutterfly(plain, both[:, :THIRD], both[:, THIRD:]), 1)
        )
    return results


def lane_mask():
    return lax.broadcasted_iota(jnp.int32, (1, THIRD), 1) < HALF


def tile_of(block, num):
    return block[:, num * THIRD : (num + 1) * THIRD]


def fold8(value):
    rows = value.reshape(value.shape[0] // 8, 8, value.shape[1]).sum(0)
    return sum(tile_of(rows, i) for i in range(value.shape[1] // THIRD))


def matvec(occ, res_ref, spec_ref, tabs, buf_ref, left_ref, right_ref, acc_ref):
    tile_count = spec_ref.shape[0]
    buf_ref[pl.ds(0, THIRD), :] = jnp.zeros((THIRD, WIN), F32)

    def body(slot, carry):
        at = [pl.ds(pl.multiple_of(slot * TILE + i * THIRD, THIRD), THIRD) for i in range(3)]

        @pl.when(occ[slot] != 0)
        def _():
            blocks = [res_ref[here, :] for here in at]
            out = window_product(blocks, spec_ref, slot, tabs)
            for block, new in zip(blocks, out):
                acc_ref[...] += fold8(block * new)
            buf_ref[at[0], :] += out[0]
            buf_ref[at[1], :] = out[1]
            buf_ref[at[2], :] = out[2]

        @pl.when(occ[slot] == 0)
        def _():
            buf_ref[at[1], :] = jnp.zeros((THIRD, WIN), F32)
            buf_ref[at[2], :] = jnp.zeros((THIRD, WIN), F32)

        return carry

    lax.fori_loop(0, tile_count, body, 0)
    low = lane_mask()

    def edges(num, carry):
        here = pl.ds(pl.multiple_of(num * THIRD, THIRD), THIRD)
        block = buf_ref[here, :]
        left_ref[here, :] = jnp.where(low, tile_of(block, 0), tile_of(block, 2))
        right_ref[here, :] = jnp.where(low, tile_of(block, 2), tile_of(block, 1))
        return carry

    lax.fori_loop(0, 2 * tile_count + 1, edges, 0)


def total(value):
    return jnp.sum(jnp.sum(value, 0, keepdims=True), 1, keepdims=True)


def partials(out_ref, *values):
    lanes = lax.broadcasted_iota(jnp.int32, out_ref.shape, 1)
    out = jnp.zeros(out_ref.shape, F32)
    for num, value in enumerate(values):
        out = jnp.where(lanes == num, value, out)
    out_ref[...] = out


def first_kernel(
    occ, obs_ref, from_left, from_right, above, below, spec_ref, *rest
):
    tabs = dict(zip(NAMES, rest[: len(NAMES)]))
    res_ref, buf_ref, left_ref, right_ref, part_ref, acc_ref = rest[len(NAMES) :]
    rows = obs_ref.shape[0]
    res_ref[pl.ds(0, HALO), :] = above[...]
    res_ref[pl.ds(HALO + rows, HALO), :] = below[...]
    res_ref[pl.ds(HALO, rows), pl.ds(0, TILE)] = obs_ref[...]
    res_ref[pl.ds(HALO, rows), pl.ds(TILE, THIRD)] = jnp.where(
        lane_mask(), from_right[...], from_left[...]
    )
    square = fold8(obs_ref[...] * obs_ref[...])
    acc_ref[...] = square
    matvec(occ, res_ref, spec_ref, tabs, buf_ref, left_ref, right_ref, acc_ref)
    partials(part_ref, total(square), total(acc_ref[...]))


def scalars(parts_ref, coef_ref):
    sums = jnp.sum(parts_ref[...], 0, keepdims=True)
    energy, curve, cross = sums[:, 0:1], sums[:, 1:2], sums[:, 2:3]
    if coef_ref is None:
        return jnp.zeros_like(energy), energy / curve, energy, curve
    ratio = energy / coef_ref[0:1, 0:1]
    power = curve + ratio * (2.0 * cross + ratio * coef_ref[0:1, 1:2])
    return ratio, energy / power, energy, power


def next_kernel(first, last, tile_count, *refs):
    refs = list(refs)
    occ, edge = refs[:2]
    refs = refs[2:]
    parts_ref = refs.pop(0)
    coef_ref = None if first else refs.pop(0)
    buf_in, from_left, from_right, above, below, res_in = refs[:6]
    refs = refs[6:]
    if first:
        dir_in = map_in = cor_in = None
    else:
        dir_in, map_in, cor_in = refs[:3]
        refs = refs[3:]
    if last:
        cor_ref, res_ref = refs
        dir_ref = map_ref = None
    else:
        spec_ref = refs.pop(0)
        tabs = dict(zip(NAMES, refs[: len(NAMES)]))
        refs = refs[len(NAMES) :]
        (res_ref, dir_ref, map_ref, cor_ref, buf_ref, left_ref, right_ref, part_ref, coef_out,
         acc_ref, cross_ref) = refs
    ratio, step, energy, power = scalars(parts_ref, coef_ref)
    low = lane_mask()
    flags = [edge[i].astype(F32) for i in range(4)]
    halo_lanes = jnp.where(low, flags[3], flags[2])
    ext = buf_in.shape[0]

    def piece(start, size, top, bottom, in_block):
        here = pl.ds(start, size)
        block = buf_in[here, :]
        west, east = from_left[here, :], from_right[here, :]
        add = [
            tile_of(block, 0) + jnp.where(low, west, 0.0),
            tile_of(block, 1) + jnp.where(low, 0.0, east),
            tile_of(block, 2) + jnp.where(low, east, west),
        ]
        if top is not None:
            add = [a + above[pl.ds(top, size), pl.ds(i * THIRD, THIRD)] for i, a in enumerate(add)]
        if bottom is not None:
            add = [a + below[pl.ds(bottom, size), pl.ds(i * THIRD, THIRD)] for i, a in enumerate(add)]
        old = res_in[here, :]
        mapped = [a + tile_of(old, i) for i, a in enumerate(add)]
        mapped[2] = mapped[2] * halo_lanes
        if not in_block:
            mapped = [a * flags[0 if bottom is None else 1] for a in mapped]
        direct = [tile_of(old, i) for i in range(3)]
        if not first:
            past, was = map_in[here, :], dir_in[here, :]
            mapped = [a + ratio * tile_of(past, i) for i, a in enumerate(mapped)]
            direct = [a + ratio * tile_of(was, i) for i, a in enumerate(direct)]
        fresh = [tile_of(old, i) - step * a for i, a in enumerate(mapped)]
        inner = pl.ds(start - HALO, size) if in_block else None
        if in_block:
            for i in range(2):
                lanes = pl.ds(i * THIRD, THIRD)
                if first:
                    cor_ref[inner, lanes] = step * direct[i]
                else:
                    cor_ref[inner, lanes] = cor_in[inner, lanes] + step * direct[i]
        if last:
            for i in range(2):
                res_ref[inner, pl.ds(i * THIRD, THIRD)] = fresh[i]
            return
        for i in range(3):
            lanes = pl.ds(i * THIRD, THIRD)
            res_ref[here, lanes] = fresh[i]
            map_ref[here, lanes] = mapped[i]
            dir_ref[here, lanes] = direct[i]
        if in_block:
            acc_ref[...] += fold8(fresh[0] * fresh[0]) + fold8(fresh[1] * fresh[1])
            cross_ref[...] += fold8(fresh[0] * mapped[0]) + fold8(fresh[1] * mapped[1])

    if not last:
        acc_ref[...] = jnp.zeros_like(acc_ref)
        cross_ref[...] = jnp.zeros_like(cross_ref)
        piece(0, HALO, 0, None, False)
        piece(ext - HALO, HALO, None, HALO, False)
    piece(HALO, HALO, HALO, None, True)
    piece(ext - 2 * HALO, HALO, None, 0, True)

    def middle(num, carry):
        piece(pl.multiple_of((num + 1) * THIRD, THIRD), THIRD, None, None, True)
        return carry

    lax.fori_loop(0, (ext - 4 * HALO) // THIRD, middle, 0)
    if last:
        return
    square = total(acc_ref[...])
    matvec(occ, res_ref, spec_ref, tabs, buf_ref, left_ref, right_ref, acc_ref)
    partials(part_ref, square, total(acc_ref[...]), total(cross_ref[...]))
    partials(coef_out, energy, power)


def vmem(count):
    return [pl.BlockSpec(memory_space=pltpu.VMEM)] * count


def smem(count):
    return [pl.BlockSpec(memory_space=pltpu.SMEM)] * count


def shape(*dims):
    return jax.ShapeDtypeStruct(dims, F32)


PARAMS = pltpu.CompilerParams(vmem_limit_bytes=40 * 1024 * 1024)


def own_part(table, tile_count):
    column = lax.dynamic_index_in_dim(table, lax.axis_index("col"), 1, keepdims=False)
    return lax.dynamic_slice_in_dim(column, lax.axis_index("row") * tile_count, tile_count)


def shards(observed, kernels, occupied, kernel_index):
    rows, cols = observed.shape
    tile_count = rows // TILE
    ext = rows + 2 * HALO
    n_row, n_col = lax.axis_size("row"), lax.axis_size("col")
    devices = n_row * n_col
    occ = own_part(occupied, tile_count)
    kid = own_part(kernel_index, tile_count)
    my_row, my_col = lax.axis_index("row"), lax.axis_index("col")
    edge = jnp.stack([my_row > 0, my_row < n_row - 1, my_col > 0, my_col < n_col - 1]).astype(jnp.int32)
    host = tables()
    consts = [jnp.asarray(host[name]) for name in NAMES]

    def shift(value, axis, forward):
        count = lax.axis_size(axis)
        pairs = [(i, i + 1) for i in range(count - 1)]
        return lax.ppermute(value, axis, pairs if forward else [(b, a) for a, b in pairs])

    low = lax.broadcasted_iota(jnp.int32, (1, THIRD), 1) < HALF

    from_left = shift(observed[:, THIRD:], "col", True)
    from_right = shift(observed[:, :THIRD], "col", False)

    padded = jnp.pad(kernels, ((0, 0), (0, THIRD - KW), (0, THIRD - KW)))
    spec = pl.pallas_call(
        spectra_kernel,
        out_shape=shape(tile_count, 2, SLOTS, SLOTS),
        in_specs=smem(2) + vmem(3),
        out_specs=vmem(1)[0],
        compiler_params=PARAMS,
    )(kid, occ, padded, jnp.asarray(host["w_left"]), jnp.asarray(host["w_right"]))

    def halo_rows(part):
        return jnp.concatenate(
            [observed[part], jnp.where(low, from_right[part], from_left[part])], 1
        )

    above = shift(halo_rows(slice(rows - HALO, rows)), "row", True)
    below = shift(halo_rows(slice(0, HALO)), "row", False)

    out_strips = [shape(ext, WIN), shape(ext, THIRD), shape(ext, THIRD), shape(devices, THIRD)]
    res, buf, to_left, to_right, part = pl.pallas_call(
        first_kernel,
        out_shape=[shape(ext, WIN)] + out_strips,
        in_specs=smem(1) + vmem(6 + len(NAMES)),
        out_specs=vmem(5),
        scratch_shapes=[pltpu.VMEM((8, THIRD), F32)],
        compiler_params=PARAMS,
    )(occ, observed, from_left, from_right, above, below, spec, *consts)

    coef = direction = mapped = corrected = None
    for iteration in range(ITERS):
        first, last = iteration == 0, iteration == ITERS - 1
        from_left = shift(to_right, "col", True)
        from_right = shift(to_left, "col", False)
        parts = lax.all_to_all(part, ("row", "col"), 0, 0, tiled=True)

        def edge_rows(start):
            here = slice(start, start + 2 * HALO)
            west, east = from_left[here], from_right[here]
            add = [jnp.where(low, west, 0.0), jnp.where(low, 0.0, east), jnp.where(low, east, west)]
            return buf[here] + jnp.concatenate(add, 1)

        above = shift(edge_rows(rows), "row", True)
        below = shift(edge_rows(0), "row", False)
        args = [occ, edge, parts]
        args += [] if first else [coef]
        args += [buf, from_left, from_right, above, below, res]
        args += [] if first else [direction, mapped, corrected]
        if last:
            outs = [shape(rows, cols), shape(rows, cols)]
            scratch = []
        else:
            args += [spec, *consts]
            outs = [shape(ext, WIN)] * 3 + [shape(rows, cols)] + out_strips + [shape(8, THIRD)]
            scratch = [pltpu.VMEM((8, THIRD), F32)] * 2
        result = pl.pallas_call(
            functools.partial(next_kernel, first, last, tile_count),
            out_shape=outs,
            in_specs=smem(2) + vmem(len(args) - 2),
            out_specs=vmem(len(outs)),
            scratch_shapes=scratch,
            compiler_params=PARAMS,
        )(*args)
        if last:
            return tuple(result)
        res, direction, mapped, corrected, buf, to_left, to_right, part, coef = result


def solution(mesh):
    placed = (P("row", "col"), P(), P(), P())
    return jax.shard_map(
        shards,
        mesh=mesh,
        in_specs=placed,
        out_specs=(P("row", "col"), P("row", "col")),
        check_vma=False,
    )
```

```python
import functools
import math

import jax
import jax.numpy as jnp
import numpy as np
from jax import lax
from jax.experimental import pallas as pl
from jax.experimental.pallas import tpu as pltpu
from jax.sharding import PartitionSpec as P

TILE = 256
HALO = 64
KW = 65
ITERS = 3
WIN = TILE + 2 * HALO
THIRD = WIN // 3
HALF = THIRD // 2
SLOTS = 2 * THIRD
BF = jnp.bfloat16
F32 = jnp.float32


def hi_lo(table):
    high = table.astype(np.float32).astype(jnp.bfloat16)
    low = (table - high.astype(np.float64)).astype(np.float32).astype(jnp.bfloat16)
    return high, low


@functools.cache
def tables():
    spots = np.arange(THIRD)
    low_freq = 3 * np.arange(HALF)
    full = math.sqrt(2.0 / WIN)
    cos_part = np.cos(2 * np.pi * (low_freq[:, None] * spots % WIN) / WIN) * full
    sin_part = np.sin(2 * np.pi * (low_freq[:, None] * spots % WIN) / WIN) * full
    cos_part[0] = math.sqrt(1.0 / WIN)
    sin_part[0] = np.where(spots % 2 == 0, 1.0, -1.0) * math.sqrt(1.0 / WIN)
    small = np.concatenate([cos_part, sin_part])
    angle = 2 * np.pi * ((3 * spots[:, None] + 1) * spots % WIN) / WIN
    root = math.sqrt(3.0) / 2
    large = full * np.block(
        [[np.cos(angle), -root * np.sin(angle)], [np.sin(angle), root * np.cos(angle)]]
    )
    freqs = np.concatenate([low_freq, low_freq, 3 * spots + 1])
    freqs[HALF] = WIN // 2
    taps = np.arange(THIRD)
    turn = 2 * np.pi * (freqs[:, None] * taps % WIN) / WIN
    keep = (taps < KW)[None, :]
    sines = np.sin(turn)
    sines[0] = 0.0
    sines[HALF] = 0.0
    waves = np.concatenate([np.cos(turn) * keep, sines * keep])

    sh, sl = hi_lo(small)
    gh, gl = hi_lo(large)
    wh, wl = hi_lo(waves)
    return dict(
        large=np.concatenate([gh, gl]),
        large_t=np.concatenate([gh.T, gl.T]),
        small=np.concatenate([sh, sl]),
        small_t=np.concatenate([sh.T, sl.T]),
        w_left=np.concatenate([wh, wl, wh], 1),
        w_right=np.concatenate([wh.T, wl.T, wh.T], 0),
    )


NAMES = ("large", "large_t", "small", "small_t")


def split(value):
    high = value.astype(BF)
    return high, (value - high.astype(F32)).astype(BF)


def dot(left, right):
    return jnp.dot(left, right, preferred_element_type=F32)


def right_large(value, table):
    high, low = split(value)
    return dot(
        jnp.concatenate([high, high, low], 1),
        jnp.concatenate([table[...], table[:SLOTS]], 0),
    )


def right_small(value, table):
    high, low = split(value)
    coarse, fine = table[:THIRD], table[THIRD:]
    both = dot(
        jnp.concatenate([high, low], 1),
        jnp.concatenate(
            [
                jnp.concatenate([coarse, fine], 1),
                jnp.concatenate([coarse, jnp.zeros_like(fine)], 1),
            ],
            0,
        ),
    )
    return both[:, :THIRD] + both[:, THIRD:]


def left_large(value, table):
    high, low = split(value)
    both = dot(table[...], high)
    return both[:SLOTS] + both[SLOTS:] + dot(table[:SLOTS], low)


def left_small(value, table):
    high, low = split(value)
    coarse, fine = table[:THIRD], table[THIRD:]
    both = dot(
        jnp.concatenate(
            [
                jnp.concatenate([coarse, coarse], 1),
                jnp.concatenate([fine, jnp.zeros_like(fine)], 1),
            ],
            0,
        ),
        jnp.concatenate([high, low], 0),
    )
    return both[:THIRD] + both[THIRD:]


def butterfly(first, second, third):
    total = second + third
    return first + total, first - 0.5 * total, second - third


def unbutterfly(plain, real, diff):
    base = plain - 0.5 * real
    return plain + real, base + diff, base - diff


def spectra_kernel(r):
    def body(slot, carry):
        @pl.when(r.occ[slot] != 0)
        def _():
            high, low = split(r.kernels[r.kid[slot]])
            half = dot(r.w_left[...], jnp.concatenate([high, high, low], 0))
            high, low = split(half)
            quads = dot(jnp.concatenate([high, high, low], 1), r.w_right[...])
            cc = quads[:SLOTS, :SLOTS]
            cs = quads[:SLOTS, SLOTS:]
            sc = quads[SLOTS:, :SLOTS]
            ss = quads[SLOTS:, SLOTS:]
            r.spec[slot, 0] = cc * cc + ss * ss + (sc * sc + cs * cs)
            r.spec[slot, 1] = 2.0 * (sc * cs - cc * ss)

        @pl.when(r.occ[slot] == 0)
        def _():
            r.spec[slot] = jnp.zeros((2, SLOTS, SLOTS), F32)

        return carry

    lax.fori_loop(0, r.spec.shape[0], body, 0)


def tile_of(block, num):
    return block[:, num * THIRD : (num + 1) * THIRD]


def lane_mask():
    return lax.broadcasted_iota(jnp.int32, (1, THIRD), 1) < HALF


def apply_spectrum(low_rows, high_rows, spec_ref, slot):
    sign = jnp.where(lane_mask(), -1.0, 1.0).astype(F32)

    def band(cos_rows, sin_rows, cos_at, sin_at, size):
        pc = spec_ref[slot, 0, pl.ds(cos_at, size), :]
        ps = spec_ref[slot, 0, pl.ds(sin_at, size), :] if sin_at != cos_at else pc
        cross = spec_ref[slot, 1, pl.ds(cos_at, size), :]
        d0, d1 = cross[:, :THIRD] * sign, cross[:, THIRD:]
        c0, c1, c2 = (tile_of(cos_rows, i) for i in range(3))
        s0, s1, s2 = (tile_of(sin_rows, i) for i in range(3))
        new_cos = jnp.concatenate(
            [
                pc[:, :THIRD] * c0 + d0 * pltpu.roll(s0, HALF, 1),
                pc[:, THIRD:] * c1 - d1 * s2,
                pc[:, THIRD:] * c2 + d1 * s1,
            ],
            1,
        )
        new_sin = jnp.concatenate(
            [
                ps[:, :THIRD] * s0 - d0 * pltpu.roll(c0, HALF, 1),
                ps[:, THIRD:] * s1 + d1 * c2,
                ps[:, THIRD:] * s2 - d1 * c1,
            ],
            1,
        )
        return new_cos, new_sin

    low = band(low_rows[:HALF], low_rows[HALF:], 0, HALF, HALF)
    high = band(high_rows[:THIRD], high_rows[THIRD:], THIRD, THIRD, THIRD)
    return jnp.concatenate(low, 0), jnp.concatenate(high, 0)


def window_products(windows, slots, r):
    count = len(windows)
    parts = []
    for blocks in windows:
        halves = []
        for block in blocks:
            plain, real, diff = butterfly(*(tile_of(block, i) for i in range(3)))
            halves.append(
                jnp.concatenate(
                    [
                        right_small(plain, r.small_t),
                        right_large(jnp.concatenate([real, diff], 1), r.large_t),
                    ],
                    1,
                )
            )
        parts.append(butterfly(*halves))
    plain, real, diff = (jnp.concatenate([part[i] for part in parts], 1) for i in range(3))
    low_rows = left_small(plain, r.small)
    high_rows = left_large(jnp.concatenate([real, diff], 0), r.large)
    bands = []
    for num, slot in enumerate(slots):
        here = slice(num * WIN, (num + 1) * WIN)
        bands.append(apply_spectrum(low_rows[:, here], high_rows[:, here], r.spec, slot))
    low_rows, high_rows = (jnp.concatenate([band[i] for band in bands], 1) for i in range(2))
    plain = left_small(low_rows, r.small_t)
    both = left_large(high_rows, r.large_t)
    rows = unbutterfly(plain, both[:THIRD], both[THIRD:])
    results = []
    for num in range(count):
        here = slice(num * WIN, (num + 1) * WIN)
        result = []
        for block in rows:
            block = block[:, here]
            plain = right_small(block[:, :THIRD], r.small)
            both = right_large(block[:, THIRD:], r.large)
            result.append(jnp.concatenate(unbutterfly(plain, both[:, :THIRD], both[:, THIRD:]), 1))
        results.append(result)
    return results


def fold8(value):
    rows = value.reshape(value.shape[0] // 8, 8, value.shape[1]).sum(0)
    return sum(tile_of(rows, i) for i in range(value.shape[1] // THIRD))


def total(value):
    return jnp.sum(jnp.sum(value, 0, keepdims=True), 1, keepdims=True)


def lanes_of(shape, *values):
    lanes = lax.broadcasted_iota(jnp.int32, shape, 1)
    out = jnp.zeros(shape, F32)
    for num, value in enumerate(values):
        out = jnp.where(lanes == num, value, out)
    return out


def rows_at(num, count=1):
    return pl.ds(num * THIRD, count * THIRD)


def put(ref, here, tiles):
    for num, tile in enumerate(tiles):
        ref[here, pl.ds(num * THIRD, THIRD)] = tile


def own_sum(r, num):
    last = 2 * r.tiles
    terms = []
    if num <= 2:
        terms.append((r.top_sum, num))
    if 2 <= num <= last - 2:
        terms.append((r.mid_sum, num - 2))
    if num >= last - 2:
        terms.append((r.low_sum, num - last + 2))
    return terms


def scalars(r):
    sums = jnp.sum(r.parts[...], 0, keepdims=True)
    energy, curve, cross = sums[:, 0:1], sums[:, 1:2], sums[:, 2:3]
    if r.stage == 1:
        return jnp.zeros_like(energy), energy / curve, energy, curve
    ratio = energy / r.coef[0:1, 0:1]
    power = curve + ratio * (2.0 * cross + ratio * r.coef[0:1, 1:2])
    return ratio, energy / power, energy, power


def update(r, num, old_refs, here, size, offset, spill, keep):
    ratio, step = r.ratio, r.step
    low = lane_mask()
    sums = [
        ref[pl.ds(block * THIRD + offset, size), :] for ref, block in own_sum(r, num)
    ]
    wide = pl.ds(num * THIRD + offset, size)
    west, east = r.from_left[wide, :], r.from_right[wide, :]
    add = [
        jnp.where(low, west, 0.0),
        jnp.where(low, 0.0, east),
        jnp.where(low, east, west),
    ]
    for block in sums + ([] if spill is None else [spill]):
        add = [a + tile_of(block, i) for i, a in enumerate(add)]
    old_res, old_dir, old_map, old_cor = old_refs
    old = old_res[here, :]
    direct = [tile_of(old, i) for i in range(3)]
    mapped = [a + b for a, b in zip(add, direct)]
    mapped[2] = mapped[2] * jnp.where(low, r.edge[3].astype(F32), r.edge[2].astype(F32))
    if keep is not None:
        mapped = [a * keep for a in mapped]
    fresh = list(direct)
    if r.stage > 1:
        past, was = old_map[here, :], old_dir[here, :]
        mapped = [a + ratio * tile_of(past, i) for i, a in enumerate(mapped)]
        direct = [a + ratio * tile_of(was, i) for i, a in enumerate(direct)]
    fresh = [a - step * b for a, b in zip(fresh, mapped)]
    return fresh, direct, mapped


def corrected_tiles(r, old_cor, here, direct):
    moved = [r.step * a for a in direct[:2]]
    if r.stage == 1:
        return moved
    old = old_cor[here, :]
    return [tile_of(old, i) + a for i, a in enumerate(moved)]


def store_state(r, name, here, fresh, direct, mapped):
    put(getattr(r, "res_" + name + "_new"), here, fresh)
    put(getattr(r, "map_" + name + "_new"), here, mapped)
    if r.stage > 1:
        put(getattr(r, "dir_" + name + "_new"), here, direct)


def old_of(r, name):
    return tuple(getattr(r, part + name, None) for part in ("res_", "dir_", "map_", "cor_"))


def unpacked_sides(r, start, size):
    half = r.side_left.shape[0]
    low = lane_mask()
    out = []
    while size:
        upper = start < half
        count = min(size, half - start) if upper else size
        here = pl.ds(start if upper else start - half, count)
        right, left = r.side_right[here, :], r.side_left[here, :]
        if upper:
            left = pltpu.roll(left, HALF, 1)
        else:
            right = pltpu.roll(right, HALF, 1)
        out.append(jnp.where(low, right, left))
        start, size = start + count, size - count
    return out[0] if len(out) == 1 else jnp.concatenate(out, 0)


def initial(r, start, size):
    here = pl.ds(start, size)
    block = r.observed[here, :]
    return [tile_of(block, 0), tile_of(block, 1), unpacked_sides(r, start, size)]


def pack_kernel(r):
    half = r.to_left.shape[0]
    low = lane_mask()
    first = [r.observed[pl.ds(start, half), pl.ds(0, THIRD)] for start in (0, half)]
    second = [r.observed[pl.ds(start, half), pl.ds(THIRD, THIRD)] for start in (0, half)]
    r.to_left[...] = jnp.where(low, first[0], pltpu.roll(first[1], HALF, 1))
    r.to_right[...] = jnp.where(low, pltpu.roll(second[0], HALF, 1), second[1])


def halo_kernel(r):
    put(r.to_up, pl.ds(0, HALO), initial(r, 0, HALO))
    put(r.to_down, pl.ds(0, HALO), initial(r, r.observed.shape[0] - HALO, HALO))


def row_strip_kernel(r):
    low = lane_mask()
    blocks = 2 * r.tiles + 1
    size = r.to_up.shape[0]
    for side, out in ((0, r.to_up), (1, r.to_down)):
        own = (r.top_sum, r.low_sum)[side][pl.ds(side * (WIN - size), size), :]
        if r.narrow:
            here = pl.ds(side * (blocks * HALO - size), size)
            west, east = r.from_left[here, :], r.from_right[here, :]
            if side:
                west = pltpu.roll(west, HALF, 1)
            else:
                east = pltpu.roll(east, HALF, 1)
            add = [jnp.where(low, west, 0.0), jnp.where(low, 0.0, east)]
        else:
            here = pl.ds(side * (blocks * THIRD - size), size)
            west, east = r.from_left[here, :], r.from_right[here, :]
            add = [
                jnp.where(low, west, 0.0),
                jnp.where(low, 0.0, east),
                jnp.where(low, east, west),
            ]
        put(out, pl.ds(0, size), [tile_of(own, i) + a for i, a in enumerate(add)])


def middle_kernel(r):
    square = cross = jnp.zeros((8, THIRD), F32)
    blocks = 2 * r.tiles + 1
    if r.stage > 0:
        r.ratio, r.step, _, _ = scalars(r)
    for num in range(1, blocks - 1):
        here = rows_at(num - 1)
        if r.stage == 0:
            fresh = initial(r, num * THIRD - HALO, THIRD)
            put(r.res_mid_new, here, fresh)
        else:
            fresh, direct, mapped = update(r, num, old_of(r, "mid"), here, THIRD, 0, None, None)
            store_state(r, "mid", here, fresh, direct, mapped)
            put(r.cor_mid_new, here, corrected_tiles(r, old_of(r, "mid")[3], here, direct))
            cross += sum(fold8(a * b) for a, b in zip(fresh[:2], mapped))
        square += sum(fold8(a * a) for a in fresh[:2])
    r.acc[0] = square
    r.acc[1] = cross
    r.acc[2] = jnp.zeros((8, THIRD), F32)
    inner = list(range(1, r.tiles - 1))
    some = r.occ[inner[0]]
    for slot in inner[1:]:
        some = some + r.occ[slot]

    @pl.when(some != 0)
    def _():
        windows = [
            [r.res_mid_new[rows_at(2 * slot + i - 1), :] for i in range(3)] for slot in inner
        ]
        results = window_products(windows, inner, r)
        curve = jnp.zeros((8, THIRD), F32)
        for num, (window, result) in enumerate(zip(windows, results)):
            curve += sum(fold8(a * b) for a, b in zip(window, result))
            first = result[0] if num == 0 else result[0] + results[num - 1][2]
            r.mid_sum_new[rows_at(2 * num), :] = first
            r.mid_sum_new[rows_at(2 * num + 1), :] = result[1]
        r.mid_sum_new[rows_at(2 * len(inner)), :] = results[-1][2]
        r.acc[2] = curve

    @pl.when(some == 0)
    def _():
        r.mid_sum_new[...] = jnp.zeros(r.mid_sum_new.shape, F32)


def edge_kernel(r):
    square, cross = r.acc[0], r.acc[1]
    blocks = 2 * r.tiles + 1
    rows = 2 * r.tiles * THIRD
    if r.stage > 0:
        r.ratio, r.step, energy, power = scalars(r)
        r.coef_new[...] = lanes_of((8, THIRD), energy, power)
    for side in range(2):
        num = side * (blocks - 1)
        for offset in (0, HALO):
            here = pl.ds(side * THIRD + offset, HALO)
            inside = (offset > 0) == (side == 0)
            if r.stage == 0:
                if inside:
                    fresh = initial(r, side * (rows - HALO), HALO)
                else:
                    halo = (r.above, r.below)[side][...]
                    fresh = [tile_of(halo, i) for i in range(3)]
                put(r.res_edge_new, here, fresh)
            else:
                spill = (r.above, r.below)[side][pl.ds(offset, HALO), :]
                keep = None if inside else r.edge[side].astype(F32)
                fresh, direct, mapped = update(
                    r, num, old_of(r, "edge"), here, HALO, offset, spill, keep
                )
                store_state(r, "edge", here, fresh, direct, mapped)
                if inside:
                    there = pl.ds(side * HALO, HALO)
                    put(r.cor_edge_new, there, corrected_tiles(r, old_of(r, "edge")[3], there, direct))
                    cross += sum(fold8(a * b) for a, b in zip(fresh[:2], mapped))
            if inside:
                square += sum(fold8(a * a) for a in fresh[:2])
    slots = [0, r.tiles - 1]
    some = r.occ[slots[0]] + r.occ[slots[1]]

    @pl.when(some != 0)
    def _():
        far = blocks - 4
        windows = [
            [r.res_edge_new[rows_at(0), :]] + [r.res_mid_new[rows_at(i), :] for i in range(2)],
            [r.res_mid_new[rows_at(far + i), :] for i in range(2)] + [r.res_edge_new[rows_at(1), :]],
        ]
        results = window_products(windows, slots, r)
        curve = jnp.zeros((8, THIRD), F32)
        for window, result, ref in zip(windows, results, (r.top_sum_new, r.low_sum_new)):
            curve += sum(fold8(a * b) for a, b in zip(window, result))
            for num in range(3):
                ref[rows_at(num), :] = result[num]
        r.curve[...] = curve

    @pl.when(some == 0)
    def _():
        r.top_sum_new[...] = jnp.zeros((WIN, WIN), F32)
        r.low_sum_new[...] = jnp.zeros((WIN, WIN), F32)
        r.curve[...] = jnp.zeros((8, THIRD), F32)

    low = lane_mask()
    new = Refs(tiles=r.tiles, top_sum=r.top_sum_new, mid_sum=r.mid_sum_new, low_sum=r.low_sum_new)
    if r.narrow:
        half = blocks * HALO
        for start in range(0, half, HALO):
            pair = []
            for row in (start, start + half):
                terms = [
                    ref[pl.ds(block * THIRD + row % THIRD, HALO), pl.ds(2 * THIRD, THIRD)]
                    for ref, block in own_sum(new, row // THIRD)
                ]
                pair.append(sum(terms[1:], terms[0]))
            here = pl.ds(start, HALO)
            r.to_right[here, :] = jnp.where(low, pair[0], pltpu.roll(pair[1], HALF, 1))
            r.to_left[here, :] = jnp.where(low, pltpu.roll(pair[0], HALF, 1), pair[1])
    else:
        for num in range(blocks):
            terms = [ref[rows_at(block), :] for ref, block in own_sum(new, num)]
            block = sum(terms[1:], terms[0])
            r.to_left[rows_at(num), :] = jnp.where(low, tile_of(block, 0), tile_of(block, 2))
            r.to_right[rows_at(num), :] = jnp.where(low, tile_of(block, 2), tile_of(block, 1))
    gamma = total(square)
    curve = gamma + total(r.acc[2] + r.curve[...])
    r.part[...] = lanes_of(r.part.shape, gamma, curve, total(cross))


def last_kernel(r):
    blocks = 2 * r.tiles + 1
    half = blocks * HALO
    r.ratio, r.step, _, _ = scalars(r)
    low = lane_mask()
    for start in range(HALO, 2 * half - HALO, HALO):
        num, offset = start // THIRD, start % THIRD
        upper = start < half
        wide = pl.ds(start if upper else start - half, HALO)
        west, east = r.from_left[wide, :], r.from_right[wide, :]
        if upper:
            east = pltpu.roll(east, HALF, 1)
        else:
            west = pltpu.roll(west, HALF, 1)
        add = [jnp.where(low, west, 0.0), jnp.where(low, 0.0, east)]
        for ref, block in own_sum(r, num):
            there = pl.ds(block * THIRD + offset, HALO)
            add = [a + ref[there, pl.ds(i * THIRD, THIRD)] for i, a in enumerate(add)]
        if start == HALO:
            add = [a + r.above[:, pl.ds(i * THIRD, THIRD)] for i, a in enumerate(add)]
        if start == 2 * half - 2 * HALO:
            add = [a + r.below[:, pl.ds(i * THIRD, THIRD)] for i, a in enumerate(add)]
        if num == 0 or num == blocks - 1:
            side = 0 if num == 0 else 1
            old, here, there = old_of(r, "edge"), pl.ds(side * THIRD + offset, HALO), pl.ds(side * HALO, HALO)
        else:
            old, here = old_of(r, "mid"), pl.ds(start - THIRD, HALO)
            there = here
        for i, a in enumerate(add):
            lanes = pl.ds(i * THIRD, THIRD)
            res = old[0][here, lanes]
            direct = res + r.ratio * old[1][here, lanes]
            mapped = a + res + r.ratio * old[2][here, lanes]
            out = pl.ds(start - HALO, HALO)
            r.corrected[out, lanes] = old[3][there, lanes] + r.step * direct
            r.residual[out, lanes] = res - r.step * mapped


class Refs:
    def __init__(self, **names):
        self.__dict__.update(names)


SCALARS = ("occ", "kid", "edge")
PARAMS = pltpu.CompilerParams(vmem_limit_bytes=16 * 1024 * 1024)


def run(body, ins, outs, scratch=None, **static):
    scratch = scratch or {}
    names = [*ins, *outs, *scratch]

    def kernel(*refs):
        body(Refs(**static, **dict(zip(names, refs))))

    result = pl.pallas_call(
        kernel,
        name=body.__name__,
        out_shape=[jax.ShapeDtypeStruct(dims, F32) for dims in outs.values()],
        in_specs=[
            pl.BlockSpec(memory_space=pltpu.SMEM if name in SCALARS else pltpu.VMEM) for name in ins
        ],
        out_specs=[pl.BlockSpec(memory_space=pltpu.VMEM)] * len(outs),
        scratch_shapes=[pltpu.VMEM(dims, F32) for dims in scratch.values()],
        compiler_params=PARAMS,
    )(*ins.values())
    return dict(zip(outs, result))


def own_part(table, tile_count):
    column = lax.dynamic_index_in_dim(table, lax.axis_index("col"), 1, keepdims=False)
    return lax.dynamic_slice_in_dim(column, lax.axis_index("row") * tile_count, tile_count)


def shift(value, axis, forward):
    count = lax.axis_size(axis)
    pairs = [(i, i + 1) for i in range(count - 1)]
    return lax.ppermute(value, axis, pairs if forward else [(b, a) for a, b in pairs])


def shards(observed, kernels, occupied, kernel_index):
    rows, cols = observed.shape
    tiles = rows // TILE
    half, mid, ext = rows // 2, rows - 2 * HALO, rows + 2 * HALO
    n_row, n_col = lax.axis_size("row"), lax.axis_size("col")
    devices = n_row * n_col
    my_row, my_col = lax.axis_index("row"), lax.axis_index("col")
    occ = own_part(occupied, tiles)
    edge = jnp.stack([my_row > 0, my_row < n_row - 1, my_col > 0, my_col < n_col - 1])
    host = {name: jnp.asarray(table) for name, table in tables().items()}
    sent = run(pack_kernel, dict(observed=observed), dict(to_left=(half, THIRD), to_right=(half, THIRD)))
    side_left = shift(sent["to_right"], "col", True)
    side_right = shift(sent["to_left"], "col", False)
    spec = run(
        spectra_kernel,
        dict(
            kid=own_part(kernel_index, tiles),
            occ=occ,
            kernels=jnp.pad(kernels, ((0, 0), (0, THIRD - KW), (0, THIRD - KW))),
            w_left=host["w_left"],
            w_right=host["w_right"],
        ),
        dict(spec=(tiles, 2, SLOTS, SLOTS)),
    )["spec"]
    side_left, side_right, spec, edge = lax.optimization_barrier(
        (side_left, side_right, spec, edge.astype(jnp.int32))
    )
    sides = dict(observed=observed, side_left=side_left, side_right=side_right)
    sent = run(halo_kernel, sides, dict(to_up=(HALO, WIN), to_down=(HALO, WIN)))
    above = shift(sent["to_down"], "row", True)
    below = shift(sent["to_up"], "row", False)
    fixed = dict(occ=occ, spec=spec, **{name: host[name] for name in NAMES})
    state = {}
    for stage in range(ITERS):
        narrow = stage == ITERS - 1
        moving = dict(sides) if stage == 0 else dict(from_left=from_left, from_right=from_right, parts=parts)
        if stage:
            moving["edge"] = edge
            if stage > 1:
                moving["coef"] = state["coef"]

        def old(names, where):
            parts_of = ["res_", "dir_", "map_", "cor_"] if stage > 1 else ["res_"] if stage else []
            return {name: state[name] for name in [a + where for a in parts_of] + (names if stage else [])}

        def new(where, height, cor_height):
            out = {"res_" + where + "_new": (height, WIN)}
            if stage:
                out["map_" + where + "_new"] = (height, WIN)
                out["cor_" + where + "_new"] = (cor_height, TILE)
            if stage > 1:
                out["dir_" + where + "_new"] = (height, WIN)
            return out

        sums = ["top_sum", "mid_sum", "low_sum"]
        middle = run(
            middle_kernel,
            {**fixed, **moving, **old(sums, "mid")},
            {**new("mid", mid, mid), "mid_sum_new": (mid - TILE, WIN), "acc": (3, 8, THIRD)},
            stage=stage,
            tiles=tiles,
        )
        outs = {**new("edge", TILE, THIRD), "top_sum_new": (WIN, WIN), "low_sum_new": (WIN, WIN)}
        strip = (ext // 2 if narrow else ext, THIRD)
        outs.update(to_left=strip, to_right=strip, part=(devices, THIRD))
        if stage:
            outs["coef_new"] = (8, THIRD)
        edges = run(
            edge_kernel,
            {
                **fixed,
                **moving,
                **old(["top_sum", "low_sum"], "edge"),
                "above": above,
                "below": below,
                **{name: middle[name] for name in ("res_mid_new", "mid_sum_new", "acc")},
            },
            outs,
            dict(curve=(8, THIRD)),
            stage=stage,
            tiles=tiles,
            narrow=narrow,
        )
        fresh = {**middle, **edges}
        if stage == 1:
            state["dir_mid"], state["dir_edge"] = state["res_mid"], state["res_edge"]
        for name, value in fresh.items():
            if name.endswith("_new"):
                state[name[:-4]] = value
        from_left = shift(edges["to_right"], "col", True)
        from_right = shift(edges["to_left"], "col", False)
        parts = lax.all_to_all(edges["part"], ("row", "col"), 0, 0, tiled=True)
        from_left, from_right, parts = lax.optimization_barrier((from_left, from_right, parts))

        strip = (HALO, TILE) if narrow else (THIRD, WIN)
        sent = run(
            row_strip_kernel,
            dict(
                from_left=from_left,
                from_right=from_right,
                top_sum=state["top_sum"],
                low_sum=state["low_sum"],
            ),
            dict(to_up=strip, to_down=strip),
            tiles=tiles,
            narrow=narrow,
        )
        above = shift(sent["to_down"], "row", True)
        below = shift(sent["to_up"], "row", False)

    names = [a + b for b in ("mid", "edge") for a in ("res_", "dir_", "map_", "cor_")]
    out = run(
        last_kernel,
        dict(
            parts=parts,
            from_left=from_left,
            from_right=from_right,
            above=above,
            below=below,
            **{name: state[name] for name in names + ["coef", "top_sum", "mid_sum", "low_sum"]},
        ),
        dict(corrected=(rows, cols), residual=(rows, cols)),
        stage=ITERS,
        tiles=tiles,
    )
    return out["corrected"], out["residual"]


def solution(mesh):
    placed = (P("row", "col"), P(), P(), P())
    return jax.shard_map(
        shards,
        mesh=mesh,
        in_specs=placed,
        out_specs=(P("row", "col"), P("row", "col")),
        check_vma=False,
    )
```

```python
import functools
import math

import jax
import jax.numpy as jnp
import numpy as np
from jax import lax
from jax.experimental import pallas as pl
from jax.experimental.pallas import tpu as pltpu
from jax.sharding import PartitionSpec as P

TILE = 256
HALO = 64
KW = 65
ITERS = 3
WIN = TILE + 2 * HALO
THIRD = WIN // 3
HALF = THIRD // 2
SLOTS = 2 * THIRD
BF = jnp.bfloat16
F32 = jnp.float32


def hi_lo(table):
    high = table.astype(np.float32).astype(jnp.bfloat16)
    low = (table - high.astype(np.float64)).astype(np.float32).astype(jnp.bfloat16)
    return high, low


@functools.cache
def tables():
    spots = np.arange(THIRD)
    low_freq = 3 * np.arange(HALF)
    full = math.sqrt(2.0 / WIN)
    cos_part = np.cos(2 * np.pi * (low_freq[:, None] * spots % WIN) / WIN) * full
    sin_part = np.sin(2 * np.pi * (low_freq[:, None] * spots % WIN) / WIN) * full
    cos_part[0] = math.sqrt(1.0 / WIN)
    sin_part[0] = np.where(spots % 2 == 0, 1.0, -1.0) * math.sqrt(1.0 / WIN)
    small = np.concatenate([cos_part, sin_part])
    angle = 2 * np.pi * ((3 * spots[:, None] + 1) * spots % WIN) / WIN
    root = math.sqrt(3.0) / 2
    large = full * np.block(
        [[np.cos(angle), -root * np.sin(angle)], [np.sin(angle), root * np.cos(angle)]]
    )
    freqs = np.concatenate([low_freq, low_freq, 3 * spots + 1])
    freqs[HALF] = WIN // 2
    taps = np.arange(THIRD)
    turn = 2 * np.pi * (freqs[:, None] * taps % WIN) / WIN
    keep = (taps < KW)[None, :]
    sines = np.sin(turn)
    sines[0] = 0.0
    sines[HALF] = 0.0
    waves = np.concatenate([np.cos(turn) * keep, sines * keep])

    sh, sl = hi_lo(small)
    gh, gl = hi_lo(large)
    wh, wl = hi_lo(waves)
    return dict(
        large=np.concatenate([gh, gl]),
        large_t=np.concatenate([gh.T, gl.T]),
        small=np.concatenate([sh, sl]),
        small_t=np.concatenate([sh.T, sl.T]),
        w_left=np.concatenate([wh, wl, wh], 1),
        w_right=np.concatenate([wh.T, wl.T, wh.T], 0),
    )


NAMES = ("large", "large_t", "small", "small_t")


def split(value):
    high = value.astype(BF)
    return high, (value - high.astype(F32)).astype(BF)


def dot(left, right):
    return jnp.dot(left, right, preferred_element_type=F32)


def right_large(value, table):
    high, low = split(value)
    return dot(
        jnp.concatenate([high, high, low], 1),
        jnp.concatenate([table[...], table[:SLOTS]], 0),
    )


def right_small(value, table):
    high, low = split(value)
    coarse, fine = table[:THIRD], table[THIRD:]
    both = dot(
        jnp.concatenate([high, low], 1),
        jnp.concatenate(
            [
                jnp.concatenate([coarse, fine], 1),
                jnp.concatenate([coarse, jnp.zeros_like(fine)], 1),
            ],
            0,
        ),
    )
    return both[:, :THIRD] + both[:, THIRD:]


def left_large(value, table):
    high, low = split(value)
    both = dot(table[...], high)
    return both[:SLOTS] + both[SLOTS:] + dot(table[:SLOTS], low)


def left_small(value, table):
    high, low = split(value)
    coarse, fine = table[:THIRD], table[THIRD:]
    both = dot(
        jnp.concatenate(
            [
                jnp.concatenate([coarse, coarse], 1),
                jnp.concatenate([fine, jnp.zeros_like(fine)], 1),
            ],
            0,
        ),
        jnp.concatenate([high, low], 0),
    )
    return both[:THIRD] + both[THIRD:]


def butterfly(first, second, third):
    total = second + third
    return first + total, first - 0.5 * total, second - third


def unbutterfly(plain, real, diff):
    base = plain - 0.5 * real
    return plain + real, base + diff, base - diff


def spectra_kernel(r):
    def body(slot, carry):
        @pl.when(r.occ[slot] != 0)
        def _():
            high, low = split(r.kernels[r.kid[slot]])
            half = dot(r.w_left[...], jnp.concatenate([high, high, low], 0))
            high, low = split(half)
            quads = dot(jnp.concatenate([high, high, low], 1), r.w_right[...])
            cc = quads[:SLOTS, :SLOTS]
            cs = quads[:SLOTS, SLOTS:]
            sc = quads[SLOTS:, :SLOTS]
            ss = quads[SLOTS:, SLOTS:]
            r.spec[slot, 0] = cc * cc + ss * ss + (sc * sc + cs * cs)
            r.spec[slot, 1] = 2.0 * (sc * cs - cc * ss)

        @pl.when(r.occ[slot] == 0)
        def _():
            r.spec[slot] = jnp.zeros((2, SLOTS, SLOTS), F32)

        return carry

    lax.fori_loop(0, r.spec.shape[0], body, 0)


def tile_of(block, num):
    return block[:, num * THIRD : (num + 1) * THIRD]


def lane_mask():
    return lax.broadcasted_iota(jnp.int32, (1, THIRD), 1) < HALF


def apply_spectrum(low_rows, high_rows, spec_ref, slot):
    sign = jnp.where(lane_mask(), -1.0, 1.0).astype(F32)

    def band(cos_rows, sin_rows, cos_at, sin_at, size):
        pc = spec_ref[slot, 0, pl.ds(cos_at, size), :]
        ps = spec_ref[slot, 0, pl.ds(sin_at, size), :] if sin_at != cos_at else pc
        cross = spec_ref[slot, 1, pl.ds(cos_at, size), :]
        d0, d1 = cross[:, :THIRD] * sign, cross[:, THIRD:]
        c0, c1, c2 = (tile_of(cos_rows, i) for i in range(3))
        s0, s1, s2 = (tile_of(sin_rows, i) for i in range(3))
        new_cos = jnp.concatenate(
            [
                pc[:, :THIRD] * c0 + d0 * pltpu.roll(s0, HALF, 1),
                pc[:, THIRD:] * c1 - d1 * s2,
                pc[:, THIRD:] * c2 + d1 * s1,
            ],
            1,
        )
        new_sin = jnp.concatenate(
            [
                ps[:, :THIRD] * s0 - d0 * pltpu.roll(c0, HALF, 1),
                ps[:, THIRD:] * s1 + d1 * c2,
                ps[:, THIRD:] * s2 - d1 * c1,
            ],
            1,
        )
        return new_cos, new_sin

    low = band(low_rows[:HALF], low_rows[HALF:], 0, HALF, HALF)
    high = band(high_rows[:THIRD], high_rows[THIRD:], THIRD, THIRD, THIRD)
    return jnp.concatenate(low, 0), jnp.concatenate(high, 0)


def window_products(windows, slots, r):
    count = len(windows)
    parts = []
    for blocks in windows:
        halves = []
        for block in blocks:
            plain, real, diff = butterfly(*(tile_of(block, i) for i in range(3)))
            halves.append(
                jnp.concatenate(
                    [
                        right_small(plain, r.small_t),
                        right_large(jnp.concatenate([real, diff], 1), r.large_t),
                    ],
                    1,
                )
            )
        parts.append(butterfly(*halves))
    plain, real, diff = (jnp.concatenate([part[i] for part in parts], 1) for i in range(3))
    low_rows = left_small(plain, r.small)
    high_rows = left_large(jnp.concatenate([real, diff], 0), r.large)
    bands = []
    for num, slot in enumerate(slots):
        here = slice(num * WIN, (num + 1) * WIN)
        bands.append(apply_spectrum(low_rows[:, here], high_rows[:, here], r.spec, slot))
    low_rows, high_rows = (jnp.concatenate([band[i] for band in bands], 1) for i in range(2))
    plain = left_small(low_rows, r.small_t)
    both = left_large(high_rows, r.large_t)
    rows = unbutterfly(plain, both[:THIRD], both[THIRD:])
    results = []
    for num in range(count):
        here = slice(num * WIN, (num + 1) * WIN)
        result = []
        for block in rows:
            block = block[:, here]
            plain = right_small(block[:, :THIRD], r.small)
            both = right_large(block[:, THIRD:], r.large)
            result.append(jnp.concatenate(unbutterfly(plain, both[:, :THIRD], both[:, THIRD:]), 1))
        results.append(result)
    return results


def fold8(value):
    rows = value.reshape(value.shape[0] // 8, 8, value.shape[1]).sum(0)
    return sum(tile_of(rows, i) for i in range(value.shape[1] // THIRD))


def total(value):
    return jnp.sum(jnp.sum(value, 0, keepdims=True), 1, keepdims=True)


def lanes_of(shape, *values):
    lanes = lax.broadcasted_iota(jnp.int32, shape, 1)
    out = jnp.zeros(shape, F32)
    for num, value in enumerate(values):
        out = jnp.where(lanes == num, value, out)
    return out


def rows_at(num, count=1):
    return pl.ds(num * THIRD, count * THIRD)


def put(ref, here, tiles):
    for num, tile in enumerate(tiles):
        ref[here, pl.ds(num * THIRD, THIRD)] = tile


def own_sum(r, num):
    last = 2 * r.tiles
    terms = []
    if num <= 2:
        terms.append((r.top_sum, num))
    if 2 <= num <= last - 2:
        terms.append((r.mid_sum, num - 2))
    if num >= last - 2:
        terms.append((r.low_sum, num - last + 2))
    return terms


def scalars(r):
    sums = jnp.sum(r.parts[...], 0, keepdims=True)
    energy, curve, cross = sums[:, 0:1], sums[:, 1:2], sums[:, 2:3]
    if r.stage == 1:
        r.steps, r.ratios = [energy / curve], []
        return energy, curve
    past = r.coef[0:1, :]
    ratio = energy / past[:, 0:1]
    power = curve + ratio * (2.0 * cross + ratio * past[:, 1:2])
    before = r.stage - 1
    r.steps = [past[:, 2 + i : 3 + i] for i in range(before)] + [energy / power]
    r.ratios = [past[:, 2 + ITERS + i : 3 + ITERS + i] for i in range(before - 1)] + [ratio]
    r.back = ratio / r.steps[-2]
    return energy, power


def pick(odd, first, second):
    return jnp.where(odd, first, second), jnp.where(odd, second, first)


def from_columns(r, here):
    return pick(r.edge[4] != 0, r.side_a[here, :], r.side_b[here, :])


def from_rows(r, side, here):
    return pick(r.edge[5] != 0, r.row_a[here, :], r.row_b[here, :])[side]


def send_columns(r, here, to_left, to_right):
    r.to_a[here, :], r.to_b[here, :] = pick(r.edge[4] != 0, to_left, to_right)


def send_rows(r, above, below):
    odd = r.edge[5] != 0
    here = pl.ds(0, r.to_a.shape[0])
    pairs = [pick(odd, a, b) for a, b in zip(above, below)]
    put(r.to_a, here, [a for a, _ in pairs])
    put(r.to_b, here, [b for _, b in pairs])


def old_of(r, name):
    return [getattr(r, "res%d_%s" % (i, name)) for i in range(r.stage)]


def update(r, num, name, here, size, offset, spill, keep):
    low = lane_mask()
    sums = [ref[pl.ds(block * THIRD + offset, size), :] for ref, block in own_sum(r, num)]
    west, east = from_columns(r, pl.ds(num * THIRD + offset, size))
    add = [
        jnp.where(low, west, 0.0),
        jnp.where(low, 0.0, east),
        jnp.where(low, east, west),
    ]
    for block in sums + ([] if spill is None else [spill]):
        add = [a + tile_of(block, i) for i, a in enumerate(add)]
    olds = [ref[here, :] for ref in old_of(r, name)[-2:]]
    old = [tile_of(olds[-1], i) for i in range(3)]
    mapped = [a + b for a, b in zip(add, old)]
    mapped[2] = mapped[2] * jnp.where(low, r.edge[3].astype(F32), r.edge[2].astype(F32))
    if keep is not None:
        mapped = [a * keep for a in mapped]
    if r.stage > 1:
        mapped = [a + r.back * (tile_of(olds[0], i) - old[i]) for i, a in enumerate(mapped)]
    return [a - r.steps[-1] * b for a, b in zip(old, mapped)], mapped


def unpacked_sides(r, start, size):
    half = r.side_a.shape[0]
    low = lane_mask()
    out = []
    while size:
        upper = start < half
        count = min(size, half - start) if upper else size
        here = pl.ds(start if upper else start - half, count)
        left, right = from_columns(r, here)
        if upper:
            left = pltpu.roll(left, HALF, 1)
        else:
            right = pltpu.roll(right, HALF, 1)
        out.append(jnp.where(low, right, left))
        start, size = start + count, size - count
    return out[0] if len(out) == 1 else jnp.concatenate(out, 0)


def initial(r, start, size):
    here = pl.ds(start, size)
    block = r.observed[here, :]
    return [tile_of(block, 0), tile_of(block, 1), unpacked_sides(r, start, size)]


def pack_kernel(r):
    half = r.to_a.shape[0]
    low = lane_mask()
    first = [r.observed[pl.ds(start, half), pl.ds(0, THIRD)] for start in (0, half)]
    second = [r.observed[pl.ds(start, half), pl.ds(THIRD, THIRD)] for start in (0, half)]
    send_columns(
        r,
        pl.ds(0, half),
        jnp.where(low, first[0], pltpu.roll(first[1], HALF, 1)),
        jnp.where(low, pltpu.roll(second[0], HALF, 1), second[1]),
    )


def halo_kernel(r):
    send_rows(r, initial(r, 0, HALO), initial(r, r.observed.shape[0] - HALO, HALO))


def row_strip_kernel(r):
    low = lane_mask()
    blocks = 2 * r.tiles + 1
    size = r.to_a.shape[0]
    strips = []
    for side, ref in ((0, r.top_sum), (1, r.low_sum)):
        own = ref[pl.ds(side * (WIN - size), size), :]
        if r.narrow:
            west, east = from_columns(r, pl.ds(side * (blocks * HALO - size), size))
            if side:
                west = pltpu.roll(west, HALF, 1)
            else:
                east = pltpu.roll(east, HALF, 1)
            add = [jnp.where(low, west, 0.0), jnp.where(low, 0.0, east)]
        else:
            west, east = from_columns(r, pl.ds(side * (blocks * THIRD - size), size))
            add = [
                jnp.where(low, west, 0.0),
                jnp.where(low, 0.0, east),
                jnp.where(low, east, west),
            ]
        strips.append([tile_of(own, i) + a for i, a in enumerate(add)])
    send_rows(r, *strips)


def middle_kernel(r):
    square = cross = jnp.zeros((8, THIRD), F32)
    blocks = 2 * r.tiles + 1
    if r.stage > 0:
        scalars(r)
    for num in range(1, blocks - 1):
        here = rows_at(num - 1)
        if r.stage == 0:
            fresh = initial(r, num * THIRD - HALO, THIRD)
        else:
            fresh, mapped = update(r, num, "mid", here, THIRD, 0, None, None)
            cross += sum(fold8(a * b) for a, b in zip(fresh[:2], mapped))
        put(r.res_mid_new, here, fresh)
        square += sum(fold8(a * a) for a in fresh[:2])
    r.acc[0] = square
    r.acc[1] = cross
    r.acc[2] = jnp.zeros((8, THIRD), F32)
    inner = list(range(1, r.tiles - 1))
    some = r.occ[inner[0]]
    for slot in inner[1:]:
        some = some + r.occ[slot]

    @pl.when(some != 0)
    def _():
        windows = [
            [r.res_mid_new[rows_at(2 * slot + i - 1), :] for i in range(3)] for slot in inner
        ]
        results = window_products(windows, inner, r)
        curve = jnp.zeros((8, THIRD), F32)
        for num, (window, result) in enumerate(zip(windows, results)):
            curve += sum(fold8(a * b) for a, b in zip(window, result))
            first = result[0] if num == 0 else result[0] + results[num - 1][2]
            r.mid_sum_new[rows_at(2 * num), :] = first
            r.mid_sum_new[rows_at(2 * num + 1), :] = result[1]
        r.mid_sum_new[rows_at(2 * len(inner)), :] = results[-1][2]
        r.acc[2] = curve

    @pl.when(some == 0)
    def _():
        r.mid_sum_new[...] = jnp.zeros(r.mid_sum_new.shape, F32)


def edge_kernel(r):
    square, cross = r.acc[0], r.acc[1]
    blocks = 2 * r.tiles + 1
    rows = 2 * r.tiles * THIRD
    if r.stage > 0:
        energy, power = scalars(r)
        fill = [jnp.zeros_like(energy)] * (ITERS - len(r.steps))
        r.coef_new[...] = lanes_of((8, THIRD), energy, power, *r.steps, *fill, *r.ratios)
    for side in range(2):
        num = side * (blocks - 1)
        for offset in (0, HALO):
            here = pl.ds(side * THIRD + offset, HALO)
            inside = (offset > 0) == (side == 0)
            if r.stage == 0:
                if inside:
                    fresh = initial(r, side * (rows - HALO), HALO)
                else:
                    halo = from_rows(r, side, pl.ds(0, HALO))
                    fresh = [tile_of(halo, i) for i in range(3)]
            else:
                spill = from_rows(r, side, pl.ds(offset, HALO))
                keep = None if inside else r.edge[side].astype(F32)
                fresh, mapped = update(r, num, "edge", here, HALO, offset, spill, keep)
                if inside:
                    cross += sum(fold8(a * b) for a, b in zip(fresh[:2], mapped))
            put(r.res_edge_new, here, fresh)
            if inside:
                square += sum(fold8(a * a) for a in fresh[:2])
    slots = [0, r.tiles - 1]
    some = r.occ[slots[0]] + r.occ[slots[1]]

    @pl.when(some != 0)
    def _():
        far = blocks - 4
        windows = [
            [r.res_edge_new[rows_at(0), :]] + [r.res_mid_new[rows_at(i), :] for i in range(2)],
            [r.res_mid_new[rows_at(far + i), :] for i in range(2)] + [r.res_edge_new[rows_at(1), :]],
        ]
        results = window_products(windows, slots, r)
        curve = jnp.zeros((8, THIRD), F32)
        for window, result, ref in zip(windows, results, (r.top_sum_new, r.low_sum_new)):
            curve += sum(fold8(a * b) for a, b in zip(window, result))
            for num in range(3):
                ref[rows_at(num), :] = result[num]
        r.curve[...] = curve

    @pl.when(some == 0)
    def _():
        r.top_sum_new[...] = jnp.zeros((WIN, WIN), F32)
        r.low_sum_new[...] = jnp.zeros((WIN, WIN), F32)
        r.curve[...] = jnp.zeros((8, THIRD), F32)

    low = lane_mask()
    new = Refs(tiles=r.tiles, top_sum=r.top_sum_new, mid_sum=r.mid_sum_new, low_sum=r.low_sum_new)
    if r.narrow:
        half = blocks * HALO
        for start in range(0, half, HALO):
            pair = []
            for row in (start, start + half):
                terms = [
                    ref[pl.ds(block * THIRD + row % THIRD, HALO), pl.ds(2 * THIRD, THIRD)]
                    for ref, block in own_sum(new, row // THIRD)
                ]
                pair.append(sum(terms[1:], terms[0]))
            here = pl.ds(start, HALO)
            send_columns(
                r,
                here,
                jnp.where(low, pltpu.roll(pair[0], HALF, 1), pair[1]),
                jnp.where(low, pair[0], pltpu.roll(pair[1], HALF, 1)),
            )
    else:
        for num in range(blocks):
            terms = [ref[rows_at(block), :] for ref, block in own_sum(new, num)]
            block = sum(terms[1:], terms[0])
            send_columns(
                r,
                rows_at(num),
                jnp.where(low, tile_of(block, 0), tile_of(block, 2)),
                jnp.where(low, tile_of(block, 2), tile_of(block, 1)),
            )
    gamma = total(square)
    curve = gamma + total(r.acc[2] + r.curve[...])
    r.part[...] = lanes_of(r.part.shape, gamma, curve, total(cross))


def last_kernel(r):
    blocks = 2 * r.tiles + 1
    half = blocks * HALO
    scalars(r)
    low = lane_mask()
    for start in range(HALO, 2 * half - HALO, HALO):
        num, offset = start // THIRD, start % THIRD
        upper = start < half
        wide = pl.ds(start if upper else start - half, HALO)
        west, east = from_columns(r, wide)
        if upper:
            east = pltpu.roll(east, HALF, 1)
        else:
            west = pltpu.roll(west, HALF, 1)
        add = [jnp.where(low, west, 0.0), jnp.where(low, 0.0, east)]
        for ref, block in own_sum(r, num):
            there = pl.ds(block * THIRD + offset, HALO)
            add = [a + ref[there, pl.ds(i * THIRD, THIRD)] for i, a in enumerate(add)]
        for side, edge in ((0, HALO), (1, 2 * half - 2 * HALO)):
            if start == edge:
                spill = from_rows(r, side, pl.ds(0, HALO))
                add = [a + tile_of(spill, i) for i, a in enumerate(add)]
        if num == 0 or num == blocks - 1:
            olds, here = old_of(r, "edge"), pl.ds((0 if num == 0 else THIRD) + offset, HALO)
        else:
            olds, here = old_of(r, "mid"), pl.ds(start - THIRD, HALO)
        for i, a in enumerate(add):
            lanes = pl.ds(i * THIRD, THIRD)
            past = [ref[here, lanes] for ref in olds]
            direct = past[0]
            moved = r.steps[0] * direct
            for old, ratio, step in zip(past[1:], r.ratios, r.steps[1:]):
                direct = old + ratio * direct
                moved = moved + step * direct
            mapped = a + past[-1] + r.back * (past[-2] - past[-1])
            out = pl.ds(start - HALO, HALO)
            r.corrected[out, lanes] = moved
            r.residual[out, lanes] = past[-1] - r.steps[-1] * mapped


class Refs:
    def __init__(self, **names):
        self.__dict__.update(names)


SCALARS = ("occ", "kid", "edge")
PARAMS = pltpu.CompilerParams(vmem_limit_bytes=16 * 1024 * 1024)


def run(body, ins, outs, scratch=None, **static):
    scratch = scratch or {}
    names = [*ins, *outs, *scratch]

    def kernel(*refs):
        body(Refs(**static, **dict(zip(names, refs))))

    result = pl.pallas_call(
        kernel,
        name=body.__name__,
        out_shape=[jax.ShapeDtypeStruct(dims, F32) for dims in outs.values()],
        in_specs=[
            pl.BlockSpec(memory_space=pltpu.SMEM if name in SCALARS else pltpu.VMEM) for name in ins
        ],
        out_specs=[pl.BlockSpec(memory_space=pltpu.VMEM)] * len(outs),
        scratch_shapes=[pltpu.VMEM(dims, F32) for dims in scratch.values()],
        compiler_params=PARAMS,
    )(*ins.values())
    return dict(zip(outs, result))


def own_part(table, tile_count):
    column = lax.dynamic_index_in_dim(table, lax.axis_index("col"), 1, keepdims=False)
    return lax.dynamic_slice_in_dim(column, lax.axis_index("row") * tile_count, tile_count)


def exchange(to_a, to_b, axis):
    count = lax.axis_size(axis)
    out = []
    for value, first in ((to_b, 1), (to_a, 0)):
        pairs = [(i, i + 1) for i in range(first, count - 1, 2)]
        out.append(lax.ppermute(value, axis, pairs + [(b, a) for a, b in pairs]))
    return out[1], out[0]


def shards(observed, kernels, occupied, kernel_index):
    rows, cols = observed.shape
    tiles = rows // TILE
    half, mid, ext = rows // 2, rows - 2 * HALO, rows + 2 * HALO
    n_row, n_col = lax.axis_size("row"), lax.axis_size("col")
    devices = n_row * n_col
    my_row, my_col = lax.axis_index("row"), lax.axis_index("col")
    occ = own_part(occupied, tiles)
    edge = jnp.stack(
        [my_row > 0, my_row < n_row - 1, my_col > 0, my_col < n_col - 1, my_col % 2 == 1, my_row % 2 == 1]
    ).astype(jnp.int32)
    host = {name: jnp.asarray(table) for name, table in tables().items()}
    sent = run(pack_kernel, dict(edge=edge, observed=observed), dict(to_a=(half, THIRD), to_b=(half, THIRD)))
    side_a, side_b = exchange(sent["to_a"], sent["to_b"], "col")
    spec = run(
        spectra_kernel,
        dict(
            kid=own_part(kernel_index, tiles),
            occ=occ,
            kernels=jnp.pad(kernels, ((0, 0), (0, THIRD - KW), (0, THIRD - KW))),
            w_left=host["w_left"],
            w_right=host["w_right"],
        ),
        dict(spec=(tiles, 2, SLOTS, SLOTS)),
    )["spec"]
    side_a, side_b, spec = lax.optimization_barrier((side_a, side_b, spec))
    sides = dict(edge=edge, side_a=side_a, side_b=side_b)
    sent = run(halo_kernel, dict(observed=observed, **sides), dict(to_a=(HALO, WIN), to_b=(HALO, WIN)))
    row_a, row_b = exchange(sent["to_a"], sent["to_b"], "row")
    fixed = dict(occ=occ, spec=spec, **{name: host[name] for name in NAMES})
    state = {}
    for stage in range(ITERS):
        narrow = stage == ITERS - 1
        moving = dict(sides)
        if stage == 0:
            moving["observed"] = observed
        else:
            moving["parts"] = parts
        if stage > 1:
            moving["coef"] = state["coef_new"]

        def old(where, *sums):
            names = ["res%d_%s" % (i, where) for i in range(stage)]
            return {name: state[name] for name in names + list(sums) if stage}

        middle = run(
            middle_kernel,
            {**fixed, **moving, **old("mid", "top_sum", "mid_sum", "low_sum")},
            {"res_mid_new": (mid, WIN), "mid_sum_new": (mid - TILE, WIN), "acc": (3, 8, THIRD)},
            stage=stage,
            tiles=tiles,
        )
        outs = {"res_edge_new": (TILE, WIN), "top_sum_new": (WIN, WIN), "low_sum_new": (WIN, WIN)}
        strip = (ext // 2 if narrow else ext, THIRD)
        outs.update(to_a=strip, to_b=strip, part=(devices, THIRD))
        if stage:
            outs["coef_new"] = (8, THIRD)
        edges = run(
            edge_kernel,
            {
                **fixed,
                **moving,
                **old("edge", "top_sum", "low_sum"),
                "row_a": row_a,
                "row_b": row_b,
                **{name: middle[name] for name in ("res_mid_new", "mid_sum_new", "acc")},
            },
            outs,
            dict(curve=(8, THIRD)),
            stage=stage,
            tiles=tiles,
            narrow=narrow,
        )
        state["res%d_mid" % stage] = middle["res_mid_new"]
        state["res%d_edge" % stage] = edges["res_edge_new"]
        state["mid_sum"] = middle["mid_sum_new"]
        state["top_sum"] = edges["top_sum_new"]
        state["low_sum"] = edges["low_sum_new"]
        state["coef_new"] = edges.get("coef_new")
        side_a, side_b = exchange(edges["to_a"], edges["to_b"], "col")
        parts = lax.all_to_all(edges["part"], ("row", "col"), 0, 0, tiled=True)
        side_a, side_b, parts = lax.optimization_barrier((side_a, side_b, parts))
        sides = dict(edge=edge, side_a=side_a, side_b=side_b)
        strip = (HALO, TILE) if narrow else (THIRD, WIN)
        sent = run(
            row_strip_kernel,
            dict(top_sum=state["top_sum"], low_sum=state["low_sum"], **sides),
            dict(to_a=strip, to_b=strip),
            tiles=tiles,
            narrow=narrow,
        )
        row_a, row_b = exchange(sent["to_a"], sent["to_b"], "row")

    names = ["res%d_%s" % (i, where) for i in range(ITERS) for where in ("mid", "edge")]
    out = run(
        last_kernel,
        dict(
            parts=parts,
            coef=state["coef_new"],
            row_a=row_a,
            row_b=row_b,
            **sides,
            **{name: state[name] for name in names + ["top_sum", "mid_sum", "low_sum"]},
        ),
        dict(corrected=(rows, cols), residual=(rows, cols)),
        stage=ITERS,
        tiles=tiles,
    )
    return out["corrected"], out["residual"]


def solution(mesh):
    placed = (P("row", "col"), P(), P(), P())
    return jax.shard_map(
        shards,
        mesh=mesh,
        in_specs=placed,
        out_specs=(P("row", "col"), P("row", "col")),
        check_vma=False,
    )
```

```python
import functools
import math

import jax
import jax.numpy as jnp
import numpy as np
from jax import lax
from jax.experimental import pallas as pl
from jax.experimental.pallas import tpu as pltpu
from jax.sharding import PartitionSpec as P

TILE = 256
HALO = 64
KW = 65
ITERS = 3
WIN = TILE + 2 * HALO
THIRD = WIN // 3
HALF = THIRD // 2
SLOTS = 2 * THIRD
BF = jnp.bfloat16
F32 = jnp.float32


def hi_lo(table):
    high = table.astype(np.float32).astype(jnp.bfloat16)
    low = (table - high.astype(np.float64)).astype(np.float32).astype(jnp.bfloat16)
    return high, low


@functools.cache
def tables():
    spots = np.arange(THIRD)
    low_freq = 3 * np.arange(HALF)
    full = math.sqrt(2.0 / WIN)
    cos_part = np.cos(2 * np.pi * (low_freq[:, None] * spots % WIN) / WIN) * full
    sin_part = np.sin(2 * np.pi * (low_freq[:, None] * spots % WIN) / WIN) * full
    cos_part[0] = math.sqrt(1.0 / WIN)
    sin_part[0] = np.where(spots % 2 == 0, 1.0, -1.0) * math.sqrt(1.0 / WIN)
    small = np.concatenate([cos_part, sin_part])
    angle = 2 * np.pi * ((3 * spots[:, None] + 1) * spots % WIN) / WIN
    root = math.sqrt(3.0) / 2
    large = full * np.block(
        [[np.cos(angle), -root * np.sin(angle)], [np.sin(angle), root * np.cos(angle)]]
    )
    freqs = np.concatenate([low_freq, low_freq, 3 * spots + 1])
    freqs[HALF] = WIN // 2
    taps = np.arange(THIRD)
    turn = 2 * np.pi * (freqs[:, None] * taps % WIN) / WIN
    keep = (taps < KW)[None, :]
    sines = np.sin(turn)
    sines[0] = 0.0
    sines[HALF] = 0.0
    waves = np.concatenate([np.cos(turn) * keep, sines * keep])

    sh, sl = hi_lo(small)
    gh, gl = hi_lo(large)
    wh, wl = hi_lo(waves)
    return dict(
        large=np.concatenate([gh, gl]),
        large_t=np.concatenate([gh.T, gl.T]),
        small=np.concatenate([sh, sl]),
        small_t=np.concatenate([sh.T, sl.T]),
        w_left=np.concatenate([wh, wl, wh], 1),
        w_right=np.concatenate([wh.T, wl.T, wh.T], 0),
    )


NAMES = ("large", "large_t", "small", "small_t")


def split(value):
    high = value.astype(BF)
    return high, (value - high.astype(F32)).astype(BF)


def dot(left, right):
    return jnp.dot(left, right, preferred_element_type=F32)


def right_large(value, table):
    high, low = split(value)
    return dot(
        jnp.concatenate([high, high, low], 1),
        jnp.concatenate([table[...], table[:SLOTS]], 0),
    )


def right_small(value, table):
    high, low = split(value)
    coarse, fine = table[:THIRD], table[THIRD:]
    both = dot(
        jnp.concatenate([high, low], 1),
        jnp.concatenate(
            [
                jnp.concatenate([coarse, fine], 1),
                jnp.concatenate([coarse, jnp.zeros_like(fine)], 1),
            ],
            0,
        ),
    )
    return both[:, :THIRD] + both[:, THIRD:]


def left_large(value, table):
    high, low = split(value)
    both = dot(table[...], high)
    return both[:SLOTS] + both[SLOTS:] + dot(table[:SLOTS], low)


def left_small(value, table):
    high, low = split(value)
    coarse, fine = table[:THIRD], table[THIRD:]
    both = dot(
        jnp.concatenate(
            [
                jnp.concatenate([coarse, coarse], 1),
                jnp.concatenate([fine, jnp.zeros_like(fine)], 1),
            ],
            0,
        ),
        jnp.concatenate([high, low], 0),
    )
    return both[:THIRD] + both[THIRD:]


def butterfly(first, second, third):
    total = second + third
    return first + total, first - 0.5 * total, second - third


def unbutterfly(plain, real, diff):
    base = plain - 0.5 * real
    return plain + real, base + diff, base - diff


def spectra_kernel(r):
    def body(slot, carry):
        @pl.when(r.occ[slot] != 0)
        def _():
            high, low = split(r.kernels[r.kid[slot]])
            half = dot(r.w_left[...], jnp.concatenate([high, high, low], 0))
            high, low = split(half)
            quads = dot(jnp.concatenate([high, high, low], 1), r.w_right[...])
            cc = quads[:SLOTS, :SLOTS]
            cs = quads[:SLOTS, SLOTS:]
            sc = quads[SLOTS:, :SLOTS]
            ss = quads[SLOTS:, SLOTS:]
            r.spec[slot, 0] = cc * cc + ss * ss + (sc * sc + cs * cs)
            r.spec[slot, 1] = 2.0 * (sc * cs - cc * ss)

        @pl.when(r.occ[slot] == 0)
        def _():
            r.spec[slot] = jnp.zeros((2, SLOTS, SLOTS), F32)

        return carry

    lax.fori_loop(0, r.spec.shape[0], body, 0)


def tile_of(block, num):
    return block[:, num * THIRD : (num + 1) * THIRD]


def lane_mask():
    return lax.broadcasted_iota(jnp.int32, (1, THIRD), 1) < HALF


def apply_spectrum(low_rows, high_rows, spec_ref, slot):
    sign = jnp.where(lane_mask(), -1.0, 1.0).astype(F32)

    def band(cos_rows, sin_rows, cos_at, sin_at, size):
        pc = spec_ref[slot, 0, pl.ds(cos_at, size), :]
        ps = spec_ref[slot, 0, pl.ds(sin_at, size), :] if sin_at != cos_at else pc
        cross = spec_ref[slot, 1, pl.ds(cos_at, size), :]
        d0, d1 = cross[:, :THIRD] * sign, cross[:, THIRD:]
        c0, c1, c2 = (tile_of(cos_rows, i) for i in range(3))
        s0, s1, s2 = (tile_of(sin_rows, i) for i in range(3))
        new_cos = jnp.concatenate(
            [
                pc[:, :THIRD] * c0 + d0 * pltpu.roll(s0, HALF, 1),
                pc[:, THIRD:] * c1 - d1 * s2,
                pc[:, THIRD:] * c2 + d1 * s1,
            ],
            1,
        )
        new_sin = jnp.concatenate(
            [
                ps[:, :THIRD] * s0 - d0 * pltpu.roll(c0, HALF, 1),
                ps[:, THIRD:] * s1 + d1 * c2,
                ps[:, THIRD:] * s2 - d1 * c1,
            ],
            1,
        )
        return new_cos, new_sin

    low = band(low_rows[:HALF], low_rows[HALF:], 0, HALF, HALF)
    high = band(high_rows[:THIRD], high_rows[THIRD:], THIRD, THIRD, THIRD)
    return jnp.concatenate(low, 0), jnp.concatenate(high, 0)


def window_products(windows, slots, r):
    count = len(windows)
    parts = []
    for blocks in windows:
        halves = []
        for block in blocks:
            plain, real, diff = butterfly(*(tile_of(block, i) for i in range(3)))
            halves.append(
                jnp.concatenate(
                    [
                        right_small(plain, r.small_t),
                        right_large(jnp.concatenate([real, diff], 1), r.large_t),
                    ],
                    1,
                )
            )
        parts.append(butterfly(*halves))
    plain, real, diff = (jnp.concatenate([part[i] for part in parts], 1) for i in range(3))
    low_rows = left_small(plain, r.small)
    high_rows = left_large(jnp.concatenate([real, diff], 0), r.large)
    bands = []
    for num, slot in enumerate(slots):
        here = slice(num * WIN, (num + 1) * WIN)
        bands.append(apply_spectrum(low_rows[:, here], high_rows[:, here], r.spec, slot))
    low_rows, high_rows = (jnp.concatenate([band[i] for band in bands], 1) for i in range(2))
    plain = left_small(low_rows, r.small_t)
    both = left_large(high_rows, r.large_t)
    rows = unbutterfly(plain, both[:THIRD], both[THIRD:])
    results = []
    for num in range(count):
        here = slice(num * WIN, (num + 1) * WIN)
        result = []
        for block in rows:
            block = block[:, here]
            plain = right_small(block[:, :THIRD], r.small)
            both = right_large(block[:, THIRD:], r.large)
            result.append(jnp.concatenate(unbutterfly(plain, both[:, :THIRD], both[:, THIRD:]), 1))
        results.append(result)
    return results


def fold8(value):
    rows = value.reshape(value.shape[0] // 8, 8, value.shape[1]).sum(0)
    return sum(tile_of(rows, i) for i in range(value.shape[1] // THIRD))


def total(value):
    return jnp.sum(jnp.sum(value, 0, keepdims=True), 1, keepdims=True)


def lanes_of(shape, *values):
    lanes = lax.broadcasted_iota(jnp.int32, shape, 1)
    out = jnp.zeros(shape, F32)
    for num, value in enumerate(values):
        out = jnp.where(lanes == num, value, out)
    return out


def rows_at(num, count=1):
    return pl.ds(num * THIRD, count * THIRD)


def put(ref, here, tiles):
    for num, tile in enumerate(tiles):
        ref[here, pl.ds(num * THIRD, THIRD)] = tile


def own_sum(r, num):
    last = 2 * r.tiles
    terms = []
    if num <= 2:
        terms.append((r.top_sum, num))
    if 2 <= num <= last - 2:
        terms.append((r.mid_sum, num - 2))
    if num >= last - 2:
        terms.append((r.low_sum, num - last + 2))
    return terms


def scalars(r):
    sums = jnp.sum(r.parts[...], 0, keepdims=True)
    energy, curve, cross = sums[:, 0:1], sums[:, 1:2], sums[:, 2:3]
    if r.stage == 1:
        r.steps, r.ratios = [energy / curve], []
        return energy, curve
    past = r.coef[0:1, :]
    ratio = energy / past[:, 0:1]
    power = curve + ratio * (2.0 * cross + ratio * past[:, 1:2])
    before = r.stage - 1
    r.steps = [past[:, 2 + i : 3 + i] for i in range(before)] + [energy / power]
    r.ratios = [past[:, 2 + ITERS + i : 3 + ITERS + i] for i in range(before - 1)] + [ratio]
    r.back = ratio / r.steps[-2]
    return energy, power


def pick(odd, first, second):
    return jnp.where(odd, first, second), jnp.where(odd, second, first)


def from_columns(r, start, size):
    second = getattr(r, "side_b", None)
    there = start
    if second is None:
        middle = r.side_mid.shape[0]
        if start < WIN:
            second = r.side_end
        elif start < WIN + middle:
            second, there = r.side_mid, start - WIN
        else:
            second, there = r.side_end, start - middle
    return pick(r.edge[4] != 0, r.side_z[pl.ds(start, size), :], second[pl.ds(there, size), :])


def from_rows(r, side, here):
    return pick(r.edge[5] != 0, r.row_a[here, :], r.row_b[here, :])[side]


def send_columns(r, here, to_left, to_right):
    r.to_a[here, :], r.to_b[here, :] = pick(r.edge[4] != 0, to_left, to_right)


def strips_of(terms):
    low = lane_mask()
    pieces = [ref[rows_at(block), :] for ref, block in terms]
    block = sum(pieces[1:], pieces[0])
    return (
        jnp.where(low, tile_of(block, 0), tile_of(block, 2)),
        jnp.where(low, tile_of(block, 2), tile_of(block, 1)),
    )


def send_rows(r, above, below):
    odd = r.edge[5] != 0
    here = pl.ds(0, r.to_a.shape[0])
    pairs = [pick(odd, a, b) for a, b in zip(above, below)]
    put(r.to_a, here, [a for a, _ in pairs])
    put(r.to_b, here, [b for _, b in pairs])


def old_of(r, name):
    return [getattr(r, "res%d_%s" % (i, name)) for i in range(r.stage)]


def update(r, num, name, here, size, offset, spill, keep):
    low = lane_mask()
    sums = [ref[pl.ds(block * THIRD + offset, size), :] for ref, block in own_sum(r, num)]
    west, east = from_columns(r, num * THIRD + offset, size)
    add = [
        jnp.where(low, west, 0.0),
        jnp.where(low, 0.0, east),
        jnp.where(low, east, west),
    ]
    for block in sums + ([] if spill is None else [spill]):
        add = [a + tile_of(block, i) for i, a in enumerate(add)]
    olds = [ref[here, :] for ref in old_of(r, name)[-2:]]
    old = [tile_of(olds[-1], i) for i in range(3)]
    mapped = [a + b for a, b in zip(add, old)]
    mapped[2] = mapped[2] * jnp.where(low, r.edge[3].astype(F32), r.edge[2].astype(F32))
    if keep is not None:
        mapped = [a * keep for a in mapped]
    if r.stage > 1:
        mapped = [a + r.back * (tile_of(olds[0], i) - old[i]) for i, a in enumerate(mapped)]
    return [a - r.steps[-1] * b for a, b in zip(old, mapped)], mapped


def unpacked_sides(r, start, size):
    half = r.side_z.shape[0]
    low = lane_mask()
    out = []
    while size:
        upper = start < half
        count = min(size, half - start) if upper else size
        left, right = from_columns(r, start if upper else start - half, count)
        if upper:
            left = pltpu.roll(left, HALF, 1)
        else:
            right = pltpu.roll(right, HALF, 1)
        out.append(jnp.where(low, right, left))
        start, size = start + count, size - count
    return out[0] if len(out) == 1 else jnp.concatenate(out, 0)


def initial(r, start, size):
    here = pl.ds(start, size)
    block = r.observed[here, :]
    return [tile_of(block, 0), tile_of(block, 1), unpacked_sides(r, start, size)]


def pack_kernel(r):
    half = r.to_a.shape[0]
    low = lane_mask()
    first = [r.observed[pl.ds(start, half), pl.ds(0, THIRD)] for start in (0, half)]
    second = [r.observed[pl.ds(start, half), pl.ds(THIRD, THIRD)] for start in (0, half)]
    send_columns(
        r,
        pl.ds(0, half),
        jnp.where(low, first[0], pltpu.roll(first[1], HALF, 1)),
        jnp.where(low, pltpu.roll(second[0], HALF, 1), second[1]),
    )


def halo_kernel(r):
    send_rows(r, initial(r, 0, HALO), initial(r, r.observed.shape[0] - HALO, HALO))


def row_strip_kernel(r):
    low = lane_mask()
    blocks = 2 * r.tiles + 1
    size = r.to_a.shape[0]
    strips = []
    for side, ref in ((0, r.top_sum), (1, r.low_sum)):
        own = ref[pl.ds(side * (WIN - size), size), :]
        if r.narrow:
            west, east = from_columns(r, side * (blocks * HALO - size), size)
            if side:
                west = pltpu.roll(west, HALF, 1)
            else:
                east = pltpu.roll(east, HALF, 1)
            add = [jnp.where(low, west, 0.0), jnp.where(low, 0.0, east)]
        else:
            west, east = from_columns(r, side * (blocks * THIRD - size), size)
            add = [
                jnp.where(low, west, 0.0),
                jnp.where(low, 0.0, east),
                jnp.where(low, east, west),
            ]
        strips.append([tile_of(own, i) + a for i, a in enumerate(add)])
    send_rows(r, *strips)


def middle_kernel(r):
    square = cross = jnp.zeros((8, THIRD), F32)
    blocks = 2 * r.tiles + 1
    if r.stage > 0:
        scalars(r)
    for num in range(1, blocks - 1):
        here = rows_at(num - 1)
        if r.stage == 0:
            fresh = initial(r, num * THIRD - HALO, THIRD)
        else:
            fresh, mapped = update(r, num, "mid", here, THIRD, 0, None, None)
            cross += sum(fold8(a * b) for a, b in zip(fresh[:2], mapped))
        put(r.res_mid_new, here, fresh)
        square += sum(fold8(a * a) for a in fresh[:2])
    r.acc[0] = square
    r.acc[1] = cross
    r.acc[2] = jnp.zeros((8, THIRD), F32)
    inner = list(range(1, r.tiles - 1))
    some = r.occ[inner[0]]
    for slot in inner[1:]:
        some = some + r.occ[slot]

    @pl.when(some != 0)
    def _():
        windows = [
            [r.res_mid_new[rows_at(2 * slot + i - 1), :] for i in range(3)] for slot in inner
        ]
        results = window_products(windows, inner, r)
        curve = jnp.zeros((8, THIRD), F32)
        for num, (window, result) in enumerate(zip(windows, results)):
            curve += sum(fold8(a * b) for a, b in zip(window, result))
            first = result[0] if num == 0 else result[0] + results[num - 1][2]
            r.mid_sum_new[rows_at(2 * num), :] = first
            r.mid_sum_new[rows_at(2 * num + 1), :] = result[1]
        r.mid_sum_new[rows_at(2 * len(inner)), :] = results[-1][2]
        r.acc[2] = curve

    @pl.when(some == 0)
    def _():
        r.mid_sum_new[...] = jnp.zeros(r.mid_sum_new.shape, F32)

    if r.parted:
        for num in range(r.to_mid.shape[0] // THIRD):
            strips = strips_of([(r.mid_sum_new, num + 1)])
            r.to_mid[rows_at(num), :] = pick(r.edge[4] != 0, *strips)[1]


def edge_kernel(r):
    square, cross = r.acc[0], r.acc[1]
    blocks = 2 * r.tiles + 1
    rows = 2 * r.tiles * THIRD
    if r.stage > 0:
        energy, power = scalars(r)
        fill = [jnp.zeros_like(energy)] * (ITERS - len(r.steps))
        r.coef_new[...] = lanes_of((8, THIRD), energy, power, *r.steps, *fill, *r.ratios)
    for side in range(2):
        num = side * (blocks - 1)
        for offset in (0, HALO):
            here = pl.ds(side * THIRD + offset, HALO)
            inside = (offset > 0) == (side == 0)
            if r.stage == 0:
                if inside:
                    fresh = initial(r, side * (rows - HALO), HALO)
                else:
                    halo = from_rows(r, side, pl.ds(0, HALO))
                    fresh = [tile_of(halo, i) for i in range(3)]
            else:
                spill = from_rows(r, side, pl.ds(offset, HALO))
                keep = None if inside else r.edge[side].astype(F32)
                fresh, mapped = update(r, num, "edge", here, HALO, offset, spill, keep)
                if inside:
                    cross += sum(fold8(a * b) for a, b in zip(fresh[:2], mapped))
            put(r.res_edge_new, here, fresh)
            if inside:
                square += sum(fold8(a * a) for a in fresh[:2])
    slots = [0, r.tiles - 1]
    some = r.occ[slots[0]] + r.occ[slots[1]]

    @pl.when(some != 0)
    def _():
        far = blocks - 4
        windows = [
            [r.res_edge_new[rows_at(0), :]] + [r.res_mid_new[rows_at(i), :] for i in range(2)],
            [r.res_mid_new[rows_at(far + i), :] for i in range(2)] + [r.res_edge_new[rows_at(1), :]],
        ]
        results = window_products(windows, slots, r)
        curve = jnp.zeros((8, THIRD), F32)
        for window, result, ref in zip(windows, results, (r.top_sum_new, r.low_sum_new)):
            curve += sum(fold8(a * b) for a, b in zip(window, result))
            for num in range(3):
                ref[rows_at(num), :] = result[num]
        r.curve[...] = curve

    @pl.when(some == 0)
    def _():
        r.top_sum_new[...] = jnp.zeros((WIN, WIN), F32)
        r.low_sum_new[...] = jnp.zeros((WIN, WIN), F32)
        r.curve[...] = jnp.zeros((8, THIRD), F32)

    low = lane_mask()
    new = Refs(tiles=r.tiles, top_sum=r.top_sum_new, mid_sum=r.mid_sum_new, low_sum=r.low_sum_new)
    if r.narrow:
        half = blocks * HALO
        for start in range(0, half, HALO):
            pair = []
            for row in (start, start + half):
                terms = [
                    ref[pl.ds(block * THIRD + row % THIRD, HALO), pl.ds(2 * THIRD, THIRD)]
                    for ref, block in own_sum(new, row // THIRD)
                ]
                pair.append(sum(terms[1:], terms[0]))
            here = pl.ds(start, HALO)
            send_columns(
                r,
                here,
                jnp.where(low, pltpu.roll(pair[0], HALF, 1), pair[1]),
                jnp.where(low, pair[0], pltpu.roll(pair[1], HALF, 1)),
            )
    else:
        middle = blocks - 6
        for num in range(blocks):
            to_a, to_b = pick(r.edge[4] != 0, *strips_of(own_sum(new, num)))
            r.to_a[rows_at(num), :] = to_a
            if not r.parted:
                r.to_b[rows_at(num), :] = to_b
            elif num < 3 or num >= 3 + middle:
                r.to_end[rows_at(num if num < 3 else num - middle), :] = to_b
    gamma = total(square)
    curve = gamma + total(r.acc[2] + r.curve[...])
    r.part[...] = lanes_of(r.part.shape, gamma, curve, total(cross))


def last_rows(r, start, corrected, residual, at):
    blocks = 2 * r.tiles + 1
    half = blocks * HALO
    low = lane_mask()
    num, offset = start // THIRD, start % THIRD
    upper = start < half
    west, east = from_columns(r, start if upper else start - half, HALO)
    if upper:
        east = pltpu.roll(east, HALF, 1)
    else:
        west = pltpu.roll(west, HALF, 1)
    add = [jnp.where(low, west, 0.0), jnp.where(low, 0.0, east)]
    for ref, block in own_sum(r, num):
        there = pl.ds(block * THIRD + offset, HALO)
        add = [a + ref[there, pl.ds(i * THIRD, THIRD)] for i, a in enumerate(add)]
    if num == 0 or num == blocks - 1:
        spill = from_rows(r, 0 if num == 0 else 1, pl.ds(0, HALO))
        add = [a + tile_of(spill, i) for i, a in enumerate(add)]
        olds, here = old_of(r, "edge"), pl.ds((0 if num == 0 else THIRD) + offset, HALO)
    else:
        olds, here = old_of(r, "mid"), pl.ds(start - THIRD, HALO)
    for i, a in enumerate(add):
        lanes = pl.ds(i * THIRD, THIRD)
        past = [ref[here, lanes] for ref in olds]
        direct = past[0]
        moved = r.steps[0] * direct
        for old, ratio, step in zip(past[1:], r.ratios, r.steps[1:]):
            direct = old + ratio * direct
            moved = moved + step * direct
        mapped = a + past[-1] + r.back * (past[-2] - past[-1])
        corrected[pl.ds(at, HALO), lanes] = moved
        residual[pl.ds(at, HALO), lanes] = past[-1] - r.steps[-1] * mapped


def last_middle_kernel(r):
    scalars(r)
    for start in range(THIRD, 2 * r.tiles * THIRD, HALO):
        last_rows(r, start, r.corrected, r.residual, start - HALO)


def last_edge_kernel(r):
    scalars(r)
    rows = 2 * r.tiles * THIRD
    copies = []
    for side in range(2):
        last_rows(r, HALO + side * (rows - HALO), r.corrected_rows, r.residual_rows, side * HALO)
        here = pl.ds(side * HALO, HALO)
        there = pl.ds(side * (rows - HALO), HALO)
        for num, (source, target) in enumerate(
            ((r.corrected_rows, r.corrected), (r.residual_rows, r.residual))
        ):
            copy = pltpu.make_async_copy(source.at[here, :], target.at[there, :], r.sems.at[side, num])
            copy.start()
            copies.append(copy)
    for copy in copies:
        copy.wait()


class Refs:
    def __init__(self, **names):
        self.__dict__.update(names)


SCALARS = ("occ", "kid", "edge")
PARAMS = pltpu.CompilerParams(vmem_limit_bytes=16 * 1024 * 1024)


def run(body, ins, outs, scratch=None, onto=None, **static):
    scratch, onto = scratch or {}, onto or {}
    names = [*ins, *("old_" + name for name in onto), *outs, *onto, *scratch]

    def kernel(*refs):
        body(Refs(**static, **dict(zip(names, refs))))

    whole = pl.BlockSpec(memory_space=pltpu.VMEM)
    placed = [pl.BlockSpec(memory_space=pl.ANY)] * len(onto)
    shapes = [*outs.values(), *(value.shape for value in onto.values())]
    result = pl.pallas_call(
        kernel,
        name=body.__name__,
        out_shape=[jax.ShapeDtypeStruct(dims, F32) for dims in shapes],
        in_specs=[
            pl.BlockSpec(memory_space=pltpu.SMEM) if name in SCALARS else whole for name in ins
        ]
        + placed,
        out_specs=[whole] * len(outs) + placed,
        scratch_shapes=[
            pltpu.VMEM(dims, F32) if isinstance(dims, tuple) else dims for dims in scratch.values()
        ],
        input_output_aliases={len(ins) + i: len(outs) + i for i in range(len(onto))},
        compiler_params=PARAMS,
    )(*ins.values(), *onto.values())
    return dict(zip([*outs, *onto], result))


def own_part(table, tile_count):
    column = lax.dynamic_index_in_dim(table, lax.axis_index("col"), 1, keepdims=False)
    return lax.dynamic_slice_in_dim(column, lax.axis_index("row") * tile_count, tile_count)


def swap(value, axis, first):
    pairs = [(i, i + 1) for i in range(first, lax.axis_size(axis) - 1, 2)]
    return lax.ppermute(value, axis, pairs + [(b, a) for a, b in pairs])


def shards(observed, kernels, occupied, kernel_index):
    rows, cols = observed.shape
    tiles = rows // TILE
    half, mid, ext = rows // 2, rows - 2 * HALO, rows + 2 * HALO
    n_row, n_col = lax.axis_size("row"), lax.axis_size("col")
    devices = n_row * n_col
    my_row, my_col = lax.axis_index("row"), lax.axis_index("col")
    occ = own_part(occupied, tiles)
    edge = jnp.stack(
        [my_row > 0, my_row < n_row - 1, my_col > 0, my_col < n_col - 1, my_col % 2 == 1, my_row % 2 == 1]
    ).astype(jnp.int32)
    host = {name: jnp.asarray(table) for name, table in tables().items()}
    sent = run(pack_kernel, dict(edge=edge, observed=observed), dict(to_a=(half, THIRD), to_b=(half, THIRD)))
    side_b = swap(sent["to_b"], "col", 1)
    side_z = swap(sent["to_a"], "col", 0)
    spec = run(
        spectra_kernel,
        dict(
            kid=own_part(kernel_index, tiles),
            occ=occ,
            kernels=jnp.pad(kernels, ((0, 0), (0, THIRD - KW), (0, THIRD - KW))),
            w_left=host["w_left"],
            w_right=host["w_right"],
        ),
        dict(spec=(tiles, 2, SLOTS, SLOTS)),
    )["spec"]
    side_b, side_z, spec = lax.optimization_barrier((side_b, side_z, spec))
    sides = dict(edge=edge, side_b=side_b, side_z=side_z)
    sent = run(halo_kernel, dict(observed=observed, **sides), dict(to_a=(HALO, WIN), to_b=(HALO, WIN)))
    sides, sent = lax.optimization_barrier((sides, sent))
    row_b, row_a = swap(sent["to_b"], "row", 1), swap(sent["to_a"], "row", 0)
    fixed = dict(occ=occ, spec=spec, **{name: host[name] for name in NAMES})
    state = {}
    for stage in range(ITERS):
        narrow = stage == ITERS - 1
        parted = 0 < stage < ITERS - 1
        moving = dict(sides)
        if stage == 0:
            moving["observed"] = observed
        else:
            moving["parts"] = parts
        if stage > 1:
            moving["coef"] = state["coef_new"]

        def old(where, *sums):
            names = ["res%d_%s" % (i, where) for i in range(stage)]
            return {name: state[name] for name in names + list(sums) if stage}

        middle = run(
            middle_kernel,
            {**fixed, **moving, **old("mid", "top_sum", "mid_sum", "low_sum")},
            {
                "res_mid_new": (mid, WIN),
                "mid_sum_new": (mid - TILE, WIN),
                "acc": (3, 8, THIRD),
                **({"to_mid": (ext - 2 * WIN, THIRD)} if parted else {}),
            },
            stage=stage,
            tiles=tiles,
            parted=parted,
        )
        if parted:
            side_mid = swap(middle["to_mid"], "col", 1)
        outs = {"res_edge_new": (TILE, WIN), "top_sum_new": (WIN, WIN), "low_sum_new": (WIN, WIN)}
        outs["to_a"] = (ext // 2 if narrow else ext, THIRD)
        outs["to_end" if parted else "to_b"] = (2 * WIN if parted else outs["to_a"][0], THIRD)
        outs["part"] = (devices, THIRD)
        if stage:
            outs["coef_new"] = (8, THIRD)
        edges = run(
            edge_kernel,
            {
                **fixed,
                **moving,
                **old("edge", "top_sum", "low_sum"),
                "row_b": row_b,
                "row_a": row_a,
                **{name: middle[name] for name in ("res_mid_new", "mid_sum_new", "acc")},
            },
            outs,
            dict(curve=(8, THIRD)),
            stage=stage,
            tiles=tiles,
            parted=parted,
            narrow=narrow,
        )
        state["res%d_mid" % stage] = middle["res_mid_new"]
        state["res%d_edge" % stage] = edges["res_edge_new"]
        state["mid_sum"] = middle["mid_sum_new"]
        state["top_sum"] = edges["top_sum_new"]
        state["low_sum"] = edges["low_sum_new"]
        state["coef_new"] = edges.get("coef_new")
        part, to_a = edges["part"], edges["to_a"]
        sides = {}
        if parted:
            sides["side_mid"], part, to_a, to_end = lax.optimization_barrier(
                (side_mid, part, to_a, edges["to_end"])
            )
        sides["side_z"] = swap(to_a, "col", 0)
        if parted:
            sides["side_end"] = swap(to_end, "col", 1)
        else:
            sides["side_b"] = swap(edges["to_b"], "col", 1)
        parts = lax.all_to_all(part, ("row", "col"), 0, 0, tiled=True)
        sides, parts = lax.optimization_barrier((sides, parts))
        sides["edge"] = edge
        strip = (HALO, TILE) if narrow else (THIRD, WIN)
        sent = run(
            row_strip_kernel,
            dict(top_sum=state["top_sum"], low_sum=state["low_sum"], **sides),
            dict(to_a=strip, to_b=strip),
            tiles=tiles,
            narrow=narrow,
        )
        row_b, row_a = swap(sent["to_b"], "row", 1), swap(sent["to_a"], "row", 0)

    def olds(where):
        return {name: state[name] for name in ["res%d_%s" % (i, where) for i in range(ITERS)]}

    ends = {name: state[name] for name in ("coef_new", "top_sum", "low_sum")}
    ends["coef"] = ends.pop("coef_new")
    out = run(
        last_middle_kernel,
        dict(parts=parts, mid_sum=state["mid_sum"], **ends, **sides, **olds("mid")),
        dict(corrected=(rows, cols), residual=(rows, cols)),
        stage=ITERS,
        tiles=tiles,
    )
    out = run(
        last_edge_kernel,
        dict(parts=parts, row_b=row_b, row_a=row_a, **ends, **sides, **olds("edge")),
        {},
        dict(
            corrected_rows=(2 * HALO, cols),
            residual_rows=(2 * HALO, cols),
            sems=pltpu.SemaphoreType.DMA((2, 2)),
        ),
        out,
        stage=ITERS,
        tiles=tiles,
    )
    return out["corrected"], out["residual"]


def solution(mesh):
    placed = (P("row", "col"), P(), P(), P())
    return jax.shard_map(
        shards,
        mesh=mesh,
        in_specs=placed,
        out_specs=(P("row", "col"), P("row", "col")),
        check_vma=False,
    )
```

```python
import functools
import math

import jax
import jax.numpy as jnp
import numpy as np
from jax import lax
from jax.experimental import pallas as pl
from jax.experimental.pallas import tpu as pltpu
from jax.sharding import PartitionSpec as P

TILE = 256
HALO = 64
KW = 65
ITERS = 3
WIN = TILE + 2 * HALO
THIRD = WIN // 3
HALF = THIRD // 2
SLOTS = 2 * THIRD
BF = jnp.bfloat16
F32 = jnp.float32


def hi_lo(table):
    high = table.astype(np.float32).astype(jnp.bfloat16)
    low = (table - high.astype(np.float64)).astype(np.float32).astype(jnp.bfloat16)
    return high, low


@functools.cache
def tables():
    spots = np.arange(THIRD)
    low_freq = 3 * np.arange(HALF)
    full = math.sqrt(2.0 / WIN)
    cos_part = np.cos(2 * np.pi * (low_freq[:, None] * spots % WIN) / WIN) * full
    sin_part = np.sin(2 * np.pi * (low_freq[:, None] * spots % WIN) / WIN) * full
    cos_part[0] = math.sqrt(1.0 / WIN)
    sin_part[0] = np.where(spots % 2 == 0, 1.0, -1.0) * math.sqrt(1.0 / WIN)
    small = np.concatenate([cos_part, sin_part])
    angle = 2 * np.pi * ((3 * spots[:, None] + 1) * spots % WIN) / WIN
    root = math.sqrt(3.0) / 2
    large = full * np.block(
        [[np.cos(angle), -root * np.sin(angle)], [np.sin(angle), root * np.cos(angle)]]
    )
    freqs = np.concatenate([low_freq, low_freq, 3 * spots + 1])
    freqs[HALF] = WIN // 2
    taps = np.arange(THIRD)
    turn = 2 * np.pi * (freqs[:, None] * taps % WIN) / WIN
    keep = (taps < KW)[None, :]
    sines = np.sin(turn)
    sines[0] = 0.0
    sines[HALF] = 0.0
    waves = np.concatenate([np.cos(turn) * keep, sines * keep])

    sh, sl = hi_lo(small)
    gh, gl = hi_lo(large)
    wh, wl = hi_lo(waves)
    return dict(
        large=np.concatenate([gh, gl]),
        large_t=np.concatenate([gh.T, gl.T]),
        small=np.concatenate([sh, sl]),
        small_t=np.concatenate([sh.T, sl.T]),
        w_left=np.concatenate([wh, wl, wh], 1),
        w_right=np.concatenate([wh.T, wl.T, wh.T], 0),
    )


NAMES = ("large", "large_t", "small", "small_t")


def split(value):
    high = value.astype(BF)
    return high, (value - high.astype(F32)).astype(BF)


def dot(left, right):
    return jnp.dot(left, right, preferred_element_type=F32)


def right_large(value, table):
    high, low = split(value)
    return dot(
        jnp.concatenate([high, high, low], 1),
        jnp.concatenate([table[...], table[:SLOTS]], 0),
    )


def right_small(value, table):
    high, low = split(value)
    coarse, fine = table[:THIRD], table[THIRD:]
    both = dot(
        jnp.concatenate([high, low], 1),
        jnp.concatenate(
            [
                jnp.concatenate([coarse, fine], 1),
                jnp.concatenate([coarse, jnp.zeros_like(fine)], 1),
            ],
            0,
        ),
    )
    return both[:, :THIRD] + both[:, THIRD:]


def left_large(value, table):
    high, low = split(value)
    both = dot(table[...], high)
    return both[:SLOTS] + both[SLOTS:] + dot(table[:SLOTS], low)


def left_small(value, table):
    high, low = split(value)
    coarse, fine = table[:THIRD], table[THIRD:]
    both = dot(
        jnp.concatenate(
            [
                jnp.concatenate([coarse, coarse], 1),
                jnp.concatenate([fine, jnp.zeros_like(fine)], 1),
            ],
            0,
        ),
        jnp.concatenate([high, low], 0),
    )
    return both[:THIRD] + both[THIRD:]


def butterfly(first, second, third):
    total = second + third
    return first + total, first - 0.5 * total, second - third


def unbutterfly(plain, real, diff):
    base = plain - 0.5 * real
    return plain + real, base + diff, base - diff


def spectra_kernel(r):
    def body(slot, carry):
        @pl.when(r.occ[slot] != 0)
        def _():
            high, low = split(r.kernels[r.kid[slot]])
            half = dot(r.w_left[...], jnp.concatenate([high, high, low], 0))
            high, low = split(half)
            quads = dot(jnp.concatenate([high, high, low], 1), r.w_right[...])
            cc = quads[:SLOTS, :SLOTS]
            cs = quads[:SLOTS, SLOTS:]
            sc = quads[SLOTS:, :SLOTS]
            ss = quads[SLOTS:, SLOTS:]
            r.spec[slot, 0] = cc * cc + ss * ss + (sc * sc + cs * cs)
            r.spec[slot, 1] = 2.0 * (sc * cs - cc * ss)

        @pl.when(r.occ[slot] == 0)
        def _():
            r.spec[slot] = jnp.zeros((2, SLOTS, SLOTS), F32)

        return carry

    lax.fori_loop(0, r.spec.shape[0], body, 0)


def tile_of(block, num):
    return block[:, num * THIRD : (num + 1) * THIRD]


def lane_mask():
    return lax.broadcasted_iota(jnp.int32, (1, THIRD), 1) < HALF


def apply_spectrum(low_rows, high_rows, spec_ref, slot, mixed):
    lanes = pl.ds(0 if mixed else THIRD, THIRD)
    sign = jnp.where(lane_mask(), -1.0, 1.0).astype(F32)

    def band(cos_rows, sin_rows, cos_at, sin_at, size):
        pc = spec_ref[slot, 0, pl.ds(cos_at, size), lanes]
        ps = spec_ref[slot, 0, pl.ds(sin_at, size), lanes] if sin_at != cos_at else pc
        cross = spec_ref[slot, 1, pl.ds(cos_at, size), lanes]
        if mixed:
            cross = cross * sign
            return (
                pc * cos_rows + cross * pltpu.roll(sin_rows, HALF, 1),
                ps * sin_rows - cross * pltpu.roll(cos_rows, HALF, 1),
            )
        c1, c2, s1, s2 = cos_rows[:, :THIRD], cos_rows[:, THIRD:], sin_rows[:, :THIRD], sin_rows[:, THIRD:]
        return (
            jnp.concatenate([pc * c1 - cross * s2, pc * c2 + cross * s1], 1),
            jnp.concatenate([ps * s1 + cross * c2, ps * s2 - cross * c1], 1),
        )

    low = band(low_rows[:HALF], low_rows[HALF:], 0, HALF, HALF)
    high = band(high_rows[:THIRD], high_rows[THIRD:], THIRD, THIRD, THIRD)
    return jnp.concatenate(low, 0), jnp.concatenate(high, 0)


def window_products(windows, slots, r):
    count = len(windows)
    folded = [
        [butterfly(*(tile_of(block, i) for i in range(3))) for block in blocks] for blocks in windows
    ]
    small = [[right_small(plain, r.small_t) for plain, _, _ in blocks] for blocks in folded]
    large = [
        [right_large(jnp.concatenate([real, diff], 1), r.large_t) for _, real, diff in blocks]
        for blocks in folded
    ]

    def to_rows(windows):
        parts = [butterfly(*blocks) for blocks in windows]
        plain, real, diff = (jnp.concatenate([part[i] for part in parts], 1) for i in range(3))
        return left_small(plain, r.small), left_large(jnp.concatenate([real, diff], 0), r.large)

    def from_rows_of(bands, mixed):
        width = THIRD if mixed else 2 * THIRD
        done = []
        for num, slot in enumerate(slots):
            here = slice(num * width, (num + 1) * width)
            done.append(apply_spectrum(bands[0][:, here], bands[1][:, here], r.spec, slot, mixed))
        low_rows, high_rows = (jnp.concatenate([band[i] for band in done], 1) for i in range(2))
        plain = left_small(low_rows, r.small_t)
        both = left_large(high_rows, r.large_t)
        return unbutterfly(plain, both[:THIRD], both[THIRD:])

    small_bands, large_bands = to_rows(small), to_rows(large)
    small = from_rows_of(small_bands, True)
    large = from_rows_of(large_bands, False)
    plain = [[right_small(tile_of(block, num), r.small) for block in small] for num in range(count)]
    results = []
    for num in range(count):
        here = slice(2 * num * THIRD, 2 * (num + 1) * THIRD)
        both = [right_large(block[:, here], r.large) for block in large]
        results.append(
            [
                jnp.concatenate(unbutterfly(a, b[:, :THIRD], b[:, THIRD:]), 1)
                for a, b in zip(plain[num], both)
            ]
        )
    return results


def fold8(value):
    rows = value.reshape(value.shape[0] // 8, 8, value.shape[1]).sum(0)
    return sum(tile_of(rows, i) for i in range(value.shape[1] // THIRD))


def total(value):
    return jnp.sum(jnp.sum(value, 0, keepdims=True), 1, keepdims=True)


def lanes_of(shape, *values):
    lanes = lax.broadcasted_iota(jnp.int32, shape, 1)
    out = jnp.zeros(shape, F32)
    for num, value in enumerate(values):
        out = jnp.where(lanes == num, value, out)
    return out


def rows_at(num, count=1):
    return pl.ds(num * THIRD, count * THIRD)


def put(ref, here, tiles):
    for num, tile in enumerate(tiles):
        ref[here, pl.ds(num * THIRD, THIRD)] = tile


def own_sum(r, num):
    last = 2 * r.tiles
    terms = []
    if num <= 2:
        terms.append((r.top_sum, num))
    if 2 <= num <= last - 2:
        terms.append((r.mid_sum, num - 2))
    if num >= last - 2:
        terms.append((r.low_sum, num - last + 2))
    return terms


ENERGY, POWER, STEP, RATIO, BACK = 0, 1, 2, 2 + ITERS, 2 + 2 * ITERS
COEFS = (3 + 2 * ITERS, 8, THIRD)


def put_scalars(r):
    sums = jnp.sum(r.parts[...], 0, keepdims=True)
    energy, curve, cross = sums[:, 0:1], sums[:, 1:2], sums[:, 2:3]
    values = {ENERGY: energy, POWER: curve}
    last = r.stage - 1
    if last:
        ratio = energy / r.coef[ENERGY, 0:1, 0:1]
        values[POWER] = curve + ratio * (2.0 * cross + ratio * r.coef[POWER, 0:1, 0:1])
        values[RATIO + last] = ratio
        values[BACK] = ratio / r.coef[STEP + last - 1, 0:1, 0:1]
        for num in range(last):
            r.coef_new[STEP + num] = r.coef[STEP + num]
            r.coef_new[RATIO + num] = r.coef[RATIO + num]
    values[STEP + last] = energy / values[POWER]
    for num, value in values.items():
        r.coef_new[num] = jnp.broadcast_to(value, (8, THIRD))


def take_scalars(r, coef):
    r.steps = [coef[STEP + i, 0:1, :] for i in range(r.stage)]
    r.ratios = [coef[RATIO + i, 0:1, :] for i in range(1, r.stage)]
    r.back = coef[BACK, 0:1, :] if r.stage > 1 else None


def pick(odd, first, second):
    return jnp.where(odd, first, second), jnp.where(odd, second, first)


def from_columns(r, start, size):
    second = getattr(r, "side_b", None)
    there = start
    if second is None:
        middle = r.side_mid.shape[0]
        if start < WIN:
            second = r.side_end
        elif start < WIN + middle:
            second, there = r.side_mid, start - WIN
        else:
            second, there = r.side_end, start - middle
    return pick(r.edge[4] != 0, r.side_z[pl.ds(start, size), :], second[pl.ds(there, size), :])


def from_rows(r, side, here):
    return pick(r.edge[5] != 0, r.row_a[here, :], r.row_b[here, :])[side]


def send_columns(r, here, to_left, to_right):
    r.to_a[here, :], r.to_b[here, :] = pick(r.edge[4] != 0, to_left, to_right)


def strips_of(terms):
    low = lane_mask()
    pieces = [ref[rows_at(block), :] for ref, block in terms]
    block = sum(pieces[1:], pieces[0])
    return (
        jnp.where(low, tile_of(block, 0), tile_of(block, 2)),
        jnp.where(low, tile_of(block, 2), tile_of(block, 1)),
    )


def send_rows(r, above, below):
    odd = r.edge[5] != 0
    here = pl.ds(0, r.to_a.shape[0])
    pairs = [pick(odd, a, b) for a, b in zip(above, below)]
    put(r.to_a, here, [a for a, _ in pairs])
    put(r.to_b, here, [b for _, b in pairs])


def old_of(r, name):
    return [getattr(r, "res%d_%s" % (i, name)) for i in range(r.stage)]


def update(r, num, name, here, size, offset, spill, keep):
    low = lane_mask()
    sums = [ref[pl.ds(block * THIRD + offset, size), :] for ref, block in own_sum(r, num)]
    west, east = from_columns(r, num * THIRD + offset, size)
    add = [
        jnp.where(low, west, 0.0),
        jnp.where(low, 0.0, east),
        jnp.where(low, east, west),
    ]
    for block in sums + ([] if spill is None else [spill]):
        add = [a + tile_of(block, i) for i, a in enumerate(add)]
    olds = [ref[here, :] for ref in old_of(r, name)[-2:]]
    old = [tile_of(olds[-1], i) for i in range(3)]
    mapped = [a + b for a, b in zip(add, old)]
    mapped[2] = mapped[2] * jnp.where(low, r.edge[3].astype(F32), r.edge[2].astype(F32))
    if keep is not None:
        mapped = [a * keep for a in mapped]
    if r.stage > 1:
        mapped = [a + r.back * (tile_of(olds[0], i) - old[i]) for i, a in enumerate(mapped)]
    return [a - r.steps[-1] * b for a, b in zip(old, mapped)], mapped


def unpacked_sides(r, start, size):
    half = r.side_z.shape[0]
    low = lane_mask()
    out = []
    while size:
        upper = start < half
        count = min(size, half - start) if upper else size
        left, right = from_columns(r, start if upper else start - half, count)
        if upper:
            left = pltpu.roll(left, HALF, 1)
        else:
            right = pltpu.roll(right, HALF, 1)
        out.append(jnp.where(low, right, left))
        start, size = start + count, size - count
    return out[0] if len(out) == 1 else jnp.concatenate(out, 0)


def initial(r, start, size):
    here = pl.ds(start, size)
    block = r.observed[here, :]
    return [tile_of(block, 0), tile_of(block, 1), unpacked_sides(r, start, size)]


def pack_kernel(r):
    half = r.to_a.shape[0]
    low = lane_mask()
    first = [r.observed[pl.ds(start, half), pl.ds(0, THIRD)] for start in (0, half)]
    second = [r.observed[pl.ds(start, half), pl.ds(THIRD, THIRD)] for start in (0, half)]
    send_columns(
        r,
        pl.ds(0, half),
        jnp.where(low, first[0], pltpu.roll(first[1], HALF, 1)),
        jnp.where(low, pltpu.roll(second[0], HALF, 1), second[1]),
    )


def halo_kernel(r):
    send_rows(r, initial(r, 0, HALO), initial(r, r.observed.shape[0] - HALO, HALO))


def row_strip_kernel(r):
    low = lane_mask()
    blocks = 2 * r.tiles + 1
    size = r.to_a.shape[0]
    strips = []
    for side, ref in ((0, r.top_sum), (1, r.low_sum)):
        own = ref[pl.ds(side * (WIN - size), size), :]
        if r.narrow:
            west, east = from_columns(r, side * (blocks * HALO - size), size)
            if side:
                west = pltpu.roll(west, HALF, 1)
            else:
                east = pltpu.roll(east, HALF, 1)
            add = [jnp.where(low, west, 0.0), jnp.where(low, 0.0, east)]
        else:
            west, east = from_columns(r, side * (blocks * THIRD - size), size)
            add = [
                jnp.where(low, west, 0.0),
                jnp.where(low, 0.0, east),
                jnp.where(low, east, west),
            ]
        strips.append([tile_of(own, i) + a for i, a in enumerate(add)])
    send_rows(r, *strips)
    if r.narrow:
        put_scalars(r)


def middle_kernel(r):
    square = cross = jnp.zeros((8, THIRD), F32)
    blocks = 2 * r.tiles + 1
    if r.stage > 0:
        put_scalars(r)
        take_scalars(r, r.coef_new)
    for num in range(1, blocks - 1):
        here = rows_at(num - 1)
        if r.stage == 0:
            fresh = initial(r, num * THIRD - HALO, THIRD)
        else:
            fresh, mapped = update(r, num, "mid", here, THIRD, 0, None, None)
            cross += sum(fold8(a * b) for a, b in zip(fresh[:2], mapped))
        put(r.res_mid_new, here, fresh)
        square += sum(fold8(a * a) for a in fresh[:2])
    r.acc[0] = square
    r.acc[1] = cross
    r.acc[2] = jnp.zeros((8, THIRD), F32)
    inner = list(range(1, r.tiles - 1))
    some = r.occ[inner[0]]
    for slot in inner[1:]:
        some = some + r.occ[slot]

    @pl.when(some != 0)
    def _():
        windows = [
            [r.res_mid_new[rows_at(2 * slot + i - 1), :] for i in range(3)] for slot in inner
        ]
        results = window_products(windows, inner, r)
        curve = jnp.zeros((8, THIRD), F32)
        for num, (window, result) in enumerate(zip(windows, results)):
            curve += sum(fold8(a * b) for a, b in zip(window, result))
            first = result[0] if num == 0 else result[0] + results[num - 1][2]
            r.mid_sum_new[rows_at(2 * num), :] = first
            r.mid_sum_new[rows_at(2 * num + 1), :] = result[1]
        r.mid_sum_new[rows_at(2 * len(inner)), :] = results[-1][2]
        r.acc[2] = curve

    @pl.when(some == 0)
    def _():
        r.mid_sum_new[...] = jnp.zeros(r.mid_sum_new.shape, F32)

    if r.parted:
        for num in range(r.to_mid.shape[0] // THIRD):
            strips = strips_of([(r.mid_sum_new, num + 1)])
            r.to_mid[rows_at(num), :] = pick(r.edge[4] != 0, *strips)[1]


def edge_kernel(r):
    square, cross = r.acc[0], r.acc[1]
    blocks = 2 * r.tiles + 1
    rows = 2 * r.tiles * THIRD
    if r.stage > 0:
        take_scalars(r, r.coef)
    for side in range(2):
        num = side * (blocks - 1)
        for offset in (0, HALO):
            here = pl.ds(side * THIRD + offset, HALO)
            inside = (offset > 0) == (side == 0)
            if r.stage == 0:
                if inside:
                    fresh = initial(r, side * (rows - HALO), HALO)
                else:
                    halo = from_rows(r, side, pl.ds(0, HALO))
                    fresh = [tile_of(halo, i) for i in range(3)]
            else:
                spill = from_rows(r, side, pl.ds(offset, HALO))
                keep = None if inside else r.edge[side].astype(F32)
                fresh, mapped = update(r, num, "edge", here, HALO, offset, spill, keep)
                if inside:
                    cross += sum(fold8(a * b) for a, b in zip(fresh[:2], mapped))
            put(r.res_edge_new, here, fresh)
            if inside:
                square += sum(fold8(a * a) for a in fresh[:2])
    slots = [0, r.tiles - 1]
    some = r.occ[slots[0]] + r.occ[slots[1]]

    @pl.when(some != 0)
    def _():
        far = blocks - 4
        windows = [
            [r.res_edge_new[rows_at(0), :]] + [r.res_mid_new[rows_at(i), :] for i in range(2)],
            [r.res_mid_new[rows_at(far + i), :] for i in range(2)] + [r.res_edge_new[rows_at(1), :]],
        ]
        results = window_products(windows, slots, r)
        curve = jnp.zeros((8, THIRD), F32)
        for window, result, ref in zip(windows, results, (r.top_sum_new, r.low_sum_new)):
            curve += sum(fold8(a * b) for a, b in zip(window, result))
            for num in range(3):
                ref[rows_at(num), :] = result[num]
        r.curve[...] = curve

    @pl.when(some == 0)
    def _():
        r.top_sum_new[...] = jnp.zeros((WIN, WIN), F32)
        r.low_sum_new[...] = jnp.zeros((WIN, WIN), F32)
        r.curve[...] = jnp.zeros((8, THIRD), F32)

    low = lane_mask()
    new = Refs(tiles=r.tiles, top_sum=r.top_sum_new, mid_sum=r.mid_sum_new, low_sum=r.low_sum_new)
    if r.narrow:
        half = blocks * HALO
        for start in range(0, half, HALO):
            pair = []
            for row in (start, start + half):
                terms = [
                    ref[pl.ds(block * THIRD + row % THIRD, HALO), pl.ds(2 * THIRD, THIRD)]
                    for ref, block in own_sum(new, row // THIRD)
                ]
                pair.append(sum(terms[1:], terms[0]))
            here = pl.ds(start, HALO)
            send_columns(
                r,
                here,
                jnp.where(low, pltpu.roll(pair[0], HALF, 1), pair[1]),
                jnp.where(low, pair[0], pltpu.roll(pair[1], HALF, 1)),
            )
    else:
        middle = blocks - 6
        for num in range(blocks):
            to_a, to_b = pick(r.edge[4] != 0, *strips_of(own_sum(new, num)))
            r.to_a[rows_at(num), :] = to_a
            if not r.parted:
                r.to_b[rows_at(num), :] = to_b
            elif num < 3 or num >= 3 + middle:
                r.to_end[rows_at(num if num < 3 else num - middle), :] = to_b
    gamma = total(square)
    curve = gamma + total(r.acc[2] + r.curve[...])
    r.part[...] = lanes_of(r.part.shape, gamma, curve, total(cross))


def last_rows(r, start, corrected, residual, at):
    blocks = 2 * r.tiles + 1
    half = blocks * HALO
    low = lane_mask()
    num, offset = start // THIRD, start % THIRD
    upper = start < half
    west, east = from_columns(r, start if upper else start - half, HALO)
    if upper:
        east = pltpu.roll(east, HALF, 1)
    else:
        west = pltpu.roll(west, HALF, 1)
    add = [jnp.where(low, west, 0.0), jnp.where(low, 0.0, east)]
    for ref, block in own_sum(r, num):
        there = pl.ds(block * THIRD + offset, HALO)
        add = [a + ref[there, pl.ds(i * THIRD, THIRD)] for i, a in enumerate(add)]
    if num == 0 or num == blocks - 1:
        spill = from_rows(r, 0 if num == 0 else 1, pl.ds(0, HALO))
        add = [a + tile_of(spill, i) for i, a in enumerate(add)]
        olds, here = old_of(r, "edge"), pl.ds((0 if num == 0 else THIRD) + offset, HALO)
    else:
        olds, here = old_of(r, "mid"), pl.ds(start - THIRD, HALO)
    for i, a in enumerate(add):
        lanes = pl.ds(i * THIRD, THIRD)
        past = [ref[here, lanes] for ref in olds]
        direct = past[0]
        moved = r.steps[0] * direct
        for old, ratio, step in zip(past[1:], r.ratios, r.steps[1:]):
            direct = old + ratio * direct
            moved = moved + step * direct
        mapped = a + past[-1] + r.back * (past[-2] - past[-1])
        corrected[pl.ds(at, HALO), lanes] = moved
        residual[pl.ds(at, HALO), lanes] = past[-1] - r.steps[-1] * mapped


def last_middle_kernel(r):
    take_scalars(r, r.coef)
    for start in range(THIRD, 2 * r.tiles * THIRD, HALO):
        last_rows(r, start, r.corrected, r.residual, start - HALO)


def last_edge_kernel(r):
    take_scalars(r, r.coef)
    rows = 2 * r.tiles * THIRD
    copies = []
    for side in range(2):
        last_rows(r, HALO + side * (rows - HALO), r.corrected_rows, r.residual_rows, side * HALO)
        here = pl.ds(side * HALO, HALO)
        there = pl.ds(side * (rows - HALO), HALO)
        for num, (source, target) in enumerate(
            ((r.corrected_rows, r.corrected), (r.residual_rows, r.residual))
        ):
            copy = pltpu.make_async_copy(source.at[here, :], target.at[there, :], r.sems.at[side, num])
            copy.start()
            copies.append(copy)
    for copy in copies:
        copy.wait()


class Refs:
    def __init__(self, **names):
        self.__dict__.update(names)


SCALARS = ("occ", "kid", "edge")
PARAMS = pltpu.CompilerParams(vmem_limit_bytes=16 * 1024 * 1024)


def run(body, ins, outs, scratch=None, onto=None, **static):
    scratch, onto = scratch or {}, onto or {}
    names = [*ins, *("old_" + name for name in onto), *outs, *onto, *scratch]

    def kernel(*refs):
        body(Refs(**static, **dict(zip(names, refs))))

    whole = pl.BlockSpec(memory_space=pltpu.VMEM)
    placed = [pl.BlockSpec(memory_space=pl.ANY)] * len(onto)
    shapes = [*outs.values(), *(value.shape for value in onto.values())]
    result = pl.pallas_call(
        kernel,
        name=body.__name__,
        out_shape=[jax.ShapeDtypeStruct(dims, F32) for dims in shapes],
        in_specs=[
            pl.BlockSpec(memory_space=pltpu.SMEM) if name in SCALARS else whole for name in ins
        ]
        + placed,
        out_specs=[whole] * len(outs) + placed,
        scratch_shapes=[
            pltpu.VMEM(dims, F32) if isinstance(dims, tuple) else dims for dims in scratch.values()
        ],
        input_output_aliases={len(ins) + i: len(outs) + i for i in range(len(onto))},
        compiler_params=PARAMS,
    )(*ins.values(), *onto.values())
    return dict(zip([*outs, *onto], result))


def own_part(table, tile_count):
    column = lax.dynamic_index_in_dim(table, lax.axis_index("col"), 1, keepdims=False)
    return lax.dynamic_slice_in_dim(column, lax.axis_index("row") * tile_count, tile_count)


def swap(value, axis, first):
    pairs = [(i, i + 1) for i in range(first, lax.axis_size(axis) - 1, 2)]
    return lax.ppermute(value, axis, pairs + [(b, a) for a, b in pairs])


def shards(observed, kernels, occupied, kernel_index):
    rows, cols = observed.shape
    tiles = rows // TILE
    half, mid, ext = rows // 2, rows - 2 * HALO, rows + 2 * HALO
    n_row, n_col = lax.axis_size("row"), lax.axis_size("col")
    devices = n_row * n_col
    my_row, my_col = lax.axis_index("row"), lax.axis_index("col")
    occ = own_part(occupied, tiles)
    edge = jnp.stack(
        [my_row > 0, my_row < n_row - 1, my_col > 0, my_col < n_col - 1, my_col % 2 == 1, my_row % 2 == 1]
    ).astype(jnp.int32)
    host = {name: jnp.asarray(table) for name, table in tables().items()}
    sent = run(pack_kernel, dict(edge=edge, observed=observed), dict(to_a=(half, THIRD), to_b=(half, THIRD)))
    side_b = swap(sent["to_b"], "col", 1)
    side_z = swap(sent["to_a"], "col", 0)
    spec = run(
        spectra_kernel,
        dict(
            kid=own_part(kernel_index, tiles),
            occ=occ,
            kernels=jnp.pad(kernels, ((0, 0), (0, THIRD - KW), (0, THIRD - KW))),
            w_left=host["w_left"],
            w_right=host["w_right"],
        ),
        dict(spec=(tiles, 2, SLOTS, SLOTS)),
    )["spec"]
    side_b, side_z, spec = lax.optimization_barrier((side_b, side_z, spec))
    sides = dict(edge=edge, side_b=side_b, side_z=side_z)
    sent = run(halo_kernel, dict(observed=observed, **sides), dict(to_a=(HALO, WIN), to_b=(HALO, WIN)))
    sides, sent = lax.optimization_barrier((sides, sent))
    row_b, row_a = swap(sent["to_b"], "row", 1), swap(sent["to_a"], "row", 0)
    fixed = dict(occ=occ, spec=spec, **{name: host[name] for name in NAMES})
    state = {}
    for stage in range(ITERS):
        narrow = stage == ITERS - 1
        parted = 0 < stage < ITERS - 1
        moving = dict(sides)
        if stage == 0:
            moving["observed"] = observed
        known = dict(parts=parts) if stage else {}
        if stage > 1:
            known["coef"] = coef

        def old(where, *sums):
            names = ["res%d_%s" % (i, where) for i in range(stage)]
            return {name: state[name] for name in names + list(sums) if stage}

        middle = run(
            middle_kernel,
            {**fixed, **moving, **known, **old("mid", "top_sum", "mid_sum", "low_sum")},
            {
                "res_mid_new": (mid, WIN),
                "mid_sum_new": (mid - TILE, WIN),
                "acc": (3, 8, THIRD),
                **(dict(coef_new=COEFS) if stage else {}),
                **({"to_mid": (ext - 2 * WIN, THIRD)} if parted else {}),
            },
            stage=stage,
            tiles=tiles,
            parted=parted,
        )
        if parted:
            side_mid = swap(middle["to_mid"], "col", 1)
        outs = {"res_edge_new": (TILE, WIN), "top_sum_new": (WIN, WIN), "low_sum_new": (WIN, WIN)}
        outs["to_a"] = (ext // 2 if narrow else ext, THIRD)
        outs["to_end" if parted else "to_b"] = (2 * WIN if parted else outs["to_a"][0], THIRD)
        outs["part"] = (devices, THIRD)
        edges = run(
            edge_kernel,
            {
                **fixed,
                **moving,
                **(dict(coef=middle["coef_new"]) if stage else {}),
                **old("edge", "top_sum", "low_sum"),
                "row_b": row_b,
                "row_a": row_a,
                **{name: middle[name] for name in ("res_mid_new", "mid_sum_new", "acc")},
            },
            outs,
            dict(curve=(8, THIRD)),
            stage=stage,
            tiles=tiles,
            parted=parted,
            narrow=narrow,
        )
        state["res%d_mid" % stage] = middle["res_mid_new"]
        state["res%d_edge" % stage] = edges["res_edge_new"]
        state["mid_sum"] = middle["mid_sum_new"]
        state["top_sum"] = edges["top_sum_new"]
        state["low_sum"] = edges["low_sum_new"]
        part, to_a = edges["part"], edges["to_a"]
        sides = {}
        if parted:
            sides["side_mid"], part, to_a, to_end = lax.optimization_barrier(
                (side_mid, part, to_a, edges["to_end"])
            )
        sides["side_z"] = swap(to_a, "col", 0)
        if parted:
            sides["side_end"] = swap(to_end, "col", 1)
        else:
            sides["side_b"] = swap(edges["to_b"], "col", 1)
        parts = lax.all_to_all(part, ("row", "col"), 0, 0, tiled=True)
        sides, parts = lax.optimization_barrier((sides, parts))
        sides["edge"] = edge
        strip = (HALO, TILE) if narrow else (THIRD, WIN)
        coef = middle.get("coef_new")
        sent = run(
            row_strip_kernel,
            dict(
                **(dict(parts=parts, coef=coef) if narrow else {}),
                top_sum=state["top_sum"],
                low_sum=state["low_sum"],
                **sides,
            ),
            dict(to_a=strip, to_b=strip, **(dict(coef_new=COEFS) if narrow else {})),
            stage=stage + 1,
            tiles=tiles,
            narrow=narrow,
        )
        row_b, row_a = swap(sent["to_b"], "row", 1), swap(sent["to_a"], "row", 0)

    def olds(where):
        return {name: state[name] for name in ["res%d_%s" % (i, where) for i in range(ITERS)]}

    coef = sent["coef_new"]
    ends = dict(top_sum=state["top_sum"], low_sum=state["low_sum"])
    out = run(
        last_middle_kernel,
        dict(coef=coef, mid_sum=state["mid_sum"], **ends, **sides, **olds("mid")),
        dict(corrected=(rows, cols), residual=(rows, cols)),
        stage=ITERS,
        tiles=tiles,
    )
    out = run(
        last_edge_kernel,
        dict(coef=coef, row_b=row_b, row_a=row_a, **ends, **sides, **olds("edge")),
        {},
        dict(
            corrected_rows=(2 * HALO, cols),
            residual_rows=(2 * HALO, cols),
            sems=pltpu.SemaphoreType.DMA((2, 2)),
        ),
        out,
        stage=ITERS,
        tiles=tiles,
    )
    return out["corrected"], out["residual"]


def solution(mesh):
    placed = (P("row", "col"), P(), P(), P())
    return jax.shard_map(
        shards,
        mesh=mesh,
        in_specs=placed,
        out_specs=(P("row", "col"), P("row", "col")),
        check_vma=False,
    )
```

```python
import functools
import math

import jax
import jax.numpy as jnp
import numpy as np
from jax import lax
from jax.experimental import pallas as pl
from jax.experimental.pallas import tpu as pltpu
from jax.sharding import PartitionSpec as P

TILE = 256
HALO = 64
KW = 65
ITERS = 3
WIN = TILE + 2 * HALO
THIRD = WIN // 3
HALF = THIRD // 2
SLOTS = 2 * THIRD
BF = jnp.bfloat16
F32 = jnp.float32


def hi_lo(table):
    high = table.astype(np.float32).astype(jnp.bfloat16)
    low = (table - high.astype(np.float64)).astype(np.float32).astype(jnp.bfloat16)
    return high, low


@functools.cache
def tables():
    spots = np.arange(THIRD)
    low_freq = 3 * np.arange(HALF)
    full = math.sqrt(2.0 / WIN)
    cos_part = np.cos(2 * np.pi * (low_freq[:, None] * spots % WIN) / WIN) * full
    sin_part = np.sin(2 * np.pi * (low_freq[:, None] * spots % WIN) / WIN) * full
    cos_part[0] = math.sqrt(1.0 / WIN)
    sin_part[0] = np.where(spots % 2 == 0, 1.0, -1.0) * math.sqrt(1.0 / WIN)
    small = np.concatenate([cos_part, sin_part])
    angle = 2 * np.pi * ((3 * spots[:, None] + 1) * spots % WIN) / WIN
    root = math.sqrt(3.0) / 2
    large = full * np.block(
        [[np.cos(angle), -root * np.sin(angle)], [np.sin(angle), root * np.cos(angle)]]
    )
    freqs = np.concatenate([low_freq, low_freq, 3 * spots + 1])
    freqs[HALF] = WIN // 2
    taps = np.arange(THIRD)
    turn = 2 * np.pi * (freqs[:, None] * taps % WIN) / WIN
    keep = (taps < KW)[None, :]
    sines = np.sin(turn)
    sines[0] = 0.0
    sines[HALF] = 0.0
    waves = np.concatenate([np.cos(turn) * keep, sines * keep])

    sh, sl = hi_lo(small)
    gh, gl = hi_lo(large)
    wh, wl = hi_lo(waves)
    return dict(
        large=np.concatenate([gh, gl]),
        large_t=np.concatenate([gh.T, gl.T]),
        small=np.concatenate([sh, sl]),
        small_t=np.concatenate([sh.T, sl.T]),
        w_left=np.concatenate([wh, wl, wh], 1),
        w_right=np.concatenate([wh.T, wl.T, wh.T], 0),
    )


NAMES = ("large", "large_t", "small", "small_t")


def split(value):
    high = value.astype(BF)
    return high, (value - high.astype(F32)).astype(BF)


def dot(left, right):
    return jnp.dot(left, right, preferred_element_type=F32)


def right_large(value, table):
    high, low = split(value)
    return dot(
        jnp.concatenate([high, high, low], 1),
        jnp.concatenate([table[...], table[:SLOTS]], 0),
    )


def right_small(value, table):
    high, low = split(value)
    coarse, fine = table[:THIRD], table[THIRD:]
    both = dot(
        jnp.concatenate([high, low], 1),
        jnp.concatenate(
            [
                jnp.concatenate([coarse, fine], 1),
                jnp.concatenate([coarse, jnp.zeros_like(fine)], 1),
            ],
            0,
        ),
    )
    return both[:, :THIRD] + both[:, THIRD:]


def left_large(value, table):
    high, low = split(value)
    both = dot(table[...], high)
    return both[:SLOTS] + both[SLOTS:] + dot(table[:SLOTS], low)


def left_small(value, table):
    high, low = split(value)
    coarse, fine = table[:THIRD], table[THIRD:]
    both = dot(
        jnp.concatenate(
            [
                jnp.concatenate([coarse, coarse], 1),
                jnp.concatenate([fine, jnp.zeros_like(fine)], 1),
            ],
            0,
        ),
        jnp.concatenate([high, low], 0),
    )
    return both[:THIRD] + both[THIRD:]


def butterfly(first, second, third):
    total = second + third
    return first + total, first - 0.5 * total, second - third


def unbutterfly(plain, real, diff):
    base = plain - 0.5 * real
    return plain + real, base + diff, base - diff


def spectra_kernel(r):
    def body(slot, carry):
        @pl.when(r.occ[slot] != 0)
        def _():
            high, low = split(r.kernels[r.kid[slot]])
            half = dot(r.w_left[...], jnp.concatenate([high, high, low], 0))
            high, low = split(half)
            quads = dot(jnp.concatenate([high, high, low], 1), r.w_right[...])
            cc = quads[:SLOTS, :SLOTS]
            cs = quads[:SLOTS, SLOTS:]
            sc = quads[SLOTS:, :SLOTS]
            ss = quads[SLOTS:, SLOTS:]
            r.spec[slot, 0] = cc * cc + ss * ss + (sc * sc + cs * cs)
            r.spec[slot, 1] = 2.0 * (sc * cs - cc * ss)

        @pl.when(r.occ[slot] == 0)
        def _():
            r.spec[slot] = jnp.zeros((2, SLOTS, SLOTS), F32)

        return carry

    lax.fori_loop(0, r.spec.shape[0], body, 0)


def tile_of(block, num):
    return block[:, num * THIRD : (num + 1) * THIRD]


def lane_mask():
    return lax.broadcasted_iota(jnp.int32, (1, THIRD), 1) < HALF


def apply_spectrum(low_rows, high_rows, spec_ref, slot, mixed):
    lanes = pl.ds(0 if mixed else THIRD, THIRD)
    sign = jnp.where(lane_mask(), -1.0, 1.0).astype(F32)

    def band(cos_rows, sin_rows, cos_at, sin_at, size):
        pc = spec_ref[slot, 0, pl.ds(cos_at, size), lanes]
        ps = spec_ref[slot, 0, pl.ds(sin_at, size), lanes] if sin_at != cos_at else pc
        cross = spec_ref[slot, 1, pl.ds(cos_at, size), lanes]
        if mixed:
            cross = cross * sign
            return (
                pc * cos_rows + cross * pltpu.roll(sin_rows, HALF, 1),
                ps * sin_rows - cross * pltpu.roll(cos_rows, HALF, 1),
            )
        c1, c2, s1, s2 = cos_rows[:, :THIRD], cos_rows[:, THIRD:], sin_rows[:, :THIRD], sin_rows[:, THIRD:]
        return (
            jnp.concatenate([pc * c1 - cross * s2, pc * c2 + cross * s1], 1),
            jnp.concatenate([ps * s1 + cross * c2, ps * s2 - cross * c1], 1),
        )

    low = band(low_rows[:HALF], low_rows[HALF:], 0, HALF, HALF)
    high = band(high_rows[:THIRD], high_rows[THIRD:], THIRD, THIRD, THIRD)
    return jnp.concatenate(low, 0), jnp.concatenate(high, 0)


def window_products(windows, slots, r):
    count = len(windows)
    folded = [
        [butterfly(*(tile_of(block, i) for i in range(3))) for block in blocks] for blocks in windows
    ]
    small = [[right_small(plain, r.small_t) for plain, _, _ in blocks] for blocks in folded]
    large = [
        [right_large(jnp.concatenate([real, diff], 1), r.large_t) for _, real, diff in blocks]
        for blocks in folded
    ]

    def to_rows(windows):
        parts = [butterfly(*blocks) for blocks in windows]
        plain, real, diff = (jnp.concatenate([part[i] for part in parts], 1) for i in range(3))
        return left_small(plain, r.small), left_large(jnp.concatenate([real, diff], 0), r.large)

    def from_rows_of(bands, mixed):
        width = THIRD if mixed else 2 * THIRD
        done = []
        for num, slot in enumerate(slots):
            here = slice(num * width, (num + 1) * width)
            done.append(apply_spectrum(bands[0][:, here], bands[1][:, here], r.spec, slot, mixed))
        low_rows, high_rows = (jnp.concatenate([band[i] for band in done], 1) for i in range(2))
        plain = left_small(low_rows, r.small_t)
        both = left_large(high_rows, r.large_t)
        return unbutterfly(plain, both[:THIRD], both[THIRD:])

    small_bands, large_bands = to_rows(small), to_rows(large)
    small = from_rows_of(small_bands, True)
    large = from_rows_of(large_bands, False)
    plain = [[right_small(tile_of(block, num), r.small) for block in small] for num in range(count)]
    results = []
    for num in range(count):
        here = slice(2 * num * THIRD, 2 * (num + 1) * THIRD)
        both = [right_large(block[:, here], r.large) for block in large]
        results.append(
            [
                jnp.concatenate(unbutterfly(a, b[:, :THIRD], b[:, THIRD:]), 1)
                for a, b in zip(plain[num], both)
            ]
        )
    return results


def fold8(value):
    rows = value.reshape(value.shape[0] // 8, 8, value.shape[1]).sum(0)
    return sum(tile_of(rows, i) for i in range(value.shape[1] // THIRD))


def total(value):
    return jnp.sum(jnp.sum(value, 0, keepdims=True), 1, keepdims=True)


def lanes_of(shape, *values):
    lanes = lax.broadcasted_iota(jnp.int32, shape, 1)
    out = jnp.zeros(shape, F32)
    for num, value in enumerate(values):
        out = jnp.where(lanes == num, value, out)
    return out


def rows_at(num, count=1):
    return pl.ds(num * THIRD, count * THIRD)


def put(ref, here, tiles):
    for num, tile in enumerate(tiles):
        ref[here, pl.ds(num * THIRD, THIRD)] = tile


def own_sum(r, num):
    last = 2 * r.tiles
    terms = []
    if num <= 2:
        terms.append((r.top_sum, num))
    if 2 <= num <= last - 2:
        terms.append((r.mid_sum, num - 2))
    if num >= last - 2:
        terms.append((r.low_sum, num - last + 2))
    return terms


ENERGY, POWER, STEP, RATIO, BACK = 0, 1, 2, 2 + ITERS, 2 + 2 * ITERS
COEFS = (3 + 2 * ITERS, 8, THIRD)


def put_scalars(r):
    sums = jnp.sum(r.parts[...], 0, keepdims=True)
    energy, curve, cross = sums[:, 0:1], sums[:, 1:2], sums[:, 2:3]
    values = {ENERGY: energy, POWER: curve}
    last = r.stage - 1
    if last:
        ratio = energy / r.coef[ENERGY, 0:1, 0:1]
        values[POWER] = curve + ratio * (2.0 * cross + ratio * r.coef[POWER, 0:1, 0:1])
        values[RATIO + last] = ratio
        values[BACK] = ratio / r.coef[STEP + last - 1, 0:1, 0:1]
        for num in range(last):
            r.coef_new[STEP + num] = r.coef[STEP + num]
            r.coef_new[RATIO + num] = r.coef[RATIO + num]
    values[STEP + last] = energy / values[POWER]
    for num, value in values.items():
        r.coef_new[num] = jnp.broadcast_to(value, (8, THIRD))


def take_scalars(r, coef):
    r.steps = [coef[STEP + i, 0:1, :] for i in range(r.stage)]
    r.ratios = [coef[RATIO + i, 0:1, :] for i in range(1, r.stage)]
    r.back = coef[BACK, 0:1, :] if r.stage > 1 else None


def pick(odd, first, second):
    return jnp.where(odd, first, second), jnp.where(odd, second, first)


def from_columns(r, start, size):
    second = getattr(r, "side_b", None)
    there = start
    if second is None:
        middle = r.side_mid.shape[0]
        if start < WIN:
            second = r.side_end
        elif start < WIN + middle:
            second, there = r.side_mid, start - WIN
        else:
            second, there = r.side_end, start - middle
    return pick(r.edge[4] != 0, r.side_z[pl.ds(start, size), :], second[pl.ds(there, size), :])


def from_rows(r, side, here):
    return pick(r.edge[5] != 0, r.row_a[here, :], r.row_b[here, :])[side]


def send_columns(r, here, to_left, to_right):
    r.to_a[here, :], r.to_b[here, :] = pick(r.edge[4] != 0, to_left, to_right)


def strips_of(terms):
    low = lane_mask()
    pieces = [ref[rows_at(block), :] for ref, block in terms]
    block = sum(pieces[1:], pieces[0])
    return (
        jnp.where(low, tile_of(block, 0), tile_of(block, 2)),
        jnp.where(low, tile_of(block, 2), tile_of(block, 1)),
    )


def send_rows(r, above, below):
    odd = r.edge[5] != 0
    here = pl.ds(0, r.to_a.shape[0])
    pairs = [pick(odd, a, b) for a, b in zip(above, below)]
    put(r.to_a, here, [a for a, _ in pairs])
    put(r.to_b, here, [b for _, b in pairs])


def old_of(r, name):
    return [getattr(r, "res%d_%s" % (i, name)) for i in range(r.stage)]


def update(r, num, name, here, size, offset, spill, keep):
    low = lane_mask()
    sums = [ref[pl.ds(block * THIRD + offset, size), :] for ref, block in own_sum(r, num)]
    west, east = from_columns(r, num * THIRD + offset, size)
    add = [
        jnp.where(low, west, 0.0),
        jnp.where(low, 0.0, east),
        jnp.where(low, east, west),
    ]
    for block in sums + ([] if spill is None else [spill]):
        add = [a + tile_of(block, i) for i, a in enumerate(add)]
    olds = [ref[here, :] for ref in old_of(r, name)[-2:]]
    old = [tile_of(olds[-1], i) for i in range(3)]
    mapped = [a + b for a, b in zip(add, old)]
    mapped[2] = mapped[2] * jnp.where(low, r.edge[3].astype(F32), r.edge[2].astype(F32))
    if keep is not None:
        mapped = [a * keep for a in mapped]
    if r.stage > 1:
        mapped = [a + r.back * (tile_of(olds[0], i) - old[i]) for i, a in enumerate(mapped)]
    return [a - r.steps[-1] * b for a, b in zip(old, mapped)], mapped


def unpacked_sides(r, start, size):
    half = r.side_z.shape[0]
    low = lane_mask()
    out = []
    while size:
        upper = start < half
        count = min(size, half - start) if upper else size
        left, right = from_columns(r, start if upper else start - half, count)
        if upper:
            left = pltpu.roll(left, HALF, 1)
        else:
            right = pltpu.roll(right, HALF, 1)
        out.append(jnp.where(low, right, left))
        start, size = start + count, size - count
    return out[0] if len(out) == 1 else jnp.concatenate(out, 0)


def initial(r, start, size):
    here = pl.ds(start, size)
    block = r.observed[here, :]
    return [tile_of(block, 0), tile_of(block, 1), unpacked_sides(r, start, size)]


def pack_kernel(r):
    half = r.to_a.shape[0]
    low = lane_mask()
    first = [r.observed[pl.ds(start, half), pl.ds(0, THIRD)] for start in (0, half)]
    second = [r.observed[pl.ds(start, half), pl.ds(THIRD, THIRD)] for start in (0, half)]
    send_columns(
        r,
        pl.ds(0, half),
        jnp.where(low, first[0], pltpu.roll(first[1], HALF, 1)),
        jnp.where(low, pltpu.roll(second[0], HALF, 1), second[1]),
    )


def halo_kernel(r):
    send_rows(r, initial(r, 0, HALO), initial(r, r.observed.shape[0] - HALO, HALO))


def row_strip_kernel(r):
    low = lane_mask()
    blocks = 2 * r.tiles + 1
    size = r.to_a.shape[0]
    strips = []
    for side, ref in ((0, r.top_sum), (1, r.low_sum)):
        own = ref[pl.ds(side * (WIN - size), size), :]
        if r.narrow:
            west, east = from_columns(r, side * (blocks * HALO - size), size)
            if side:
                west = pltpu.roll(west, HALF, 1)
            else:
                east = pltpu.roll(east, HALF, 1)
            add = [jnp.where(low, west, 0.0), jnp.where(low, 0.0, east)]
        else:
            west, east = from_columns(r, side * (blocks * THIRD - size), size)
            add = [
                jnp.where(low, west, 0.0),
                jnp.where(low, 0.0, east),
                jnp.where(low, east, west),
            ]
        strips.append([tile_of(own, i) + a for i, a in enumerate(add)])
    send_rows(r, *strips)
    if r.narrow:
        put_scalars(r)


def middle_kernel(r):
    square = cross = jnp.zeros((8, THIRD), F32)
    blocks = 2 * r.tiles + 1
    if r.stage > 0:
        put_scalars(r)
        take_scalars(r, r.coef_new)
    for num in range(1, blocks - 1):
        here = rows_at(num - 1)
        if r.stage == 0:
            fresh = initial(r, num * THIRD - HALO, THIRD)
        else:
            fresh, mapped = update(r, num, "mid", here, THIRD, 0, None, None)
            cross += sum(fold8(a * b) for a, b in zip(fresh[:2], mapped))
        put(r.res_mid_new, here, fresh)
        square += sum(fold8(a * a) for a in fresh[:2])
    r.acc[0] = square
    r.acc[1] = cross
    r.acc[2] = jnp.zeros((8, THIRD), F32)
    inner = list(range(1, r.tiles - 1))
    some = r.occ[inner[0]]
    for slot in inner[1:]:
        some = some + r.occ[slot]

    @pl.when(some != 0)
    def _():
        windows = [
            [r.res_mid_new[rows_at(2 * slot + i - 1), :] for i in range(3)] for slot in inner
        ]
        results = window_products(windows, inner, r)
        curve = jnp.zeros((8, THIRD), F32)
        for num, (window, result) in enumerate(zip(windows, results)):
            curve += sum(fold8(a * b) for a, b in zip(window, result))
            first = result[0] if num == 0 else result[0] + results[num - 1][2]
            r.mid_sum_new[rows_at(2 * num), :] = first
            r.mid_sum_new[rows_at(2 * num + 1), :] = result[1]
        r.mid_sum_new[rows_at(2 * len(inner)), :] = results[-1][2]
        r.acc[2] = curve

    @pl.when(some == 0)
    def _():
        r.mid_sum_new[...] = jnp.zeros(r.mid_sum_new.shape, F32)

    if r.parted:
        for num in range(r.to_mid.shape[0] // THIRD):
            strips = strips_of([(r.mid_sum_new, num + 1)])
            r.to_mid[rows_at(num), :] = pick(r.edge[4] != 0, *strips)[1]


def edge_kernel(r):
    square, cross = r.acc[0], r.acc[1]
    blocks = 2 * r.tiles + 1
    rows = 2 * r.tiles * THIRD
    if r.stage > 0:
        take_scalars(r, r.coef)
    for side in range(2):
        num = side * (blocks - 1)
        for offset in (0, HALO):
            here = pl.ds(side * THIRD + offset, HALO)
            inside = (offset > 0) == (side == 0)
            if r.stage == 0:
                if inside:
                    fresh = initial(r, side * (rows - HALO), HALO)
                else:
                    halo = from_rows(r, side, pl.ds(0, HALO))
                    fresh = [tile_of(halo, i) for i in range(3)]
            else:
                spill = from_rows(r, side, pl.ds(offset, HALO))
                keep = None if inside else r.edge[side].astype(F32)
                fresh, mapped = update(r, num, "edge", here, HALO, offset, spill, keep)
                if inside:
                    cross += sum(fold8(a * b) for a, b in zip(fresh[:2], mapped))
            put(r.res_edge_new, here, fresh)
            if inside:
                square += sum(fold8(a * a) for a in fresh[:2])
    slots = [0, r.tiles - 1]
    some = r.occ[slots[0]] + r.occ[slots[1]]

    @pl.when(some != 0)
    def _():
        far = blocks - 4
        windows = [
            [r.res_edge_new[rows_at(0), :]] + [r.res_mid_new[rows_at(i), :] for i in range(2)],
            [r.res_mid_new[rows_at(far + i), :] for i in range(2)] + [r.res_edge_new[rows_at(1), :]],
        ]
        results = window_products(windows, slots, r)
        curve = jnp.zeros((8, THIRD), F32)
        for window, result, ref in zip(windows, results, (r.top_sum_new, r.low_sum_new)):
            curve += sum(fold8(a * b) for a, b in zip(window, result))
            for num in range(3):
                ref[rows_at(num), :] = result[num]
        r.curve[...] = curve

    @pl.when(some == 0)
    def _():
        r.top_sum_new[...] = jnp.zeros((WIN, WIN), F32)
        r.low_sum_new[...] = jnp.zeros((WIN, WIN), F32)
        r.curve[...] = jnp.zeros((8, THIRD), F32)

    gamma = total(square)
    curve = gamma + total(r.acc[2] + r.curve[...])
    r.part[...] = lanes_of(r.part.shape, gamma, curve, total(cross))

    low = lane_mask()
    new = Refs(tiles=r.tiles, top_sum=r.top_sum_new, mid_sum=r.mid_sum_new, low_sum=r.low_sum_new)
    if r.narrow:
        half = blocks * HALO
        for start in range(0, half, HALO):
            pair = []
            for row in (start, start + half):
                terms = [
                    ref[pl.ds(block * THIRD + row % THIRD, HALO), pl.ds(2 * THIRD, THIRD)]
                    for ref, block in own_sum(new, row // THIRD)
                ]
                pair.append(sum(terms[1:], terms[0]))
            here = pl.ds(start, HALO)
            send_columns(
                r,
                here,
                jnp.where(low, pltpu.roll(pair[0], HALF, 1), pair[1]),
                jnp.where(low, pair[0], pltpu.roll(pair[1], HALF, 1)),
            )
    else:
        middle = blocks - 6
        for num in range(blocks):
            to_a, to_b = pick(r.edge[4] != 0, *strips_of(own_sum(new, num)))
            r.to_a[rows_at(num), :] = to_a
            if not r.parted:
                r.to_b[rows_at(num), :] = to_b
            elif num < 3 or num >= 3 + middle:
                r.to_end[rows_at(num if num < 3 else num - middle), :] = to_b


def last_rows(r, start, corrected, residual, at):
    blocks = 2 * r.tiles + 1
    half = blocks * HALO
    low = lane_mask()
    num, offset = start // THIRD, start % THIRD
    upper = start < half
    west, east = from_columns(r, start if upper else start - half, HALO)
    if upper:
        east = pltpu.roll(east, HALF, 1)
    else:
        west = pltpu.roll(west, HALF, 1)
    add = [jnp.where(low, west, 0.0), jnp.where(low, 0.0, east)]
    for ref, block in own_sum(r, num):
        there = pl.ds(block * THIRD + offset, HALO)
        add = [a + ref[there, pl.ds(i * THIRD, THIRD)] for i, a in enumerate(add)]
    if num == 0 or num == blocks - 1:
        spill = from_rows(r, 0 if num == 0 else 1, pl.ds(0, HALO))
        add = [a + tile_of(spill, i) for i, a in enumerate(add)]
        olds, here = old_of(r, "edge"), pl.ds((0 if num == 0 else THIRD) + offset, HALO)
    else:
        olds, here = old_of(r, "mid"), pl.ds(start - THIRD, HALO)
    for i, a in enumerate(add):
        lanes = pl.ds(i * THIRD, THIRD)
        past = [ref[here, lanes] for ref in olds]
        direct = past[0]
        moved = r.steps[0] * direct
        for old, ratio, step in zip(past[1:], r.ratios, r.steps[1:]):
            direct = old + ratio * direct
            moved = moved + step * direct
        mapped = a + past[-1] + r.back * (past[-2] - past[-1])
        corrected[pl.ds(at, HALO), lanes] = moved
        residual[pl.ds(at, HALO), lanes] = past[-1] - r.steps[-1] * mapped


def last_middle_kernel(r):
    take_scalars(r, r.coef)
    for start in range(THIRD, 2 * r.tiles * THIRD, HALO):
        last_rows(r, start, r.corrected, r.residual, start - HALO)


def last_edge_kernel(r):
    take_scalars(r, r.coef)
    rows = 2 * r.tiles * THIRD
    copies = []
    for side in range(2):
        last_rows(r, HALO + side * (rows - HALO), r.corrected_rows, r.residual_rows, side * HALO)
        here = pl.ds(side * HALO, HALO)
        there = pl.ds(side * (rows - HALO), HALO)
        for num, (source, target) in enumerate(
            ((r.corrected_rows, r.corrected), (r.residual_rows, r.residual))
        ):
            copy = pltpu.make_async_copy(source.at[here, :], target.at[there, :], r.sems.at[side, num])
            copy.start()
            copies.append(copy)
    for copy in copies:
        copy.wait()


class Refs:
    def __init__(self, **names):
        self.__dict__.update(names)


SCALARS = ("occ", "kid", "edge")
PARAMS = pltpu.CompilerParams(vmem_limit_bytes=16 * 1024 * 1024)


def run(body, ins, outs, scratch=None, onto=None, **static):
    scratch, onto = scratch or {}, onto or {}
    names = [*ins, *("old_" + name for name in onto), *outs, *onto, *scratch]

    def kernel(*refs):
        body(Refs(**static, **dict(zip(names, refs))))

    whole = pl.BlockSpec(memory_space=pltpu.VMEM)
    placed = [pl.BlockSpec(memory_space=pl.ANY)] * len(onto)
    shapes = [*outs.values(), *(value.shape for value in onto.values())]
    result = pl.pallas_call(
        kernel,
        name=body.__name__,
        out_shape=[jax.ShapeDtypeStruct(dims, F32) for dims in shapes],
        in_specs=[
            pl.BlockSpec(memory_space=pltpu.SMEM) if name in SCALARS else whole for name in ins
        ]
        + placed,
        out_specs=[whole] * len(outs) + placed,
        scratch_shapes=[
            pltpu.VMEM(dims, F32) if isinstance(dims, tuple) else dims for dims in scratch.values()
        ],
        input_output_aliases={len(ins) + i: len(outs) + i for i in range(len(onto))},
        compiler_params=PARAMS,
    )(*ins.values(), *onto.values())
    return dict(zip([*outs, *onto], result))


def own_part(table, tile_count):
    column = lax.dynamic_index_in_dim(table, lax.axis_index("col"), 1, keepdims=False)
    return lax.dynamic_slice_in_dim(column, lax.axis_index("row") * tile_count, tile_count)


def swap(value, axis, first):
    pairs = [(i, i + 1) for i in range(first, lax.axis_size(axis) - 1, 2)]
    return lax.ppermute(value, axis, pairs + [(b, a) for a, b in pairs])


def shards(observed, kernels, occupied, kernel_index):
    rows, cols = observed.shape
    tiles = rows // TILE
    half, mid, ext = rows // 2, rows - 2 * HALO, rows + 2 * HALO
    n_row, n_col = lax.axis_size("row"), lax.axis_size("col")
    devices = n_row * n_col
    my_row, my_col = lax.axis_index("row"), lax.axis_index("col")
    occ = own_part(occupied, tiles)
    edge = jnp.stack(
        [my_row > 0, my_row < n_row - 1, my_col > 0, my_col < n_col - 1, my_col % 2 == 1, my_row % 2 == 1]
    ).astype(jnp.int32)
    host = {name: jnp.asarray(table) for name, table in tables().items()}
    sent = run(pack_kernel, dict(edge=edge, observed=observed), dict(to_a=(half, THIRD), to_b=(half, THIRD)))
    side_b = swap(sent["to_b"], "col", 1)
    side_z = swap(sent["to_a"], "col", 0)
    spec = run(
        spectra_kernel,
        dict(
            kid=own_part(kernel_index, tiles),
            occ=occ,
            kernels=jnp.pad(kernels, ((0, 0), (0, THIRD - KW), (0, THIRD - KW))),
            w_left=host["w_left"],
            w_right=host["w_right"],
        ),
        dict(spec=(tiles, 2, SLOTS, SLOTS)),
    )["spec"]
    side_b, side_z, spec = lax.optimization_barrier((side_b, side_z, spec))
    sides = dict(edge=edge, side_b=side_b, side_z=side_z)
    sent = run(halo_kernel, dict(observed=observed, **sides), dict(to_a=(HALO, WIN), to_b=(HALO, WIN)))
    sides, sent = lax.optimization_barrier((sides, sent))
    row_b, row_a = swap(sent["to_b"], "row", 1), swap(sent["to_a"], "row", 0)
    fixed = dict(occ=occ, spec=spec, **{name: host[name] for name in NAMES})
    state = {}
    for stage in range(ITERS):
        narrow = stage == ITERS - 1
        parted = 0 < stage < ITERS - 1
        moving = dict(sides)
        if stage == 0:
            moving["observed"] = observed
        known = dict(parts=parts) if stage else {}
        if stage > 1:
            known["coef"] = coef

        def old(where, *sums):
            names = ["res%d_%s" % (i, where) for i in range(stage)]
            return {name: state[name] for name in names + list(sums) if stage}

        middle = run(
            middle_kernel,
            {**fixed, **moving, **known, **old("mid", "top_sum", "mid_sum", "low_sum")},
            {
                "res_mid_new": (mid, WIN),
                "mid_sum_new": (mid - TILE, WIN),
                "acc": (3, 8, THIRD),
                **(dict(coef_new=COEFS) if stage else {}),
                **({"to_mid": (ext - 2 * WIN, THIRD)} if parted else {}),
            },
            stage=stage,
            tiles=tiles,
            parted=parted,
        )
        if parted:
            side_mid = swap(middle["to_mid"], "col", 1)
        outs = {"res_edge_new": (TILE, WIN), "top_sum_new": (WIN, WIN), "low_sum_new": (WIN, WIN)}
        outs["to_a"] = (ext // 2 if narrow else ext, THIRD)
        outs["to_end" if parted else "to_b"] = (2 * WIN if parted else outs["to_a"][0], THIRD)
        outs["part"] = (devices, THIRD)
        edges = run(
            edge_kernel,
            {
                **fixed,
                **moving,
                **(dict(coef=middle["coef_new"]) if stage else {}),
                **old("edge", "top_sum", "low_sum"),
                "row_b": row_b,
                "row_a": row_a,
                **{name: middle[name] for name in ("res_mid_new", "mid_sum_new", "acc")},
            },
            outs,
            dict(curve=(8, THIRD)),
            stage=stage,
            tiles=tiles,
            parted=parted,
            narrow=narrow,
        )
        state["res%d_mid" % stage] = middle["res_mid_new"]
        state["res%d_edge" % stage] = edges["res_edge_new"]
        state["mid_sum"] = middle["mid_sum_new"]
        state["top_sum"] = edges["top_sum_new"]
        state["low_sum"] = edges["low_sum_new"]
        part, to_a = edges["part"], edges["to_a"]
        sides = {}
        if parted:
            sides["side_mid"], part, to_a, to_end = lax.optimization_barrier(
                (side_mid, part, to_a, edges["to_end"])
            )
        sides["side_z"] = swap(to_a, "col", 0)
        if parted:
            sides["side_end"] = swap(to_end, "col", 1)
        else:
            sides["side_b"] = swap(edges["to_b"], "col", 1)
        parts = lax.all_to_all(part, ("row", "col"), 0, 0, tiled=True)
        sides, parts = lax.optimization_barrier((sides, parts))
        sides["edge"] = edge
        strip = (HALO, TILE) if narrow else (THIRD, WIN)
        coef = middle.get("coef_new")
        sent = run(
            row_strip_kernel,
            dict(
                **(dict(parts=parts, coef=coef) if narrow else {}),
                top_sum=state["top_sum"],
                low_sum=state["low_sum"],
                **sides,
            ),
            dict(to_a=strip, to_b=strip, **(dict(coef_new=COEFS) if narrow else {})),
            stage=stage + 1,
            tiles=tiles,
            narrow=narrow,
        )
        row_b, row_a = swap(sent["to_b"], "row", 1), swap(sent["to_a"], "row", 0)

    def olds(where):
        return {name: state[name] for name in ["res%d_%s" % (i, where) for i in range(ITERS)]}

    coef = sent["coef_new"]
    ends = dict(top_sum=state["top_sum"], low_sum=state["low_sum"])
    out = run(
        last_middle_kernel,
        dict(coef=coef, mid_sum=state["mid_sum"], **ends, **sides, **olds("mid")),
        dict(corrected=(rows, cols), residual=(rows, cols)),
        stage=ITERS,
        tiles=tiles,
    )
    out = run(
        last_edge_kernel,
        dict(coef=coef, row_b=row_b, row_a=row_a, **ends, **sides, **olds("edge")),
        {},
        dict(
            corrected_rows=(2 * HALO, cols),
            residual_rows=(2 * HALO, cols),
            sems=pltpu.SemaphoreType.DMA((2, 2)),
        ),
        out,
        stage=ITERS,
        tiles=tiles,
    )
    return out["corrected"], out["residual"]


def solution(mesh):
    placed = (P("row", "col"), P(), P(), P())
    return jax.shard_map(
        shards,
        mesh=mesh,
        in_specs=placed,
        out_specs=(P("row", "col"), P("row", "col")),
        check_vma=False,
    )
```

```python
import functools
import math

import jax
import jax.numpy as jnp
import numpy as np
from jax import lax
from jax.experimental import pallas as pl
from jax.experimental.pallas import tpu as pltpu
from jax.sharding import PartitionSpec as P

TILE = 256
HALO = 64
KW = 65
ITERS = 3
WIN = TILE + 2 * HALO
THIRD = WIN // 3
HALF = THIRD // 2
SLOTS = 2 * THIRD
BF = jnp.bfloat16
F32 = jnp.float32


def hi_lo(table):
    high = table.astype(np.float32).astype(jnp.bfloat16)
    low = (table - high.astype(np.float64)).astype(np.float32).astype(jnp.bfloat16)
    return high, low


@functools.cache
def tables():
    spots = np.arange(THIRD)
    low_freq = 3 * np.arange(HALF)
    full = math.sqrt(2.0 / WIN)
    cos_part = np.cos(2 * np.pi * (low_freq[:, None] * spots % WIN) / WIN) * full
    sin_part = np.sin(2 * np.pi * (low_freq[:, None] * spots % WIN) / WIN) * full
    cos_part[0] = math.sqrt(1.0 / WIN)
    sin_part[0] = np.where(spots % 2 == 0, 1.0, -1.0) * math.sqrt(1.0 / WIN)
    small = np.concatenate([cos_part, sin_part])
    angle = 2 * np.pi * ((3 * spots[:, None] + 1) * spots % WIN) / WIN
    root = math.sqrt(3.0) / 2
    large = full * np.block(
        [[np.cos(angle), -root * np.sin(angle)], [np.sin(angle), root * np.cos(angle)]]
    )
    freqs = np.concatenate([low_freq, low_freq, 3 * spots + 1])
    freqs[HALF] = WIN // 2
    taps = np.arange(THIRD)
    turn = 2 * np.pi * (freqs[:, None] * taps % WIN) / WIN
    keep = (taps < KW)[None, :]
    sines = np.sin(turn)
    sines[0] = 0.0
    sines[HALF] = 0.0
    waves = np.concatenate([np.cos(turn) * keep, sines * keep])

    sh, sl = hi_lo(small)
    gh, gl = hi_lo(large)
    wh, wl = hi_lo(waves)
    return dict(
        large=np.concatenate([gh, gl]),
        large_t=np.concatenate([gh.T, gl.T]),
        small=np.concatenate([sh, sl]),
        small_t=np.concatenate([sh.T, sl.T]),
        w_left=np.concatenate([wh, wl, wh], 1),
        w_right=np.concatenate([wh.T, wl.T, wh.T], 0),
    )


NAMES = ("large", "large_t", "small", "small_t")


def split(value):
    high = value.astype(BF)
    return high, (value - high.astype(F32)).astype(BF)


def dot(left, right):
    return jnp.dot(left, right, preferred_element_type=F32)


def right_large(value, table):
    high, low = split(value)
    return dot(
        jnp.concatenate([high, high, low], 1),
        jnp.concatenate([table[...], table[:SLOTS]], 0),
    )


def right_small(value, table):
    high, low = split(value)
    coarse, fine = table[:THIRD], table[THIRD:]
    both = dot(
        jnp.concatenate([high, low], 1),
        jnp.concatenate(
            [
                jnp.concatenate([coarse, fine], 1),
                jnp.concatenate([coarse, jnp.zeros_like(fine)], 1),
            ],
            0,
        ),
    )
    return both[:, :THIRD] + both[:, THIRD:]


def left_large(value, table):
    high, low = split(value)
    both = dot(table[...], high)
    return both[:SLOTS] + both[SLOTS:] + dot(table[:SLOTS], low)


def left_small(value, table):
    high, low = split(value)
    coarse, fine = table[:THIRD], table[THIRD:]
    both = dot(
        jnp.concatenate(
            [
                jnp.concatenate([coarse, coarse], 1),
                jnp.concatenate([fine, jnp.zeros_like(fine)], 1),
            ],
            0,
        ),
        jnp.concatenate([high, low], 0),
    )
    return both[:THIRD] + both[THIRD:]


def butterfly(first, second, third):
    total = second + third
    return first + total, first - 0.5 * total, second - third


def unbutterfly(plain, real, diff):
    base = plain - 0.5 * real
    return plain + real, base + diff, base - diff


def spectra_kernel(r):
    def body(slot, carry):
        @pl.when(r.occ[slot] != 0)
        def _():
            high, low = split(r.kernels[r.kid[slot]])
            half = dot(r.w_left[...], jnp.concatenate([high, high, low], 0))
            high, low = split(half)
            quads = dot(jnp.concatenate([high, high, low], 1), r.w_right[...])
            cc = quads[:SLOTS, :SLOTS]
            cs = quads[:SLOTS, SLOTS:]
            sc = quads[SLOTS:, :SLOTS]
            ss = quads[SLOTS:, SLOTS:]
            r.spec[slot, 0] = cc * cc + ss * ss + (sc * sc + cs * cs)
            r.spec[slot, 1] = 2.0 * (sc * cs - cc * ss)

        @pl.when(r.occ[slot] == 0)
        def _():
            r.spec[slot] = jnp.zeros((2, SLOTS, SLOTS), F32)

        return carry

    lax.fori_loop(0, r.spec.shape[0], body, 0)


def tile_of(block, num):
    return block[:, num * THIRD : (num + 1) * THIRD]


def lane_mask():
    return lax.broadcasted_iota(jnp.int32, (1, THIRD), 1) < HALF


def apply_spectrum(low_rows, high_rows, spec_ref, slot, mixed):
    lanes = pl.ds(0 if mixed else THIRD, THIRD)
    sign = jnp.where(lane_mask(), -1.0, 1.0).astype(F32)

    def band(cos_rows, sin_rows, cos_at, sin_at, size):
        pc = spec_ref[slot, 0, pl.ds(cos_at, size), lanes]
        ps = spec_ref[slot, 0, pl.ds(sin_at, size), lanes] if sin_at != cos_at else pc
        cross = spec_ref[slot, 1, pl.ds(cos_at, size), lanes]
        if mixed:
            cross = cross * sign
            return (
                pc * cos_rows + cross * pltpu.roll(sin_rows, HALF, 1),
                ps * sin_rows - cross * pltpu.roll(cos_rows, HALF, 1),
            )
        c1, c2, s1, s2 = cos_rows[:, :THIRD], cos_rows[:, THIRD:], sin_rows[:, :THIRD], sin_rows[:, THIRD:]
        return (
            jnp.concatenate([pc * c1 - cross * s2, pc * c2 + cross * s1], 1),
            jnp.concatenate([ps * s1 + cross * c2, ps * s2 - cross * c1], 1),
        )

    low = band(low_rows[:HALF], low_rows[HALF:], 0, HALF, HALF)
    high = band(high_rows[:THIRD], high_rows[THIRD:], THIRD, THIRD, THIRD)
    return jnp.concatenate(low, 0), jnp.concatenate(high, 0)


def window_products(windows, slots, r):
    count = len(windows)
    folded = [
        [butterfly(*(tile_of(block, i) for i in range(3))) for block in blocks] for blocks in windows
    ]
    small = [[right_small(plain, r.small_t) for plain, _, _ in blocks] for blocks in folded]
    large = [
        [right_large(jnp.concatenate([real, diff], 1), r.large_t) for _, real, diff in blocks]
        for blocks in folded
    ]

    def to_rows(windows):
        parts = [butterfly(*blocks) for blocks in windows]
        plain, real, diff = (jnp.concatenate([part[i] for part in parts], 1) for i in range(3))
        return left_small(plain, r.small), left_large(jnp.concatenate([real, diff], 0), r.large)

    def from_rows_of(bands, mixed):
        width = THIRD if mixed else 2 * THIRD
        done = []
        for num, slot in enumerate(slots):
            here = slice(num * width, (num + 1) * width)
            done.append(apply_spectrum(bands[0][:, here], bands[1][:, here], r.spec, slot, mixed))
        low_rows, high_rows = (jnp.concatenate([band[i] for band in done], 1) for i in range(2))
        plain = left_small(low_rows, r.small_t)
        both = left_large(high_rows, r.large_t)
        return unbutterfly(plain, both[:THIRD], both[THIRD:])

    small_bands, large_bands = to_rows(small), to_rows(large)
    small = from_rows_of(small_bands, True)
    large = from_rows_of(large_bands, False)
    plain = [[right_small(tile_of(block, num), r.small) for block in small] for num in range(count)]
    results = []
    for num in range(count):
        here = slice(2 * num * THIRD, 2 * (num + 1) * THIRD)
        both = [right_large(block[:, here], r.large) for block in large]
        results.append(
            [
                jnp.concatenate(unbutterfly(a, b[:, :THIRD], b[:, THIRD:]), 1)
                for a, b in zip(plain[num], both)
            ]
        )
    return results


def fold8(value):
    rows = value.reshape(value.shape[0] // 8, 8, value.shape[1]).sum(0)
    return sum(tile_of(rows, i) for i in range(value.shape[1] // THIRD))


def total(value):
    return jnp.sum(jnp.sum(value, 0, keepdims=True), 1, keepdims=True)


def lanes_of(shape, *values):
    lanes = lax.broadcasted_iota(jnp.int32, shape, 1)
    out = jnp.zeros(shape, F32)
    for num, value in enumerate(values):
        out = jnp.where(lanes == num, value, out)
    return out


def rows_at(num, count=1):
    return pl.ds(num * THIRD, count * THIRD)


def put(ref, here, tiles):
    for num, tile in enumerate(tiles):
        ref[here, pl.ds(num * THIRD, THIRD)] = tile


def own_sum(r, num):
    last = 2 * r.tiles
    terms = []
    if num <= 2:
        terms.append((r.top_sum, num))
    if 2 <= num <= last - 2:
        terms.append((r.mid_sum, num - 2))
    if num >= last - 2:
        terms.append((r.low_sum, num - last + 2))
    return terms


ENERGY, POWER, STEP, RATIO, BACK = 0, 1, 2, 2 + ITERS, 2 + 2 * ITERS
COEFS = (3 + 2 * ITERS, 8, THIRD)


def put_scalars(r):
    sums = jnp.sum(r.parts[...], 0, keepdims=True)
    energy, curve, cross = sums[:, 0:1], sums[:, 1:2], sums[:, 2:3]
    values = {ENERGY: energy, POWER: curve}
    last = r.stage - 1
    if last:
        ratio = energy / r.coef[ENERGY, 0:1, 0:1]
        values[POWER] = curve + ratio * (2.0 * cross + ratio * r.coef[POWER, 0:1, 0:1])
        values[RATIO + last] = ratio
        values[BACK] = ratio / r.coef[STEP + last - 1, 0:1, 0:1]
        for num in range(last):
            r.coef_new[STEP + num] = r.coef[STEP + num]
            r.coef_new[RATIO + num] = r.coef[RATIO + num]
    values[STEP + last] = energy / values[POWER]
    for num, value in values.items():
        r.coef_new[num] = jnp.broadcast_to(value, (8, THIRD))


def take_scalars(r, coef):
    r.steps = [coef[STEP + i, 0:1, :] for i in range(r.stage)]
    r.ratios = [coef[RATIO + i, 0:1, :] for i in range(1, r.stage)]
    r.back = coef[BACK, 0:1, :] if r.stage > 1 else None


def pick(odd, first, second):
    return jnp.where(odd, first, second), jnp.where(odd, second, first)


def from_columns(r, start, size):
    def part(whole, middle, ends):
        if whole is not None:
            return whole[pl.ds(start, size), :]
        count = middle.shape[0]
        if WIN <= start < WIN + count:
            return middle[pl.ds(start - WIN, size), :]
        return ends[pl.ds(start if start < WIN else start - count, size), :]

    names = r.__dict__
    return pick(
        r.edge[4] != 0,
        *(part(*(names.get(kind + pair) for kind in ("side", "middle", "ends"))) for pair in "zb"),
    )


def from_rows(r, side, here):
    return pick(r.edge[5] != 0, r.row_a[here, :], r.row_b[here, :])[side]


def send_columns(r, here, to_left, to_right):
    r.to_a[here, :], r.to_b[here, :] = pick(r.edge[4] != 0, to_left, to_right)


def strips_of(terms):
    low = lane_mask()
    pieces = [ref[rows_at(block), :] for ref, block in terms]
    block = sum(pieces[1:], pieces[0])
    return (
        jnp.where(low, tile_of(block, 0), tile_of(block, 2)),
        jnp.where(low, tile_of(block, 2), tile_of(block, 1)),
    )


def send_rows(r, above, below):
    odd = r.edge[5] != 0
    here = pl.ds(0, r.to_a.shape[0])
    pairs = [pick(odd, a, b) for a, b in zip(above, below)]
    put(r.to_a, here, [a for a, _ in pairs])
    put(r.to_b, here, [b for _, b in pairs])


def old_of(r, name):
    return [getattr(r, "res%d_%s" % (i, name)) for i in range(r.stage)]


def update(r, num, name, here, size, offset, spill, keep):
    low = lane_mask()
    sums = [ref[pl.ds(block * THIRD + offset, size), :] for ref, block in own_sum(r, num)]
    west, east = from_columns(r, num * THIRD + offset, size)
    add = [
        jnp.where(low, west, 0.0),
        jnp.where(low, 0.0, east),
        jnp.where(low, east, west),
    ]
    for block in sums + ([] if spill is None else [spill]):
        add = [a + tile_of(block, i) for i, a in enumerate(add)]
    olds = [ref[here, :] for ref in old_of(r, name)[-2:]]
    old = [tile_of(olds[-1], i) for i in range(3)]
    mapped = [a + b for a, b in zip(add, old)]
    mapped[2] = mapped[2] * jnp.where(low, r.edge[3].astype(F32), r.edge[2].astype(F32))
    if keep is not None:
        mapped = [a * keep for a in mapped]
    if r.stage > 1:
        mapped = [a + r.back * (tile_of(olds[0], i) - old[i]) for i, a in enumerate(mapped)]
    return [a - r.steps[-1] * b for a, b in zip(old, mapped)], mapped


def unpacked_sides(r, start, size):
    half = r.sidez.shape[0]
    low = lane_mask()
    out = []
    while size:
        upper = start < half
        count = min(size, half - start) if upper else size
        left, right = from_columns(r, start if upper else start - half, count)
        if upper:
            left = pltpu.roll(left, HALF, 1)
        else:
            right = pltpu.roll(right, HALF, 1)
        out.append(jnp.where(low, right, left))
        start, size = start + count, size - count
    return out[0] if len(out) == 1 else jnp.concatenate(out, 0)


def initial(r, start, size):
    here = pl.ds(start, size)
    block = r.observed[here, :]
    return [tile_of(block, 0), tile_of(block, 1), unpacked_sides(r, start, size)]


def pack_kernel(r):
    half = r.to_a.shape[0]
    low = lane_mask()
    first = [r.observed[pl.ds(start, half), pl.ds(0, THIRD)] for start in (0, half)]
    second = [r.observed[pl.ds(start, half), pl.ds(THIRD, THIRD)] for start in (0, half)]
    send_columns(
        r,
        pl.ds(0, half),
        jnp.where(low, first[0], pltpu.roll(first[1], HALF, 1)),
        jnp.where(low, pltpu.roll(second[0], HALF, 1), second[1]),
    )


def halo_kernel(r):
    send_rows(r, initial(r, 0, HALO), initial(r, r.observed.shape[0] - HALO, HALO))


def row_strip_kernel(r):
    low = lane_mask()
    blocks = 2 * r.tiles + 1
    size = r.to_a.shape[0]
    strips = []
    for side, ref in ((0, r.top_sum), (1, r.low_sum)):
        own = ref[pl.ds(side * (WIN - size), size), :]
        if r.narrow:
            west, east = from_columns(r, side * (blocks * HALO - size), size)
            if side:
                west = pltpu.roll(west, HALF, 1)
            else:
                east = pltpu.roll(east, HALF, 1)
            add = [jnp.where(low, west, 0.0), jnp.where(low, 0.0, east)]
        else:
            west, east = from_columns(r, side * (blocks * THIRD - size), size)
            add = [
                jnp.where(low, west, 0.0),
                jnp.where(low, 0.0, east),
                jnp.where(low, east, west),
            ]
        strips.append([tile_of(own, i) + a for i, a in enumerate(add)])
    send_rows(r, *strips)
    if r.narrow:
        put_scalars(r)


def middle_kernel(r):
    square = cross = jnp.zeros((8, THIRD), F32)
    blocks = 2 * r.tiles + 1
    if r.stage > 0:
        put_scalars(r)
        take_scalars(r, r.coef_new)
    for num in range(1, blocks - 1):
        here = rows_at(num - 1)
        if r.stage == 0:
            fresh = initial(r, num * THIRD - HALO, THIRD)
        else:
            fresh, mapped = update(r, num, "mid", here, THIRD, 0, None, None)
            cross += sum(fold8(a * b) for a, b in zip(fresh[:2], mapped))
        put(r.res_mid_new, here, fresh)
        square += sum(fold8(a * a) for a in fresh[:2])
    r.acc[0] = square
    r.acc[1] = cross
    r.acc[2] = jnp.zeros((8, THIRD), F32)
    inner = list(range(1, r.tiles - 1))
    some = r.occ[inner[0]]
    for slot in inner[1:]:
        some = some + r.occ[slot]

    @pl.when(some != 0)
    def _():
        windows = [
            [r.res_mid_new[rows_at(2 * slot + i - 1), :] for i in range(3)] for slot in inner
        ]
        results = window_products(windows, inner, r)
        curve = jnp.zeros((8, THIRD), F32)
        for num, (window, result) in enumerate(zip(windows, results)):
            curve += sum(fold8(a * b) for a, b in zip(window, result))
            first = result[0] if num == 0 else result[0] + results[num - 1][2]
            r.mid_sum_new[rows_at(2 * num), :] = first
            r.mid_sum_new[rows_at(2 * num + 1), :] = result[1]
        r.mid_sum_new[rows_at(2 * len(inner)), :] = results[-1][2]
        r.acc[2] = curve

    @pl.when(some == 0)
    def _():
        r.mid_sum_new[...] = jnp.zeros(r.mid_sum_new.shape, F32)

    if r.parted:
        for num in range(r.mid_a.shape[0] // THIRD):
            strips = strips_of([(r.mid_sum_new, num + 1)])
            r.mid_a[rows_at(num), :], r.mid_b[rows_at(num), :] = pick(r.edge[4] != 0, *strips)


def edge_kernel(r):
    square, cross = r.acc[0], r.acc[1]
    blocks = 2 * r.tiles + 1
    rows = 2 * r.tiles * THIRD
    if r.stage > 0:
        take_scalars(r, r.coef)
    for side in range(2):
        num = side * (blocks - 1)
        for offset in (0, HALO):
            here = pl.ds(side * THIRD + offset, HALO)
            inside = (offset > 0) == (side == 0)
            if r.stage == 0:
                if inside:
                    fresh = initial(r, side * (rows - HALO), HALO)
                else:
                    halo = from_rows(r, side, pl.ds(0, HALO))
                    fresh = [tile_of(halo, i) for i in range(3)]
            else:
                spill = from_rows(r, side, pl.ds(offset, HALO))
                keep = None if inside else r.edge[side].astype(F32)
                fresh, mapped = update(r, num, "edge", here, HALO, offset, spill, keep)
                if inside:
                    cross += sum(fold8(a * b) for a, b in zip(fresh[:2], mapped))
            put(r.res_edge_new, here, fresh)
            if inside:
                square += sum(fold8(a * a) for a in fresh[:2])
    slots = [0, r.tiles - 1]
    some = r.occ[slots[0]] + r.occ[slots[1]]

    @pl.when(some != 0)
    def _():
        far = blocks - 4
        windows = [
            [r.res_edge_new[rows_at(0), :]] + [r.res_mid_new[rows_at(i), :] for i in range(2)],
            [r.res_mid_new[rows_at(far + i), :] for i in range(2)] + [r.res_edge_new[rows_at(1), :]],
        ]
        results = window_products(windows, slots, r)
        curve = jnp.zeros((8, THIRD), F32)
        for window, result, ref in zip(windows, results, (r.top_sum_new, r.low_sum_new)):
            curve += sum(fold8(a * b) for a, b in zip(window, result))
            for num in range(3):
                ref[rows_at(num), :] = result[num]
        r.curve[...] = curve

    @pl.when(some == 0)
    def _():
        r.top_sum_new[...] = jnp.zeros((WIN, WIN), F32)
        r.low_sum_new[...] = jnp.zeros((WIN, WIN), F32)
        r.curve[...] = jnp.zeros((8, THIRD), F32)

    low = lane_mask()
    new = Refs(tiles=r.tiles, top_sum=r.top_sum_new, mid_sum=r.mid_sum_new, low_sum=r.low_sum_new)
    if r.narrow:
        half = blocks * HALO
        for start in range(0, half, HALO):
            pair = []
            for row in (start, start + half):
                terms = [
                    ref[pl.ds(block * THIRD + row % THIRD, HALO), pl.ds(2 * THIRD, THIRD)]
                    for ref, block in own_sum(new, row // THIRD)
                ]
                pair.append(sum(terms[1:], terms[0]))
            here = pl.ds(start, HALO)
            send_columns(
                r,
                here,
                jnp.where(low, pltpu.roll(pair[0], HALF, 1), pair[1]),
                jnp.where(low, pair[0], pltpu.roll(pair[1], HALF, 1)),
            )
    else:
        middle = blocks - 6
        for num in range(blocks):
            strips = strips_of(own_sum(new, num))
            if not r.parted:
                send_columns(r, rows_at(num), *strips)
            elif num < 3 or num >= 3 + middle:
                send_columns(r, rows_at(num if num < 3 else num - middle), *strips)
    gamma = total(square)
    curve = gamma + total(r.acc[2] + r.curve[...])
    r.part[...] = lanes_of(r.part.shape, gamma, curve, total(cross))


def last_rows(r, start, corrected, residual, at):
    blocks = 2 * r.tiles + 1
    half = blocks * HALO
    low = lane_mask()
    num, offset = start // THIRD, start % THIRD
    upper = start < half
    west, east = from_columns(r, start if upper else start - half, HALO)
    if upper:
        east = pltpu.roll(east, HALF, 1)
    else:
        west = pltpu.roll(west, HALF, 1)
    add = [jnp.where(low, west, 0.0), jnp.where(low, 0.0, east)]
    for ref, block in own_sum(r, num):
        there = pl.ds(block * THIRD + offset, HALO)
        add = [a + ref[there, pl.ds(i * THIRD, THIRD)] for i, a in enumerate(add)]
    if num == 0 or num == blocks - 1:
        spill = from_rows(r, 0 if num == 0 else 1, pl.ds(0, HALO))
        add = [a + tile_of(spill, i) for i, a in enumerate(add)]
        olds, here = old_of(r, "edge"), pl.ds((0 if num == 0 else THIRD) + offset, HALO)
    else:
        olds, here = old_of(r, "mid"), pl.ds(start - THIRD, HALO)
    for i, a in enumerate(add):
        lanes = pl.ds(i * THIRD, THIRD)
        past = [ref[here, lanes] for ref in olds]
        direct = past[0]
        moved = r.steps[0] * direct
        for old, ratio, step in zip(past[1:], r.ratios, r.steps[1:]):
            direct = old + ratio * direct
            moved = moved + step * direct
        mapped = a + past[-1] + r.back * (past[-2] - past[-1])
        corrected[pl.ds(at, HALO), lanes] = moved
        residual[pl.ds(at, HALO), lanes] = past[-1] - r.steps[-1] * mapped


def last_middle_kernel(r):
    take_scalars(r, r.coef)
    for start in range(THIRD, 2 * r.tiles * THIRD, HALO):
        last_rows(r, start, r.corrected, r.residual, start - HALO)


def last_edge_kernel(r):
    take_scalars(r, r.coef)
    rows = 2 * r.tiles * THIRD
    copies = []
    for side in range(2):
        last_rows(r, HALO + side * (rows - HALO), r.corrected_rows, r.residual_rows, side * HALO)
        here = pl.ds(side * HALO, HALO)
        there = pl.ds(side * (rows - HALO), HALO)
        for num, (source, target) in enumerate(
            ((r.corrected_rows, r.corrected), (r.residual_rows, r.residual))
        ):
            copy = pltpu.make_async_copy(source.at[here, :], target.at[there, :], r.sems.at[side, num])
            copy.start()
            copies.append(copy)
    for copy in copies:
        copy.wait()


class Refs:
    def __init__(self, **names):
        self.__dict__.update(names)


SCALARS = ("occ", "kid", "edge")
PARAMS = pltpu.CompilerParams(vmem_limit_bytes=16 * 1024 * 1024)


def run(body, ins, outs, scratch=None, onto=None, **static):
    scratch, onto = scratch or {}, onto or {}
    names = [*ins, *("old_" + name for name in onto), *outs, *onto, *scratch]

    def kernel(*refs):
        body(Refs(**static, **dict(zip(names, refs))))

    whole = pl.BlockSpec(memory_space=pltpu.VMEM)
    placed = [pl.BlockSpec(memory_space=pl.ANY)] * len(onto)
    shapes = [*outs.values(), *(value.shape for value in onto.values())]
    result = pl.pallas_call(
        kernel,
        name=body.__name__,
        out_shape=[jax.ShapeDtypeStruct(dims, F32) for dims in shapes],
        in_specs=[
            pl.BlockSpec(memory_space=pltpu.SMEM) if name in SCALARS else whole for name in ins
        ]
        + placed,
        out_specs=[whole] * len(outs) + placed,
        scratch_shapes=[
            pltpu.VMEM(dims, F32) if isinstance(dims, tuple) else dims for dims in scratch.values()
        ],
        input_output_aliases={len(ins) + i: len(outs) + i for i in range(len(onto))},
        compiler_params=PARAMS,
    )(*ins.values(), *onto.values())
    return dict(zip([*outs, *onto], result))


def own_part(table, tile_count):
    column = lax.dynamic_index_in_dim(table, lax.axis_index("col"), 1, keepdims=False)
    return lax.dynamic_slice_in_dim(column, lax.axis_index("row") * tile_count, tile_count)


def swap(value, axis, first):
    pairs = [(i, i + 1) for i in range(first, lax.axis_size(axis) - 1, 2)]
    return lax.ppermute(value, axis, pairs + [(b, a) for a, b in pairs])


def shards(observed, kernels, occupied, kernel_index):
    rows, cols = observed.shape
    tiles = rows // TILE
    half, mid, ext = rows // 2, rows - 2 * HALO, rows + 2 * HALO
    n_row, n_col = lax.axis_size("row"), lax.axis_size("col")
    devices = n_row * n_col
    my_row, my_col = lax.axis_index("row"), lax.axis_index("col")
    occ = own_part(occupied, tiles)
    edge = jnp.stack(
        [my_row > 0, my_row < n_row - 1, my_col > 0, my_col < n_col - 1, my_col % 2 == 1, my_row % 2 == 1]
    ).astype(jnp.int32)
    host = {name: jnp.asarray(table) for name, table in tables().items()}
    sent = run(pack_kernel, dict(edge=edge, observed=observed), dict(to_a=(half, THIRD), to_b=(half, THIRD)))
    sideb = swap(sent["to_b"], "col", 1)
    sidez = swap(sent["to_a"], "col", 0)
    spec = run(
        spectra_kernel,
        dict(
            kid=own_part(kernel_index, tiles),
            occ=occ,
            kernels=jnp.pad(kernels, ((0, 0), (0, THIRD - KW), (0, THIRD - KW))),
            w_left=host["w_left"],
            w_right=host["w_right"],
        ),
        dict(spec=(tiles, 2, SLOTS, SLOTS)),
    )["spec"]
    sideb, sidez, spec = lax.optimization_barrier((sideb, sidez, spec))
    sides = dict(edge=edge, sideb=sideb, sidez=sidez)
    sent = run(halo_kernel, dict(observed=observed, **sides), dict(to_a=(HALO, WIN), to_b=(HALO, WIN)))
    sides, sent = lax.optimization_barrier((sides, sent))
    row_b, row_a = swap(sent["to_b"], "row", 1), swap(sent["to_a"], "row", 0)
    fixed = dict(occ=occ, spec=spec, **{name: host[name] for name in NAMES})
    state = {}
    for stage in range(ITERS):
        narrow = stage == ITERS - 1
        parted = 0 < stage < ITERS - 1
        moving = dict(sides)
        if stage == 0:
            moving["observed"] = observed
        known = dict(parts=parts) if stage else {}
        if stage > 1:
            known["coef"] = coef

        def old(where, *sums):
            names = ["res%d_%s" % (i, where) for i in range(stage)]
            return {name: state[name] for name in names + list(sums) if stage}

        middle = run(
            middle_kernel,
            {**fixed, **moving, **known, **old("mid", "top_sum", "mid_sum", "low_sum")},
            {
                "res_mid_new": (mid, WIN),
                "mid_sum_new": (mid - TILE, WIN),
                "acc": (3, 8, THIRD),
                **(dict(coef_new=COEFS) if stage else {}),
                **({name: (ext - 2 * WIN, THIRD) for name in ("mid_a", "mid_b") if parted}),
            },
            stage=stage,
            tiles=tiles,
            parted=parted,
        )
        if parted:
            middleb, middlez = swap(middle["mid_b"], "col", 1), swap(middle["mid_a"], "col", 0)
        outs = {"res_edge_new": (TILE, WIN), "top_sum_new": (WIN, WIN), "low_sum_new": (WIN, WIN)}
        outs["to_a"] = outs["to_b"] = (ext // 2 if narrow else 2 * WIN if parted else ext, THIRD)
        outs["part"] = (devices, THIRD)
        edges = run(
            edge_kernel,
            {
                **fixed,
                **moving,
                **(dict(coef=middle["coef_new"]) if stage else {}),
                **old("edge", "top_sum", "low_sum"),
                "row_b": row_b,
                "row_a": row_a,
                **{name: middle[name] for name in ("res_mid_new", "mid_sum_new", "acc")},
            },
            outs,
            dict(curve=(8, THIRD)),
            stage=stage,
            tiles=tiles,
            parted=parted,
            narrow=narrow,
        )
        state["res%d_mid" % stage] = middle["res_mid_new"]
        state["res%d_edge" % stage] = edges["res_edge_new"]
        state["mid_sum"] = middle["mid_sum_new"]
        state["top_sum"] = edges["top_sum_new"]
        state["low_sum"] = edges["low_sum_new"]
        part, to_a, to_b = edges["part"], edges["to_a"], edges["to_b"]
        if parted:
            middleb, middlez, to_b, to_a, part = lax.optimization_barrier((middleb, middlez, to_b, to_a, part))
        keys = ("endsb", "endsz") if parted else ("sideb", "sidez")
        sides = dict(zip(keys, (swap(to_b, "col", 1), swap(to_a, "col", 0))))
        if parted:
            sides.update(middleb=middleb, middlez=middlez)
        parts = lax.all_to_all(part, ("row", "col"), 0, 0, tiled=True)
        sides, parts = lax.optimization_barrier((sides, parts))
        sides["edge"] = edge
        strip = (HALO, TILE) if narrow else (THIRD, WIN)
        coef = middle.get("coef_new")
        sent = run(
            row_strip_kernel,
            dict(
                **(dict(parts=parts, coef=coef) if narrow else {}),
                top_sum=state["top_sum"],
                low_sum=state["low_sum"],
                **sides,
            ),
            dict(to_a=strip, to_b=strip, **(dict(coef_new=COEFS) if narrow else {})),
            stage=stage + 1,
            tiles=tiles,
            narrow=narrow,
        )
        row_b, row_a = swap(sent["to_b"], "row", 1), swap(sent["to_a"], "row", 0)

    def olds(where):
        return {name: state[name] for name in ["res%d_%s" % (i, where) for i in range(ITERS)]}

    coef = sent["coef_new"]
    ends = dict(top_sum=state["top_sum"], low_sum=state["low_sum"])
    out = run(
        last_middle_kernel,
        dict(coef=coef, mid_sum=state["mid_sum"], **ends, **sides, **olds("mid")),
        dict(corrected=(rows, cols), residual=(rows, cols)),
        stage=ITERS,
        tiles=tiles,
    )
    out = run(
        last_edge_kernel,
        dict(coef=coef, row_b=row_b, row_a=row_a, **ends, **sides, **olds("edge")),
        {},
        dict(
            corrected_rows=(2 * HALO, cols),
            residual_rows=(2 * HALO, cols),
            sems=pltpu.SemaphoreType.DMA((2, 2)),
        ),
        out,
        stage=ITERS,
        tiles=tiles,
    )
    return out["corrected"], out["residual"]


def solution(mesh):
    placed = (P("row", "col"), P(), P(), P())
    return jax.shard_map(
        shards,
        mesh=mesh,
        in_specs=placed,
        out_specs=(P("row", "col"), P("row", "col")),
        check_vma=False,
    )
```

```python
import functools
import math

import jax
import jax.numpy as jnp
import numpy as np
from jax import lax
from jax.experimental import pallas as pl
from jax.experimental.pallas import tpu as pltpu
from jax.sharding import PartitionSpec as P

TILE = 256
HALO = 64
KW = 65
ITERS = 3
WIN = TILE + 2 * HALO
THIRD = WIN // 3
HALF = THIRD // 2
SLOTS = 2 * THIRD
BF = jnp.bfloat16
F32 = jnp.float32


def hi_lo(table):
    high = table.astype(np.float32).astype(jnp.bfloat16)
    low = (table - high.astype(np.float64)).astype(np.float32).astype(jnp.bfloat16)
    return high, low


@functools.cache
def tables():
    spots = np.arange(THIRD)
    low_freq = 3 * np.arange(HALF)
    full = math.sqrt(2.0 / WIN)
    cos_part = np.cos(2 * np.pi * (low_freq[:, None] * spots % WIN) / WIN) * full
    sin_part = np.sin(2 * np.pi * (low_freq[:, None] * spots % WIN) / WIN) * full
    cos_part[0] = math.sqrt(1.0 / WIN)
    sin_part[0] = np.where(spots % 2 == 0, 1.0, -1.0) * math.sqrt(1.0 / WIN)
    small = np.concatenate([cos_part, sin_part])
    angle = 2 * np.pi * ((3 * spots[:, None] + 1) * spots % WIN) / WIN
    root = math.sqrt(3.0) / 2
    large = full * np.block(
        [[np.cos(angle), -root * np.sin(angle)], [np.sin(angle), root * np.cos(angle)]]
    )
    freqs = np.concatenate([low_freq, low_freq, 3 * spots + 1])
    freqs[HALF] = WIN // 2
    taps = np.arange(THIRD)
    turn = 2 * np.pi * (freqs[:, None] * taps % WIN) / WIN
    keep = (taps < KW)[None, :]
    sines = np.sin(turn)
    sines[0] = 0.0
    sines[HALF] = 0.0
    waves = np.concatenate([np.cos(turn) * keep, sines * keep])

    sh, sl = hi_lo(small)
    gh, gl = hi_lo(large)
    wh, wl = hi_lo(waves)
    return dict(
        large=np.concatenate([gh, gl]),
        large_t=np.concatenate([gh.T, gl.T]),
        small=np.concatenate([sh, sl]),
        small_t=np.concatenate([sh.T, sl.T]),
        w_left=np.concatenate([wh, wl, wh], 1),
        w_right=np.concatenate([wh.T, wl.T, wh.T], 0),
    )


NAMES = ("large", "large_t", "small", "small_t")


def split(value):
    high = value.astype(BF)
    return high, (value - high.astype(F32)).astype(BF)


def dot(left, right):
    return jnp.dot(left, right, preferred_element_type=F32)


def right_large(value, table):
    high, low = split(value)
    return dot(
        jnp.concatenate([high, high, low], 1),
        jnp.concatenate([table[...], table[:SLOTS]], 0),
    )


def right_small(value, table):
    high, low = split(value)
    coarse, fine = table[:THIRD], table[THIRD:]
    both = dot(
        jnp.concatenate([high, low], 1),
        jnp.concatenate(
            [
                jnp.concatenate([coarse, fine], 1),
                jnp.concatenate([coarse, jnp.zeros_like(fine)], 1),
            ],
            0,
        ),
    )
    return both[:, :THIRD] + both[:, THIRD:]


def left_large(value, table):
    high, low = split(value)
    both = dot(table[...], high)
    return both[:SLOTS] + both[SLOTS:] + dot(table[:SLOTS], low)


def left_small(value, table):
    high, low = split(value)
    coarse, fine = table[:THIRD], table[THIRD:]
    both = dot(
        jnp.concatenate(
            [
                jnp.concatenate([coarse, coarse], 1),
                jnp.concatenate([fine, jnp.zeros_like(fine)], 1),
            ],
            0,
        ),
        jnp.concatenate([high, low], 0),
    )
    return both[:THIRD] + both[THIRD:]


def butterfly(first, second, third):
    total = second + third
    return first + total, first - 0.5 * total, second - third


def unbutterfly(plain, real, diff):
    base = plain - 0.5 * real
    return plain + real, base + diff, base - diff


def spectra_kernel(r):
    def body(slot, carry):
        @pl.when(r.occ[slot] != 0)
        def _():
            high, low = split(r.kernels[r.kid[slot]])
            half = dot(r.w_left[...], jnp.concatenate([high, high, low], 0))
            high, low = split(half)
            quads = dot(jnp.concatenate([high, high, low], 1), r.w_right[...])
            cc = quads[:SLOTS, :SLOTS]
            cs = quads[:SLOTS, SLOTS:]
            sc = quads[SLOTS:, :SLOTS]
            ss = quads[SLOTS:, SLOTS:]
            r.spec[slot, 0] = cc * cc + ss * ss + (sc * sc + cs * cs)
            r.spec[slot, 1] = 2.0 * (sc * cs - cc * ss)

        @pl.when(r.occ[slot] == 0)
        def _():
            r.spec[slot] = jnp.zeros((2, SLOTS, SLOTS), F32)

        return carry

    lax.fori_loop(0, r.spec.shape[0], body, 0)


def tile_of(block, num):
    return block[:, num * THIRD : (num + 1) * THIRD]


def lane_mask():
    return lax.broadcasted_iota(jnp.int32, (1, THIRD), 1) < HALF


def apply_spectrum(low_rows, high_rows, spec_ref, slot, mixed):
    lanes = pl.ds(0 if mixed else THIRD, THIRD)
    sign = jnp.where(lane_mask(), -1.0, 1.0).astype(F32)

    def band(cos_rows, sin_rows, cos_at, sin_at, size):
        pc = spec_ref[slot, 0, pl.ds(cos_at, size), lanes]
        ps = spec_ref[slot, 0, pl.ds(sin_at, size), lanes] if sin_at != cos_at else pc
        cross = spec_ref[slot, 1, pl.ds(cos_at, size), lanes]
        if mixed:
            cross = cross * sign
            return (
                pc * cos_rows + cross * pltpu.roll(sin_rows, HALF, 1),
                ps * sin_rows - cross * pltpu.roll(cos_rows, HALF, 1),
            )
        c1, c2, s1, s2 = cos_rows[:, :THIRD], cos_rows[:, THIRD:], sin_rows[:, :THIRD], sin_rows[:, THIRD:]
        return (
            jnp.concatenate([pc * c1 - cross * s2, pc * c2 + cross * s1], 1),
            jnp.concatenate([ps * s1 + cross * c2, ps * s2 - cross * c1], 1),
        )

    low = band(low_rows[:HALF], low_rows[HALF:], 0, HALF, HALF)
    high = band(high_rows[:THIRD], high_rows[THIRD:], THIRD, THIRD, THIRD)
    return jnp.concatenate(low, 0), jnp.concatenate(high, 0)


def window_products(windows, slots, r):
    count = len(windows)
    folded = [
        [butterfly(*(tile_of(block, i) for i in range(3))) for block in blocks] for blocks in windows
    ]
    small = [[right_small(plain, r.small_t) for plain, _, _ in blocks] for blocks in folded]
    large = [
        [right_large(jnp.concatenate([real, diff], 1), r.large_t) for _, real, diff in blocks]
        for blocks in folded
    ]

    def to_rows(windows):
        parts = [butterfly(*blocks) for blocks in windows]
        plain, real, diff = (jnp.concatenate([part[i] for part in parts], 1) for i in range(3))
        return left_small(plain, r.small), left_large(jnp.concatenate([real, diff], 0), r.large)

    def from_rows_of(bands, mixed):
        width = THIRD if mixed else 2 * THIRD
        done = []
        for num, slot in enumerate(slots):
            here = slice(num * width, (num + 1) * width)
            done.append(apply_spectrum(bands[0][:, here], bands[1][:, here], r.spec, slot, mixed))
        low_rows, high_rows = (jnp.concatenate([band[i] for band in done], 1) for i in range(2))
        plain = left_small(low_rows, r.small_t)
        both = left_large(high_rows, r.large_t)
        return unbutterfly(plain, both[:THIRD], both[THIRD:])

    small_bands, large_bands = to_rows(small), to_rows(large)
    small = from_rows_of(small_bands, True)
    large = from_rows_of(large_bands, False)
    plain = [[right_small(tile_of(block, num), r.small) for block in small] for num in range(count)]
    results = []
    for num in range(count):
        here = slice(2 * num * THIRD, 2 * (num + 1) * THIRD)
        both = [right_large(block[:, here], r.large) for block in large]
        results.append(
            [
                jnp.concatenate(unbutterfly(a, b[:, :THIRD], b[:, THIRD:]), 1)
                for a, b in zip(plain[num], both)
            ]
        )
    return results


def fold8(value):
    rows = value.reshape(value.shape[0] // 8, 8, value.shape[1]).sum(0)
    return sum(tile_of(rows, i) for i in range(value.shape[1] // THIRD))


def total(value):
    return jnp.sum(jnp.sum(value, 0, keepdims=True), 1, keepdims=True)


def lanes_of(shape, *values):
    lanes = lax.broadcasted_iota(jnp.int32, shape, 1)
    out = jnp.zeros(shape, F32)
    for num, value in enumerate(values):
        out = jnp.where(lanes == num, value, out)
    return out


def rows_at(num, count=1):
    return pl.ds(num * THIRD, count * THIRD)


def put(ref, here, tiles):
    for num, tile in enumerate(tiles):
        ref[here, pl.ds(num * THIRD, THIRD)] = tile


def own_sum(r, num):
    last = 2 * r.tiles
    terms = []
    if num <= 2:
        terms.append((r.top_sum, num))
    if 2 <= num <= last - 2:
        terms.append((r.mid_sum, num - 2))
    if num >= last - 2:
        terms.append((r.low_sum, num - last + 2))
    return terms


ENERGY, POWER, STEP, RATIO, BACK = 0, 1, 2, 2 + ITERS, 2 + 2 * ITERS
COEFS = (3 + 2 * ITERS, 8, THIRD)


def put_scalars(r):
    sums = jnp.sum(r.parts[...], 0, keepdims=True)
    energy, curve, cross = sums[:, 0:1], sums[:, 1:2], sums[:, 2:3]
    values = {ENERGY: energy, POWER: curve}
    last = r.stage - 1
    if last:
        ratio = energy / r.coef[ENERGY, 0:1, 0:1]
        values[POWER] = curve + ratio * (2.0 * cross + ratio * r.coef[POWER, 0:1, 0:1])
        values[RATIO + last] = ratio
        values[BACK] = ratio / r.coef[STEP + last - 1, 0:1, 0:1]
        for num in range(last):
            r.coef_new[STEP + num] = r.coef[STEP + num]
            r.coef_new[RATIO + num] = r.coef[RATIO + num]
    values[STEP + last] = energy / values[POWER]
    for num, value in values.items():
        r.coef_new[num] = jnp.broadcast_to(value, (8, THIRD))


def take_scalars(r, coef):
    r.steps = [coef[STEP + i, 0:1, :] for i in range(r.stage)]
    r.ratios = [coef[RATIO + i, 0:1, :] for i in range(1, r.stage)]
    r.back = coef[BACK, 0:1, :] if r.stage > 1 else None


def pick(odd, first, second):
    return jnp.where(odd, first, second), jnp.where(odd, second, first)


def from_columns(r, start, size):
    def part(whole, middle, ends):
        if whole is not None:
            return whole[pl.ds(start, size), :]
        count = middle.shape[0]
        if WIN <= start < WIN + count:
            return middle[pl.ds(start - WIN, size), :]
        return ends[pl.ds(start if start < WIN else start - count, size), :]

    names = r.__dict__
    return pick(
        r.edge[4] != 0,
        *(part(*(names.get(kind + pair) for kind in ("side", "middle", "ends"))) for pair in "zb"),
    )


def from_rows(r, side, here):
    return pick(r.edge[5] != 0, r.row_a[here, :], r.row_b[here, :])[side]


def send_columns(r, here, to_left, to_right):
    r.to_a[here, :], r.to_b[here, :] = pick(r.edge[4] != 0, to_left, to_right)


def strips_of(terms):
    low = lane_mask()
    pieces = [ref[rows_at(block), :] for ref, block in terms]
    block = sum(pieces[1:], pieces[0])
    return (
        jnp.where(low, tile_of(block, 0), tile_of(block, 2)),
        jnp.where(low, tile_of(block, 2), tile_of(block, 1)),
    )


def send_rows(r, above, below):
    odd = r.edge[5] != 0
    here = pl.ds(0, r.to_a.shape[0])
    pairs = [pick(odd, a, b) for a, b in zip(above, below)]
    put(r.to_a, here, [a for a, _ in pairs])
    put(r.to_b, here, [b for _, b in pairs])


def old_of(r, name):
    return [getattr(r, "res%d_%s" % (i, name)) for i in range(r.stage)]


def update(r, num, name, here, size, offset, spill, keep):
    low = lane_mask()
    sums = [ref[pl.ds(block * THIRD + offset, size), :] for ref, block in own_sum(r, num)]
    west, east = from_columns(r, num * THIRD + offset, size)
    add = [
        jnp.where(low, west, 0.0),
        jnp.where(low, 0.0, east),
        jnp.where(low, east, west),
    ]
    for block in sums + ([] if spill is None else [spill]):
        add = [a + tile_of(block, i) for i, a in enumerate(add)]
    olds = [ref[here, :] for ref in old_of(r, name)[-2:]]
    old = [tile_of(olds[-1], i) for i in range(3)]
    mapped = [a + b for a, b in zip(add, old)]
    mapped[2] = mapped[2] * jnp.where(low, r.edge[3].astype(F32), r.edge[2].astype(F32))
    if keep is not None:
        mapped = [a * keep for a in mapped]
    if r.stage > 1:
        mapped = [a + r.back * (tile_of(olds[0], i) - old[i]) for i, a in enumerate(mapped)]
    return [a - r.steps[-1] * b for a, b in zip(old, mapped)], mapped


def unpacked_sides(r, start, size):
    half = r.sidez.shape[0]
    low = lane_mask()
    out = []
    while size:
        upper = start < half
        count = min(size, half - start) if upper else size
        left, right = from_columns(r, start if upper else start - half, count)
        if upper:
            left = pltpu.roll(left, HALF, 1)
        else:
            right = pltpu.roll(right, HALF, 1)
        out.append(jnp.where(low, right, left))
        start, size = start + count, size - count
    return out[0] if len(out) == 1 else jnp.concatenate(out, 0)


def initial(r, start, size):
    here = pl.ds(start, size)
    block = r.observed[here, :]
    return [tile_of(block, 0), tile_of(block, 1), unpacked_sides(r, start, size)]


def pack_kernel(r):
    half = r.to_a.shape[0]
    low = lane_mask()
    first = [r.observed[pl.ds(start, half), pl.ds(0, THIRD)] for start in (0, half)]
    second = [r.observed[pl.ds(start, half), pl.ds(THIRD, THIRD)] for start in (0, half)]
    send_columns(
        r,
        pl.ds(0, half),
        jnp.where(low, first[0], pltpu.roll(first[1], HALF, 1)),
        jnp.where(low, pltpu.roll(second[0], HALF, 1), second[1]),
    )


def halo_kernel(r):
    send_rows(r, initial(r, 0, HALO), initial(r, r.observed.shape[0] - HALO, HALO))


def row_strip_kernel(r):
    low = lane_mask()
    blocks = 2 * r.tiles + 1
    size = r.to_a.shape[0]
    strips = []
    for side, ref in ((0, r.top_sum), (1, r.low_sum)):
        own = ref[pl.ds(side * (WIN - size), size), :]
        if r.narrow:
            west, east = from_columns(r, side * (blocks * HALO - size), size)
            if side:
                west = pltpu.roll(west, HALF, 1)
            else:
                east = pltpu.roll(east, HALF, 1)
            add = [jnp.where(low, west, 0.0), jnp.where(low, 0.0, east)]
        else:
            west, east = from_columns(r, side * (blocks * THIRD - size), size)
            add = [
                jnp.where(low, west, 0.0),
                jnp.where(low, 0.0, east),
                jnp.where(low, east, west),
            ]
        strips.append([tile_of(own, i) + a for i, a in enumerate(add)])
    send_rows(r, *strips)
    if r.narrow:
        put_scalars(r)


def middle_kernel(r):
    square = cross = jnp.zeros((8, THIRD), F32)
    blocks = 2 * r.tiles + 1
    if r.stage > 0:
        put_scalars(r)
        take_scalars(r, r.coef_new)
    for num in range(1, blocks - 1):
        here = rows_at(num - 1)
        if r.stage == 0:
            fresh = initial(r, num * THIRD - HALO, THIRD)
        else:
            fresh, mapped = update(r, num, "mid", here, THIRD, 0, None, None)
            cross += sum(fold8(a * b) for a, b in zip(fresh[:2], mapped))
        put(r.res_mid_new, here, fresh)
        square += sum(fold8(a * a) for a in fresh[:2])
    r.acc[0] = square
    r.acc[1] = cross
    r.acc[2] = jnp.zeros((8, THIRD), F32)
    inner = list(range(1, r.tiles - 1))
    some = r.occ[inner[0]]
    for slot in inner[1:]:
        some = some + r.occ[slot]

    @pl.when(some != 0)
    def _():
        windows = [
            [r.res_mid_new[rows_at(2 * slot + i - 1), :] for i in range(3)] for slot in inner
        ]
        results = window_products(windows, inner, r)
        curve = jnp.zeros((8, THIRD), F32)
        for num, (window, result) in enumerate(zip(windows, results)):
            curve += sum(fold8(a * b) for a, b in zip(window, result))
            first = result[0] if num == 0 else result[0] + results[num - 1][2]
            r.mid_sum_new[rows_at(2 * num), :] = first
            r.mid_sum_new[rows_at(2 * num + 1), :] = result[1]
        r.mid_sum_new[rows_at(2 * len(inner)), :] = results[-1][2]
        r.acc[2] = curve

    @pl.when(some == 0)
    def _():
        r.mid_sum_new[...] = jnp.zeros(r.mid_sum_new.shape, F32)

    if r.parted:
        for num in range(r.mid_a.shape[0] // THIRD):
            strips = strips_of([(r.mid_sum_new, num + 1)])
            r.mid_a[rows_at(num), :], r.mid_b[rows_at(num), :] = pick(r.edge[4] != 0, *strips)


def edge_kernel(r):
    square, cross = r.acc[0], r.acc[1]
    blocks = 2 * r.tiles + 1
    rows = 2 * r.tiles * THIRD
    if r.stage > 0:
        take_scalars(r, r.coef)
    for side in range(2):
        num = side * (blocks - 1)
        for offset in (0, HALO):
            here = pl.ds(side * THIRD + offset, HALO)
            inside = (offset > 0) == (side == 0)
            if r.stage == 0:
                if inside:
                    fresh = initial(r, side * (rows - HALO), HALO)
                else:
                    halo = from_rows(r, side, pl.ds(0, HALO))
                    fresh = [tile_of(halo, i) for i in range(3)]
            else:
                spill = from_rows(r, side, pl.ds(offset, HALO))
                keep = None if inside else r.edge[side].astype(F32)
                fresh, mapped = update(r, num, "edge", here, HALO, offset, spill, keep)
                if inside:
                    cross += sum(fold8(a * b) for a, b in zip(fresh[:2], mapped))
            put(r.res_edge_new, here, fresh)
            if inside:
                square += sum(fold8(a * a) for a in fresh[:2])
    slots = [0, r.tiles - 1]
    some = r.occ[slots[0]] + r.occ[slots[1]]

    @pl.when(some != 0)
    def _():
        far = blocks - 4
        windows = [
            [r.res_edge_new[rows_at(0), :]] + [r.res_mid_new[rows_at(i), :] for i in range(2)],
            [r.res_mid_new[rows_at(far + i), :] for i in range(2)] + [r.res_edge_new[rows_at(1), :]],
        ]
        results = window_products(windows, slots, r)
        curve = jnp.zeros((8, THIRD), F32)
        for window, result, ref in zip(windows, results, (r.top_sum_new, r.low_sum_new)):
            curve += sum(fold8(a * b) for a, b in zip(window, result))
            for num in range(3):
                ref[rows_at(num), :] = result[num]
        r.curve[...] = curve

    @pl.when(some == 0)
    def _():
        r.top_sum_new[...] = jnp.zeros((WIN, WIN), F32)
        r.low_sum_new[...] = jnp.zeros((WIN, WIN), F32)
        r.curve[...] = jnp.zeros((8, THIRD), F32)

    gamma = total(square)
    curve = gamma + total(r.acc[2] + r.curve[...])
    r.part[...] = lanes_of(r.part.shape, gamma, curve, total(cross))

    low = lane_mask()
    new = Refs(tiles=r.tiles, top_sum=r.top_sum_new, mid_sum=r.mid_sum_new, low_sum=r.low_sum_new)
    if r.narrow:
        half = blocks * HALO
        for start in range(0, half, HALO):
            pair = []
            for row in (start, start + half):
                terms = [
                    ref[pl.ds(block * THIRD + row % THIRD, HALO), pl.ds(2 * THIRD, THIRD)]
                    for ref, block in own_sum(new, row // THIRD)
                ]
                pair.append(sum(terms[1:], terms[0]))
            here = pl.ds(start, HALO)
            send_columns(
                r,
                here,
                jnp.where(low, pltpu.roll(pair[0], HALF, 1), pair[1]),
                jnp.where(low, pair[0], pltpu.roll(pair[1], HALF, 1)),
            )
    else:
        middle = blocks - 6
        for num in range(blocks):
            strips = strips_of(own_sum(new, num))
            if not r.parted:
                send_columns(r, rows_at(num), *strips)
            elif num < 3 or num >= 3 + middle:
                send_columns(r, rows_at(num if num < 3 else num - middle), *strips)


def last_rows(r, start, corrected, residual, at):
    blocks = 2 * r.tiles + 1
    half = blocks * HALO
    low = lane_mask()
    num, offset = start // THIRD, start % THIRD
    upper = start < half
    west, east = from_columns(r, start if upper else start - half, HALO)
    if upper:
        east = pltpu.roll(east, HALF, 1)
    else:
        west = pltpu.roll(west, HALF, 1)
    add = [jnp.where(low, west, 0.0), jnp.where(low, 0.0, east)]
    for ref, block in own_sum(r, num):
        there = pl.ds(block * THIRD + offset, HALO)
        add = [a + ref[there, pl.ds(i * THIRD, THIRD)] for i, a in enumerate(add)]
    if num == 0 or num == blocks - 1:
        spill = from_rows(r, 0 if num == 0 else 1, pl.ds(0, HALO))
        add = [a + tile_of(spill, i) for i, a in enumerate(add)]
        olds, here = old_of(r, "edge"), pl.ds((0 if num == 0 else THIRD) + offset, HALO)
    else:
        olds, here = old_of(r, "mid"), pl.ds(start - THIRD, HALO)
    for i, a in enumerate(add):
        lanes = pl.ds(i * THIRD, THIRD)
        past = [ref[here, lanes] for ref in olds]
        direct = past[0]
        moved = r.steps[0] * direct
        for old, ratio, step in zip(past[1:], r.ratios, r.steps[1:]):
            direct = old + ratio * direct
            moved = moved + step * direct
        mapped = a + past[-1] + r.back * (past[-2] - past[-1])
        corrected[pl.ds(at, HALO), lanes] = moved
        residual[pl.ds(at, HALO), lanes] = past[-1] - r.steps[-1] * mapped


def last_middle_kernel(r):
    take_scalars(r, r.coef)
    for start in range(THIRD, 2 * r.tiles * THIRD, HALO):
        last_rows(r, start, r.corrected, r.residual, start - HALO)


def last_edge_kernel(r):
    take_scalars(r, r.coef)
    rows = 2 * r.tiles * THIRD
    copies = []
    for side in range(2):
        last_rows(r, HALO + side * (rows - HALO), r.corrected_rows, r.residual_rows, side * HALO)
        here = pl.ds(side * HALO, HALO)
        there = pl.ds(side * (rows - HALO), HALO)
        for num, (source, target) in enumerate(
            ((r.corrected_rows, r.corrected), (r.residual_rows, r.residual))
        ):
            copy = pltpu.make_async_copy(source.at[here, :], target.at[there, :], r.sems.at[side, num])
            copy.start()
            copies.append(copy)
    for copy in copies:
        copy.wait()


class Refs:
    def __init__(self, **names):
        self.__dict__.update(names)


SCALARS = ("occ", "kid", "edge")
PARAMS = pltpu.CompilerParams(vmem_limit_bytes=16 * 1024 * 1024)


def run(body, ins, outs, scratch=None, onto=None, **static):
    scratch, onto = scratch or {}, onto or {}
    names = [*ins, *("old_" + name for name in onto), *outs, *onto, *scratch]

    def kernel(*refs):
        body(Refs(**static, **dict(zip(names, refs))))

    whole = pl.BlockSpec(memory_space=pltpu.VMEM)
    placed = [pl.BlockSpec(memory_space=pl.ANY)] * len(onto)
    shapes = [*outs.values(), *(value.shape for value in onto.values())]
    result = pl.pallas_call(
        kernel,
        name=body.__name__,
        out_shape=[jax.ShapeDtypeStruct(dims, F32) for dims in shapes],
        in_specs=[
            pl.BlockSpec(memory_space=pltpu.SMEM) if name in SCALARS else whole for name in ins
        ]
        + placed,
        out_specs=[whole] * len(outs) + placed,
        scratch_shapes=[
            pltpu.VMEM(dims, F32) if isinstance(dims, tuple) else dims for dims in scratch.values()
        ],
        input_output_aliases={len(ins) + i: len(outs) + i for i in range(len(onto))},
        compiler_params=PARAMS,
    )(*ins.values(), *onto.values())
    return dict(zip([*outs, *onto], result))


def own_part(table, tile_count):
    column = lax.dynamic_index_in_dim(table, lax.axis_index("col"), 1, keepdims=False)
    return lax.dynamic_slice_in_dim(column, lax.axis_index("row") * tile_count, tile_count)


def swap(value, axis, first):
    pairs = [(i, i + 1) for i in range(first, lax.axis_size(axis) - 1, 2)]
    return lax.ppermute(value, axis, pairs + [(b, a) for a, b in pairs])


def shards(observed, kernels, occupied, kernel_index):
    rows, cols = observed.shape
    tiles = rows // TILE
    half, mid, ext = rows // 2, rows - 2 * HALO, rows + 2 * HALO
    n_row, n_col = lax.axis_size("row"), lax.axis_size("col")
    devices = n_row * n_col
    my_row, my_col = lax.axis_index("row"), lax.axis_index("col")
    occ = own_part(occupied, tiles)
    edge = jnp.stack(
        [my_row > 0, my_row < n_row - 1, my_col > 0, my_col < n_col - 1, my_col % 2 == 1, my_row % 2 == 1]
    ).astype(jnp.int32)
    host = {name: jnp.asarray(table) for name, table in tables().items()}
    sent = run(pack_kernel, dict(edge=edge, observed=observed), dict(to_a=(half, THIRD), to_b=(half, THIRD)))
    sideb = swap(sent["to_b"], "col", 1)
    sidez = swap(sent["to_a"], "col", 0)
    spec = run(
        spectra_kernel,
        dict(
            kid=own_part(kernel_index, tiles),
            occ=occ,
            kernels=jnp.pad(kernels, ((0, 0), (0, THIRD - KW), (0, THIRD - KW))),
            w_left=host["w_left"],
            w_right=host["w_right"],
        ),
        dict(spec=(tiles, 2, SLOTS, SLOTS)),
    )["spec"]
    sideb, sidez, spec = lax.optimization_barrier((sideb, sidez, spec))
    sides = dict(edge=edge, sideb=sideb, sidez=sidez)
    sent = run(halo_kernel, dict(observed=observed, **sides), dict(to_a=(HALO, WIN), to_b=(HALO, WIN)))
    sides, sent = lax.optimization_barrier((sides, sent))
    row_b, row_a = swap(sent["to_b"], "row", 1), swap(sent["to_a"], "row", 0)
    fixed = dict(occ=occ, spec=spec, **{name: host[name] for name in NAMES})
    state = {}
    for stage in range(ITERS):
        narrow = stage == ITERS - 1
        parted = 0 < stage < ITERS - 1
        moving = dict(sides)
        if stage == 0:
            moving["observed"] = observed
        known = dict(parts=parts) if stage else {}
        if stage > 1:
            known["coef"] = coef

        def old(where, *sums):
            names = ["res%d_%s" % (i, where) for i in range(stage)]
            return {name: state[name] for name in names + list(sums) if stage}

        middle = run(
            middle_kernel,
            {**fixed, **moving, **known, **old("mid", "top_sum", "mid_sum", "low_sum")},
            {
                "res_mid_new": (mid, WIN),
                "mid_sum_new": (mid - TILE, WIN),
                "acc": (3, 8, THIRD),
                **(dict(coef_new=COEFS) if stage else {}),
                **({name: (ext - 2 * WIN, THIRD) for name in ("mid_a", "mid_b") if parted}),
            },
            stage=stage,
            tiles=tiles,
            parted=parted,
        )
        if parted:
            middleb, middlez = swap(middle["mid_b"], "col", 1), swap(middle["mid_a"], "col", 0)
        outs = {"res_edge_new": (TILE, WIN), "top_sum_new": (WIN, WIN), "low_sum_new": (WIN, WIN)}
        outs["to_a"] = outs["to_b"] = (ext // 2 if narrow else 2 * WIN if parted else ext, THIRD)
        outs["part"] = (devices, THIRD)
        edges = run(
            edge_kernel,
            {
                **fixed,
                **moving,
                **(dict(coef=middle["coef_new"]) if stage else {}),
                **old("edge", "top_sum", "low_sum"),
                "row_b": row_b,
                "row_a": row_a,
                **{name: middle[name] for name in ("res_mid_new", "mid_sum_new", "acc")},
            },
            outs,
            dict(curve=(8, THIRD)),
            stage=stage,
            tiles=tiles,
            parted=parted,
            narrow=narrow,
        )
        state["res%d_mid" % stage] = middle["res_mid_new"]
        state["res%d_edge" % stage] = edges["res_edge_new"]
        state["mid_sum"] = middle["mid_sum_new"]
        state["top_sum"] = edges["top_sum_new"]
        state["low_sum"] = edges["low_sum_new"]
        part, to_a, to_b = edges["part"], edges["to_a"], edges["to_b"]
        if parted:
            middleb, middlez, to_b, to_a, part = lax.optimization_barrier((middleb, middlez, to_b, to_a, part))
        keys = ("endsb", "endsz") if parted else ("sideb", "sidez")
        sides = dict(zip(keys, (swap(to_b, "col", 1), swap(to_a, "col", 0))))
        if parted:
            sides.update(middleb=middleb, middlez=middlez)
        parts = lax.all_to_all(part, ("row", "col"), 0, 0, tiled=True)
        sides, parts = lax.optimization_barrier((sides, parts))
        sides["edge"] = edge
        strip = (HALO, TILE) if narrow else (THIRD, WIN)
        coef = middle.get("coef_new")
        sent = run(
            row_strip_kernel,
            dict(
                **(dict(parts=parts, coef=coef) if narrow else {}),
                top_sum=state["top_sum"],
                low_sum=state["low_sum"],
                **sides,
            ),
            dict(to_a=strip, to_b=strip, **(dict(coef_new=COEFS) if narrow else {})),
            stage=stage + 1,
            tiles=tiles,
            narrow=narrow,
        )
        row_b, row_a = swap(sent["to_b"], "row", 1), swap(sent["to_a"], "row", 0)

    def olds(where):
        return {name: state[name] for name in ["res%d_%s" % (i, where) for i in range(ITERS)]}

    coef = sent["coef_new"]
    ends = dict(top_sum=state["top_sum"], low_sum=state["low_sum"])
    out = run(
        last_middle_kernel,
        dict(coef=coef, mid_sum=state["mid_sum"], **ends, **sides, **olds("mid")),
        dict(corrected=(rows, cols), residual=(rows, cols)),
        stage=ITERS,
        tiles=tiles,
    )
    out = run(
        last_edge_kernel,
        dict(coef=coef, row_b=row_b, row_a=row_a, **ends, **sides, **olds("edge")),
        {},
        dict(
            corrected_rows=(2 * HALO, cols),
            residual_rows=(2 * HALO, cols),
            sems=pltpu.SemaphoreType.DMA((2, 2)),
        ),
        out,
        stage=ITERS,
        tiles=tiles,
    )
    return out["corrected"], out["residual"]


def solution(mesh):
    placed = (P("row", "col"), P(), P(), P())
    return jax.shard_map(
        shards,
        mesh=mesh,
        in_specs=placed,
        out_specs=(P("row", "col"), P("row", "col")),
        check_vma=False,
    )
```
